32 devices in a mesh: dp: 8 (over y, x, core), mp: 4 (over z).
Axes of the slice: x: 2, y: 2, z: 4, core: 2. Of those that a mesh axis runs over, the one named last changes fastest.
Arguments:
- token_ids: int32 [8192], P('dp'), may hold values from 0 to 8191
- segment_ids: int32 [8192], P('dp'), may hold values from 0 to 64, as said below
- timesteps: int32 [8], P('dp'), may hold values from 0 to 999
- token_table: bfloat16 [8192, 768], P(None, 'mp'), may hold values from -4.1875 to 4.1875
- time_table: bfloat16 [1000, 768], P(None, 'mp'), may hold values from -4.1875 to 4.1875
- ln1_gain: float32 [768], replicated, may hold values from 0.1 to 1.9
- ln1_bias: float32 [768], replicated, may hold values from -1.8 to 1.8
- w_qkv: bfloat16 [768, 3, 768], P(None, None, 'mp'), may hold values from -0.3125 to 0.3125
- w_out: bfloat16 [768, 768], P('mp'), may hold values from -1.25 to 1.25
- attn_bias: float32 [768], replicated, may hold values from -3 to 3
- ln2_gain: float32 [768], replicated, may hold values from 0.1 to 1.9
- ln2_bias: float32 [768], replicated, may hold values from -1.8 to 1.8
- w_up: bfloat16 [768, 3072], P(None, 'mp'), may hold values from -0.21875 to 0.21875
- w_down: bfloat16 [3072, 768], P('mp'), may hold values from -0.15625 to 0.15625
- mlp_bias: float32 [768], replicated, may hold values from -3 to 3
- cotangent: bfloat16 [8192, 768], P(('dp', 'mp')), may hold values from -6 to 6
Outputs:
- output: bfloat16 [8192, 768], P(('dp', 'mp'))
- input_grad: float32 [8192, 768], P(('dp', 'mp'))
- grad_token_table: float32 [8192, 768], P('dp', 'mp')
- grad_time_table: float32 [1000, 768], replicated
- grad_ln1_gain: float32 [768], replicated
- grad_ln1_bias: float32 [768], replicated
- grad_w_qkv: float32 [768, 3, 768], P('dp', None, 'mp')
- grad_w_out: float32 [768, 768], P('mp', 'dp')
- grad_attn_bias: float32 [768], replicated
- grad_ln2_gain: float32 [768], replicated
- grad_ln2_bias: float32 [768], replicated
- grad_w_up: float32 [768, 3072], P('dp', 'mp')
- grad_w_down: float32 [3072, 768], P('mp', 'dp')
- grad_mlp_bias: float32 [768], replicated
The draws below stay inside these ranges and needn't reach their ends.
Inputs may be any that keep to these rules, and one draw needn't show every extreme that they name: `segment_ids`: within each sequence of 1024 tokens the ids start at 1 and rise by 0 or 1 from one token to the next; a tail of padding zeros may follow.
All inputs are finite; a program needn't handle non-finite values.
Results may differ from the reference program's by a relative error of at most 0.018.
The reference program's roundings to bfloat16 on the way count: a program that leaves them out, or rounds other values in their place, can miss the bound.
Values may be sent and summed in bfloat16 or wider, within the bound.
A program may use at most 128 MiB of HBM per device.

```python
import math
import jax
import jax.numpy as jnp
import numpy as np
from jax import lax

D = 768
HEADS = 12
HD = 64
FF = 3072
VOCAB = 8192
TSTEPS = 1000
L = 1024
SEQS = 8
TOKENS = 8192


def draw_segment_ids(key, part):
    seq_total = TOKENS // L
    mark_key = jax.random.fold_in(key, 11)
    tail_key = jax.random.fold_in(key, 12)
    boundary = (jax.random.randint(mark_key, (seq_total, L), 0, 32) == 0).astype(jnp.int32)
    positions = jnp.arange(L)[None, :]
    regular = (positions % 16 == 0).astype(jnp.int32)
    first_seq = jnp.arange(seq_total)[:, None] == 0
    boundary = jnp.where(first_seq, regular, boundary)
    boundary = boundary.at[:, 0].set(0)
    numbers = jnp.minimum(1 + jnp.cumsum(boundary, axis=1), L // 16)
    pad_lengths = jax.random.randint(tail_key, (seq_total, 1), 0, L // 4 + 1)
    pad_lengths = jnp.where(first_seq, 0, pad_lengths)
    numbers = jnp.where(positions >= L - pad_lengths, 0, numbers)
    return numbers.reshape(TOKENS).astype(jnp.int32)


def with_ends(drawn, stream_key, smallest, top_value):
    index_at = [jax.random.randint(jax.random.fold_in(stream_key, axis), (), 0, length) for axis, length in enumerate(drawn.shape)]
    main_axis = drawn.shape.index(max(drawn.shape))
    next_to = index_at[:main_axis] + [(index_at[main_axis] + 1) % drawn.shape[main_axis]] + index_at[main_axis + 1:]
    return drawn.at[tuple(index_at)].set(smallest).at[tuple(next_to)].set(top_value)


def with_spikes(drawn, stream_key, source, target, shards_of, factor):
    def block_of(axis_at):
        return (jnp.arange(drawn.shape[axis_at]) // (drawn.shape[axis_at] // shards_of)).reshape((-1,) + (1,) * (drawn.ndim - 1 - axis_at))

    one_side = jax.random.permutation(stream_key, shards_of)[block_of(target)]
    second = (block_of(target) + shards_of // 2) % shards_of
    return jnp.where((block_of(source) == one_side) | (block_of(source) == second), factor * drawn, drawn)


def steps_of(key, dims, pieces, least, high):
    factor_of, own = 1.0, jax.random.fold_in(key, 6)
    for dim, shards_of in pieces:
        heights = jnp.exp(jax.random.uniform(jax.random.fold_in(own, dim), (shards_of,), jnp.float32, least / len(pieces), high / len(pieces)))
        factor_of = factor_of * jnp.repeat(heights, dims[dim] // shards_of).reshape([-1 if axis == dim else 1 for axis in range(len(dims))])
    return factor_of


def rank_bounds(number_of, skew):
    portions = [(1 << 20) // math.isqrt(grade ** skew) + 1 for grade in range(1, number_of + 1)]
    width = 1 + sum(portions) // (1 << 30)
    return np.cumsum(np.array([max(1, weight // width) for weight in portions]))


def ranked(rng, extent, amount, skew):
    table = rank_bounds(amount, skew)
    ticket = jax.random.randint(jax.random.fold_in(rng, 1), extent, 0, int(table[amount - 1]))
    rank = jnp.searchsorted(jnp.asarray(table, jnp.int32), ticket, side="right")
    return jax.random.permutation(jax.random.fold_in(rng, 2), amount)[rank].astype(jnp.int32)


def centred(rng, extent, width, most, pieces=(), dtype=jnp.bfloat16):
    entries = width * jax.random.normal(rng, extent, jnp.float32)
    if pieces:
        entries = entries * steps_of(rng, extent, pieces, -0.22, 0.18)
    return jnp.clip(entries, -most, most).astype(dtype)


def gaussian_with(own_key, extent, deviation, bound, shards, heavy, held_as=jnp.bfloat16):
    entries = deviation * jax.random.normal(own_key, extent, jnp.float32)
    if shards:
        entries = entries * steps_of(own_key, extent, shards, -0.22, 0.18)
    return jnp.clip(with_spikes(entries, jax.random.fold_in(own_key, 3), *heavy), -bound, bound).astype(held_as)


def setup_inputs(seed: int = 0) -> dict:
    seeds = jax.random.split(jax.random.key(seed), 17)
    return {
        "token_ids": with_ends(ranked(seeds[0], (TOKENS,), VOCAB, 2), jax.random.fold_in(seeds[0], 3), 0, VOCAB - 1).astype(jnp.int32),
        "segment_ids": draw_segment_ids(jax.random.fold_in(seeds[16], 71), 0),
        "timesteps": with_ends(jax.random.randint(seeds[2], (SEQS,), 0, TSTEPS), jax.random.fold_in(seeds[2], 1), 0, TSTEPS - 1).astype(jnp.int32),
        "token_table": centred(seeds[3], (VOCAB, D), 0.7, 4.1875, ((1, 4),)),
        "time_table": centred(seeds[4], (TSTEPS, D), 0.7, 4.1875, ((1, 4),)),
        "ln1_gain": jnp.clip(1.0 + 0.18 * jax.random.normal(seeds[5], (D,), jnp.float32), 0.1, 1.9),
        "ln1_bias": centred(seeds[6], (D,), 0.3, 1.8, (), jnp.float32),
        "w_qkv": centred(seeds[7], (D, 3, D), (D // 2) ** -0.5, 0.3125, ((2, 4),)),
        "w_out": centred(seeds[8], (D, D), (D // 32) ** -0.5, 1.25, ((0, 4),)),
        "attn_bias": centred(seeds[9], (D,), 0.5, 3.0, (), jnp.float32),
        "ln2_gain": jnp.clip(1.0 + 0.18 * jax.random.normal(seeds[10], (D,), jnp.float32), 0.1, 1.9),
        "ln2_bias": centred(seeds[11], (D,), 0.3, 1.8, (), jnp.float32),
        "w_up": centred(seeds[12], (D, FF), D ** -0.5, 0.21875, ((1, 4),)),
        "w_down": centred(seeds[13], (FF, D), (FF // 2) ** -0.5, 0.15625, ((0, 4),)),
        "mlp_bias": centred(seeds[14], (D,), 0.5, 3.0, (), jnp.float32),
        "cotangent": gaussian_with(seeds[15], (TOKENS, D), 1.0, 6.0, ((0, 32),), (0, 1, 32, 2.75)),
    }


PRECISE = lax.Precision.HIGHEST

@jax.custom_vjp
def low(v):
    return lax.optimization_barrier(v.astype(jnp.bfloat16)).astype(jnp.float32)

@jax.custom_vjp
def low_back(v):
    return v

def low_keep(v):
    return (low(v), None)

def low_pass(kept, grad):
    return (grad,)

def back_keep(v):
    return (v, None)

def back_low(kept, grad):
    return (low(grad),)
low.defvjp(low_keep, low_pass)
low_back.defvjp(back_keep, back_low)

def layer_norm(stream, gain, shift):
    average = lax.optimization_barrier(jnp.mean(stream, axis=-1, keepdims=True))
    centered = stream - average
    variance = lax.optimization_barrier(jnp.mean(centered * centered, axis=-1, keepdims=True))
    return centered * lax.rsqrt(variance + 1e-05) * gain + shift

def attend_sequence(queries, key_rows, value_rows, segments):
    positions = jnp.arange(segments.shape[0])
    allowed = (segments[:, None] == segments[None, :]) & ((segments[:, None] != 0) | (positions[:, None] == positions[None, :]))
    scores = low_back(jnp.einsum('qhd,khd->hqk', queries, key_rows, precision=PRECISE) * 0.125)
    masked = jnp.where(allowed[None], scores, -1e+30)
    highest = lax.optimization_barrier(jnp.max(masked, axis=-1, keepdims=True))
    exponents = jnp.exp(masked - highest)
    probs = exponents / lax.optimization_barrier(jnp.sum(exponents, axis=-1, keepdims=True))
    attended = jnp.einsum('hqk,khd->qhd', low(probs), value_rows, precision=PRECISE)
    return low_back(low(attended))

def block_forward(stream_in, segments, ln1_gain, ln1_bias, w_qkv, w_out, attn_bias, ln2_gain, ln2_bias, w_up, w_down, mlp_bias):
    row_count = stream_in.shape[0]
    normed_one = low(layer_norm(stream_in, ln1_gain, ln1_bias))
    packed = jnp.dot(normed_one, w_qkv.reshape(D, 3 * D), precision=PRECISE).reshape(row_count // L, L, 3, HEADS, HD)
    queries = low_back(low(packed[:, :, 0]))
    key_rows = low_back(low(packed[:, :, 1]))
    value_rows = low_back(low(packed[:, :, 2]))
    attend_saved = jax.checkpoint(attend_sequence)
    attended = lax.map(lambda per_seq: attend_saved(per_seq[0], per_seq[1], per_seq[2], per_seq[3]), (queries, key_rows, value_rows, segments.reshape(row_count // L, L)))
    attn_branch = low_back(jnp.dot(attended.reshape(row_count, D), w_out, precision=PRECISE))
    stream_mid = stream_in + attn_branch + attn_bias
    normed_two = low(layer_norm(stream_mid, ln2_gain, ln2_bias))
    pre_act = low_back(jnp.dot(normed_two, w_up, precision=PRECISE))
    activation = low(jax.nn.gelu(pre_act, approximate=True))
    mlp_branch = low_back(jnp.dot(activation, w_down, precision=PRECISE))
    return stream_mid + mlp_branch + mlp_bias

def embed_rows(token_float, time_float, id_rows, step_rows):
    return token_float[id_rows] + jnp.repeat(time_float[step_rows], L, axis=0)

def reference(token_ids, segment_ids, timesteps, token_table, time_table, ln1_gain, ln1_bias, w_qkv, w_out, attn_bias, ln2_gain, ln2_bias, w_up, w_down, mlp_bias, cotangent):
    group = 4
    token_float = token_table.astype(jnp.float32)
    time_float = time_table.astype(jnp.float32)
    params = (ln1_gain, ln1_bias, w_qkv.astype(jnp.float32), w_out.astype(jnp.float32), attn_bias, ln2_gain, ln2_bias, w_up.astype(jnp.float32), w_down.astype(jnp.float32), mlp_bias)
    step_count = timesteps.shape[0] // group
    id_groups = token_ids.reshape(step_count, group * L)
    seg_groups = segment_ids.reshape(step_count, group * L)
    time_groups = timesteps.reshape(step_count, group)
    cot_groups = cotangent.reshape(step_count, group * L, D)

    def one_group(carry, inputs):
        id_rows, seg_rows, step_rows, cot_rows = inputs
        stream_in, embed_back = jax.vjp(lambda table_one, table_two: embed_rows(table_one, table_two, id_rows, step_rows), token_float, time_float)
        output, layer_back = jax.vjp(lambda stream, *weights: block_forward(stream, seg_rows, *weights), stream_in, *params)
        valid = (seg_rows != 0).astype(jnp.float32)[:, None]
        grads = layer_back(cot_rows.astype(jnp.float32) * valid)
        token_grad, time_grad = embed_back(grads[0])
        totals = (carry[0] + token_grad, carry[1] + time_grad) + tuple((acc + new for acc, new in zip(carry[2:], grads[1:])))
        return (totals, (output.astype(jnp.bfloat16), grads[0]))
    start = (jnp.zeros_like(token_float), jnp.zeros_like(time_float)) + tuple((jnp.zeros_like(weight) for weight in params))
    totals, (outputs, input_grads) = lax.scan(one_group, start, (id_groups, seg_groups, time_groups, cot_groups))
    return (outputs.reshape(-1, D), input_grads.reshape(-1, D), totals[0], totals[1], totals[2], totals[3], totals[4], totals[5], totals[6], totals[7], totals[8], totals[9], totals[10], totals[11])
```

```python
import functools

import jax
import jax.numpy as jnp
from jax import lax
from jax.experimental import pallas as pl
from jax.experimental.pallas import tpu as pltpu
from jax.sharding import PartitionSpec as P

D = 768
HD = 64
L = 1024
QBLK = 512
BF = jnp.bfloat16
F32 = jnp.float32
MESH = pl.DeviceIdType.MESH
ANY = pl.BlockSpec(memory_space=pl.ANY)
DMA = pltpu.SemaphoreType.DMA


class Place:
    def __init__(self):
        self.p = p = lax.axis_index("dp")
        self.j = lax.axis_index("mp")
        core, x, y = p % 2, (p // 2) % 2, p // 4
        self.core, self.m = core, p // 2
        self.px = p + 2 - 4 * x
        self.py = p + 4 - 8 * y
        self.pd = self.px + 4 - 8 * y
        self.pc = p + 1 - 2 * core
        self.mx = self.px // 2
        self.my = self.py // 2
        self.md = self.pd // 2

    def z(self, hop):
        return (self.p, (self.j + hop) % 4)

    def at(self, dp):
        return (dp, self.j)


def meet(devices):
    barrier = pltpu.get_barrier_semaphore()
    for device in devices:
        pl.semaphore_signal(barrier, inc=1, device_id=device, device_id_type=MESH)
    pl.semaphore_wait(barrier, len(devices))


def push(src, dst, send, recv, device):
    return pltpu.make_async_remote_copy(
        src_ref=src, dst_ref=dst, send_sem=send, recv_sem=recv, device_id=device, device_id_type=MESH
    )


def params(cid):
    return pltpu.CompilerParams(collective_id=cid, has_side_effects=True, vmem_limit_bytes=56 << 20)


def gather_kernel(emb, trow, ids, w2, wo, E, TR, IDS, W2, WO, zs, zr, ts, tr, is_, ir, ps, pr, ls):
    me = Place()
    p, j = me.p, me.j
    plane = [me.at((p + k) % 8) for k in range(1, 8)]
    meet([me.z(1), me.z(2), me.z(3)] + plane)

    def part(a, q, piece, half=None):
        if a == 0:
            lo, n = (0, 96) if half is None else (48 * half, 48)
            return W2.at[q, :, pl.ds(96 * piece + lo, n), :]
        lo, n = (0, 144) if half is None else ((0, 80), (80, 64))[half]
        return WO.at[q, pl.ds(144 * piece + lo, n), :]

    own = (w2.at[:, pl.ds(96 * p, 96), :], wo.at[pl.ds(144 * p, 144), :])

    def quarter(d, k):
        return (j - k + 4) % 4 if d == 0 else (j + k) % 4

    def sends(d, k):
        return (j < 3) & (j >= k) if d == 0 else (j > 0) & (j + k <= 3)

    def gets(d, k):
        return j >= k + 1 if d == 0 else j + k + 1 <= 3

    def zcopy(d, k, a):
        q = quarter(d, k)
        if a == 2:
            src = emb if k == 0 else E.at[q]
            dst = E.at[q]
        else:
            src = own[a] if k == 0 else part(a, q, p)
            dst = part(a, q, p)
        return push(src, dst, zs.at[d, k, a], zr.at[d, k, a], me.z(1 if d == 0 else 3))

    def zgot(d, k, a):
        q = quarter(d, k + 1)
        dst = E.at[q] if a == 2 else part(a, q, p)
        return push(dst, dst, zs.at[d, k, a], zr.at[d, k, a], me.z(1))

    def zstart(k, arrays):
        for d in (0, 1):

            @pl.when(sends(d, k))
            def _():
                for a in arrays:
                    zcopy(d, k, a).start()

    def zwait(k, arrays):
        for d in (0, 1):

            @pl.when(gets(d, k))
            def _():
                for a in arrays:
                    zgot(d, k, a).wait_recv()

    def routes(d, k, a, stage):
        q = quarter(d, k + 1)
        if stage == 0:
            return [(part(a, q, p), me.px), (part(a, q, p), me.py), (part(a, q, p), me.pc)]
        if stage == 1:
            return [
                (part(a, q, me.py, 0), me.px),
                (part(a, q, me.px, 1), me.py),
                (part(a, q, me.px), me.pc),
                (part(a, q, me.py), me.pc),
            ]
        return [(part(a, q, me.pd), me.pc)]

    def arrivals(d, k, a, stage):
        q = quarter(d, k + 1)
        if stage == 0:
            return [part(a, q, me.px), part(a, q, me.py), part(a, q, me.pc)]
        if stage == 1:
            return [
                part(a, q, me.pd, 0),
                part(a, q, me.pd, 1),
                part(a, q, me.px + me.pc - p),
                part(a, q, me.py + me.pc - p),
            ]
        return [part(a, q, me.pd + me.pc - p)]

    def pstart(k, stage):
        for d in (0, 1):

            @pl.when(gets(d, k))
            def _():
                for a in (0, 1):
                    for i, (ref, dp) in enumerate(routes(d, k, a, stage)):
                        s = 3 * stage + i if stage < 2 else 7
                        push(ref, ref, ps.at[d, k, a, s], pr.at[d, k, a, s], me.at(dp)).start()

    def pwait(k, stage, which, send=False):
        for d in (0, 1):

            @pl.when(gets(d, k))
            def _():
                for a in (0, 1):
                    refs = [r for r, _ in routes(d, k, a, stage)] if send else arrivals(d, k, a, stage)
                    for i in which:
                        s = 3 * stage + i if stage < 2 else 7
                        c = push(refs[i], refs[i], ps.at[d, k, a, s], pr.at[d, k, a, s], me.at(me.pc))
                        c.wait_send() if send else c.wait_recv()

    locals_ = [
        pltpu.make_async_copy(emb, E.at[j], ls.at[0]),
        pltpu.make_async_copy(trow, TR.at[j], ls.at[1]),
        pltpu.make_async_copy(ids, IDS.at[p], ls.at[2]),
        pltpu.make_async_copy(w2, W2.at[j], ls.at[3]),
        pltpu.make_async_copy(wo, WO.at[j], ls.at[4]),
    ]
    small = [push(trow, TR.at[j], ts.at[k - 1], tr.at[k - 1], me.z(k)) for k in (1, 2, 3)]
    small += [push(ids, IDS.at[p], is_.at[k - 1], ir.at[k - 1], me.at((p + k) % 8)) for k in range(1, 8)]

    zstart(0, (0, 1))
    for c in small + locals_:
        c.start()
    zwait(0, (0, 1))
    zstart(1, (0, 1))
    pstart(0, 0)
    zstart(0, (2,))
    zwait(1, (0, 1))
    zstart(2, (0, 1))
    pwait(0, 0, (0, 1))
    pstart(0, 1)
    pstart(1, 0)
    zwait(0, (2,))
    zstart(1, (2,))
    zwait(2, (0, 1))
    pwait(0, 1, (0, 1))
    pstart(0, 2)
    pwait(1, 0, (0, 1))
    pstart(1, 1)
    pstart(2, 0)
    zwait(1, (2,))
    zstart(2, (2,))
    pwait(1, 1, (0, 1))
    pstart(1, 2)
    pwait(2, 0, (0, 1))
    pstart(2, 1)
    pwait(2, 1, (0, 1))
    pstart(2, 2)
    zwait(2, (2,))
    for k in range(3):
        pwait(k, 0, (2,))
        pwait(k, 1, (2, 3))
        pwait(k, 2, (0,))
        pwait(k, 0, (0, 1, 2), send=True)
        pwait(k, 1, (0, 1, 2, 3), send=True)
        pwait(k, 2, (0,), send=True)
        for d in (0, 1):

            @pl.when(sends(d, k))
            def _():
                for a in (0, 1, 2):
                    zcopy(d, k, a).wait_send()

    for c in small + locals_:
        c.wait()


def gather_all(emb, trow, ids, w2, wo):
    return pl.pallas_call(
        gather_kernel,
        out_shape=(
            jax.ShapeDtypeStruct((4,) + emb.shape, BF),
            jax.ShapeDtypeStruct((4,) + trow.shape, BF),
            jax.ShapeDtypeStruct((8,) + ids.shape, jnp.int32),
            jax.ShapeDtypeStruct((4,) + w2.shape, BF),
            jax.ShapeDtypeStruct((4,) + wo.shape, BF),
        ),
        in_specs=[ANY] * 5,
        out_specs=(ANY,) * 5,
        scratch_shapes=[
            DMA((2, 3, 3)),
            DMA((2, 3, 3)),
            DMA((3,)),
            DMA((3,)),
            DMA((7,)),
            DMA((7,)),
            DMA((2, 3, 2, 8)),
            DMA((2, 3, 2, 8)),
            DMA((5,)),
        ],
        compiler_params=params(0),
        name="gather_all",
    )(emb, trow, ids, w2, wo)


def exchange_kernel(x, out, send, recv, local):
    me = Place()
    meet([me.z(1), me.z(2), me.z(3)])
    mine = pltpu.make_async_copy(x.at[me.j], out.at[me.j], local)
    copies = [
        push(x.at[(me.j + k) % 4], out.at[me.j], send.at[k - 1], recv.at[k - 1], me.z(k)) for k in (1, 2, 3)
    ]
    for c in copies:
        c.start()
    mine.start()
    for c in copies:
        c.wait()
    mine.wait()


def exchange(x, cid, name):
    return pl.pallas_call(
        exchange_kernel,
        out_shape=jax.ShapeDtypeStruct(x.shape, x.dtype),
        in_specs=[ANY],
        out_specs=ANY,
        scratch_shapes=[DMA((3,)), DMA((3,)), DMA],
        compiler_params=params(cid),
        name=name,
    )(x)


class Line:
    def __init__(self, me, acc, up, down, sems):
        self.me, self.acc, self.up, self.down = me, acc, up, down
        self.us, self.ur, self.ds, self.dr = (sems.at[i] for i in range(4))

    def send(self, q, d):
        if d == 0:
            return push(self.acc(q), self.up.at[q], self.us.at[q], self.ur.at[q], self.me.z(1))
        return push(self.acc(q), self.down.at[q], self.ds.at[q], self.dr.at[q], self.me.z(3))

    def go(self, q, d):
        j, ref = self.me.j, self.acc(q)
        here = (j < q) if d == 0 else (j > q)
        inner = (j > 0) if d == 0 else (j < 3)
        got = self.up if d == 0 else self.down

        @pl.when(here & inner)
        def _():
            self.send(q, d).wait_recv()
            ref[...] = ref[...] + got[q]

        @pl.when(here)
        def _():
            self.send(q, d).start()

    def first(self):
        j = self.me.j

        @pl.when(j == 0)
        def _():
            for q in (3, 2, 1):
                self.send(q, 0).start()

        @pl.when(j == 3)
        def _():
            for q in (0, 1, 2):
                self.send(q, 1).start()

    def inner(self, steps):
        j = self.me.j
        for q, d in steps:
            got = self.up if d == 0 else self.down
            cond = ((j < q) & (j > 0)) if d == 0 else ((j > q) & (j < 3))

            @pl.when(cond)
            def _():
                c = self.send(q, d)
                c.wait_recv()
                ref = self.acc(q)
                ref[...] = ref[...] + got[q]
                c.start()

    def finish(self, out):
        j = self.me.j
        for q in range(4):

            @pl.when(j == q)
            def _():
                total = self.acc(q)[...].astype(F32)
                if q > 0:
                    self.send(q, 0).wait_recv()
                    total = total + self.up[q].astype(F32)
                if q < 3:
                    self.send(q, 1).wait_recv()
                    total = total + self.down[q].astype(F32)
                out[...] = total

            @pl.when(j < q)
            def _():
                self.send(q, 0).wait_send()

            @pl.when(j > q)
            def _():
                self.send(q, 1).wait_send()


OUTER = ((3, 0), (0, 1))
MIDDLE = ((2, 0), (1, 1))


class Unit:
    def __init__(self, me, src, acc, rc, rx, ry, rx2, ry2, sems, lsem):
        self.me, self.src, self.acc = me, src, acc
        self.rc, self.rx, self.ry, self.rx2, self.ry2 = rc, rx, ry, rx2, ry2
        self.s, self.r, self.lsem = sems.at[0], sems.at[1], lsem
        self.nq = acc.shape[0]

    def copies(self, stage):
        me, acc, s, r = self.me, self.acc, self.s, self.r
        lo, hi = pl.ds(0, 48), pl.ds(48, 48)
        if stage == 0:
            return [push(self.src.at[:, :, 1 - me.core], self.rc, s.at[0], r.at[0], me.at(me.pc))]
        if stage == 1:
            return [
                push(acc.at[:, me.md, lo], self.rx.at[:, 1], s.at[1], r.at[1], me.at(me.px)),
                push(acc.at[:, me.md, hi], self.ry.at[:, 1], s.at[2], r.at[2], me.at(me.py)),
                push(acc.at[:, me.mx, lo], self.rx.at[:, 0], s.at[3], r.at[3], me.at(me.px)),
                push(acc.at[:, me.my, hi], self.ry.at[:, 0], s.at[4], r.at[4], me.at(me.py)),
            ]
        return [
            push(acc.at[:, me.my, lo], self.ry2, s.at[5], r.at[5], me.at(me.py)),
            push(acc.at[:, me.mx, hi], self.rx2, s.at[6], r.at[6], me.at(me.px)),
        ]

    def load(self):
        return pltpu.make_async_copy(self.src.at[:, :, self.me.core], self.acc, self.lsem)

    def begin(self):
        self.copies(0)[0].start()
        self.load().start()

    def chip(self):
        self.load().wait()
        self.copies(0)[0].wait_recv()

        @pl.loop(0, self.nq)
        def _(q):
            for m in range(4):
                self.acc[q, m] = self.acc[q, m] + self.rc[q, m]

    def cross(self):
        for c in self.copies(1):
            c.start()

    def turn(self):
        me = self.me
        for c in self.copies(1):
            c.wait()

        @pl.loop(0, self.nq)
        def _(q):
            self.acc[q, me.my, 0:48] = self.acc[q, me.my, 0:48] + self.rx[q, 1]
            self.acc[q, me.mx, 48:96] = self.acc[q, me.mx, 48:96] + self.ry[q, 1]

        for c in self.copies(2):
            c.start()

        @pl.loop(0, self.nq)
        def _(q):
            self.acc[q, me.m, 0:48] = self.acc[q, me.m, 0:48] + self.rx[q, 0]
            self.acc[q, me.m, 48:96] = self.acc[q, me.m, 48:96] + self.ry[q, 0]

    def settle(self):
        me = self.me
        for c in self.copies(2):
            c.wait()

        @pl.loop(0, self.nq)
        def _(q):
            self.acc[q, me.m, 0:48] = self.acc[q, me.m, 0:48] + self.ry2[q]
            self.acc[q, me.m, 48:96] = self.acc[q, me.m, 48:96] + self.rx2[q]

        self.copies(0)[0].wait_send()

    def own(self, q):
        return self.acc.at[q, self.me.m]


def reduce_kernel(gn, dw, dwo, dqkv, o_gn, o_up, o_down, o_out, o_qkv, *scratch):
    me = Place()
    meet([me.z(1), me.z(2), me.z(3), me.at(me.px), me.at(me.py), me.at(me.pc)])
    it = iter(scratch)
    take = lambda n: [next(it) for _ in range(n)]
    gacc, gup, gdown, gsem, gl = take(5)
    sources = (dw.at[1], dw.at[0], dwo, dqkv)
    units, lines = [], []
    for i, src in enumerate(sources):
        acc, rc, rx, ry, rx2, ry2, sems, lsem = take(8)
        unit = Unit(me, src, acc, rc, rx, ry, rx2, ry2, sems, lsem)
        units.append(unit)
        if i < 3:
            up, down, sem = take(3)
            lines.append(Line(me, unit.own, up, down, sem))
    own = Line(me, lambda q: gacc.at[q], gup, gdown, gsem)
    load = pltpu.make_async_copy(gn, gacc, gl)
    load.start()
    for u in units:
        u.begin()
    load.wait()
    own.first()
    units[0].chip()
    units[0].cross()
    for u in units[1:]:
        u.chip()
    own.inner(OUTER)
    units[0].turn()
    units[1].cross()
    own.inner(MIDDLE)
    units[0].settle()
    lines[0].first()
    units[1].turn()
    units[2].cross()
    units[3].cross()
    own.inner(((3, 0), (0, 1))[:0])
    lines[0].inner(OUTER)
    units[1].settle()
    lines[1].first()
    units[2].turn()
    units[3].turn()
    lines[0].inner(MIDDLE)
    own.finish(o_gn)
    units[2].settle()
    lines[2].first()
    lines[1].inner(OUTER)
    units[3].settle()
    lines[2].inner(OUTER)
    lines[1].inner(MIDDLE)
    lines[2].inner(MIDDLE)
    lines[0].finish(o_down)
    lines[1].finish(o_up)
    lines[2].finish(o_out)
    o_qkv[...] = units[3].acc[0, me.m].astype(F32)


def reduce_all(gn, dw, dwo, dqkv):
    scratch = [
        pltpu.VMEM((4, 256, 768), BF),
        pltpu.VMEM((4, 256, 768), BF),
        pltpu.VMEM((4, 256, 768), BF),
        DMA((4, 4)),
        DMA,
    ]
    for i, (nq, w) in enumerate(((4, 768), (4, 768), (4, 256), (1, 640))):
        scratch += [
            pltpu.VMEM((nq, 4, 96, w), BF),
            pltpu.VMEM((nq, 4, 96, w), BF),
            pltpu.VMEM((nq, 2, 48, w), BF),
            pltpu.VMEM((nq, 2, 48, w), BF),
            pltpu.VMEM((nq, 48, w), BF),
            pltpu.VMEM((nq, 48, w), BF),
            DMA((2, 7)),
            DMA,
        ]
        if i < 3:
            scratch += [pltpu.VMEM((4, 96, w), BF), pltpu.VMEM((4, 96, w), BF), DMA((4, 4))]
    vm = pl.BlockSpec(memory_space=pltpu.VMEM)
    return pl.pallas_call(
        reduce_kernel,
        out_shape=(
            jax.ShapeDtypeStruct((256, 768), F32),
            jax.ShapeDtypeStruct((96, 768), F32),
            jax.ShapeDtypeStruct((96, 768), F32),
            jax.ShapeDtypeStruct((96, 256), F32),
            jax.ShapeDtypeStruct((96, 640), F32),
        ),
        in_specs=[ANY] * 4,
        out_specs=(vm,) * 5,
        scratch_shapes=scratch,
        compiler_params=params(3),
        name="reduce_all",
    )(gn, dw, dwo, dqkv)


def final_kernel(tp, vec, X, SP, SZ, vs, zs, zr, vzs, vzr, ps, pr, vps, vpr, ls):
    me = Place()
    p, j = me.p, me.j
    meet([me.z(1), me.z(2), me.z(3)] + [me.at((p + k) % 8) for k in range(1, 8)])
    small = [push(vec, SZ.at[j], vzs.at[k - 1], vzr.at[k - 1], me.z(k)) for k in (1, 2, 3)]
    big = [push(tp.at[(j + k) % 4], X.at[p, j], zs.at[k - 1], zr.at[k - 1], me.z(k)) for k in (1, 2, 3)]
    mine = pltpu.make_async_copy(tp.at[j], X.at[p, j], ls.at[0])
    mine_v = pltpu.make_async_copy(vec, SZ.at[j], ls.at[1])
    for c in small + big + [mine, mine_v]:
        c.start()
    for c in small + [mine_v]:
        c.wait()
    vs[...] = SZ[0] + SZ[1] + SZ[2] + SZ[3]
    out_v = [push(vs, SP.at[p], vps.at[k - 1], vpr.at[k - 1], me.at((p + k) % 8)) for k in range(1, 8)]
    own_v = pltpu.make_async_copy(vs, SP.at[p], ls.at[2])
    for c in out_v + [own_v]:
        c.start()
    for c in big + [mine]:
        c.wait()
    lo, hi = pl.ds(0, 2), pl.ds(2, 2)

    def to(ref, i, dp):
        return push(ref, ref, ps.at[i], pr.at[i], me.at(dp))

    first = [to(X.at[p], 0, me.px), to(X.at[p], 1, me.py), to(X.at[p], 2, me.pc)]
    for c in first:
        c.start()
    here = me.pc - p
    to(X.at[me.px], 0, me.px).wait_recv()
    to(X.at[me.py], 1, me.py).wait_recv()
    second = [
        to(X.at[me.py, lo], 3, me.px),
        to(X.at[me.px, hi], 4, me.py),
        to(X.at[me.px], 5, me.pc),
        to(X.at[me.py], 6, me.pc),
    ]
    for c in second:
        c.start()
    to(X.at[me.pd, lo], 3, me.px).wait_recv()
    to(X.at[me.pd, hi], 4, me.px).wait_recv()
    third = to(X.at[me.pd], 7, me.pc)
    third.start()
    to(X.at[me.pc], 2, me.pc).wait_recv()
    to(X.at[me.px + here], 5, me.pc).wait_recv()
    to(X.at[me.py + here], 6, me.pc).wait_recv()
    to(X.at[me.pd + here], 7, me.pc).wait_recv()
    for c in first + second + [third]:
        c.wait_send()
    for c in out_v + [own_v]:
        c.wait()


def final_exchange(tp, vec):
    return pl.pallas_call(
        final_kernel,
        out_shape=(
            jax.ShapeDtypeStruct((8,) + tp.shape, BF),
            jax.ShapeDtypeStruct((8, 8, D), F32),
        ),
        in_specs=[ANY] * 2,
        out_specs=(ANY,) * 2,
        scratch_shapes=[
            pltpu.VMEM((4, 8, D), F32),
            pltpu.VMEM((8, D), F32),
            DMA((3,)),
            DMA((3,)),
            DMA((3,)),
            DMA((3,)),
            DMA((8,)),
            DMA((8,)),
            DMA((7,)),
            DMA((7,)),
            DMA((3,)),
        ],
        compiler_params=params(4),
        name="final_exchange",
    )(tp, vec)


class Native:
    def __init__(self, ndp, nmp):
        self.ndp, self.nmp = ndp, nmp

    def gather_all(self, emb, trow, ids, w2, wo):
        over_mp = lambda a: lax.all_gather(a, "mp", axis=0, tiled=False)
        return (
            over_mp(emb),
            over_mp(trow),
            lax.all_gather(ids, "dp", axis=0, tiled=False),
            over_mp(w2),
            over_mp(wo),
        )

    def exchange(self, x, cid, name):
        return lax.all_to_all(x, "mp", split_axis=0, concat_axis=0, tiled=True)

    def reduce_all(self, gn, dw, dwo, dqkv):
        sum_mp = lambda a: lax.psum_scatter(a.astype(F32), "mp", scatter_dimension=0, tiled=True)
        sum_dp = lambda a: lax.psum_scatter(a, "dp", scatter_dimension=0, tiled=True)
        flat = lambda a: a.reshape(D, a.shape[-1])
        return (
            sum_mp(gn).reshape(gn.shape[1:]),
            sum_dp(flat(sum_mp(dw[0]))),
            sum_dp(flat(sum_mp(dw[1]))),
            sum_dp(flat(sum_mp(dwo[..., : D // self.nmp]))),
            sum_dp(flat(dqkv[..., : 3 * D // self.nmp].astype(F32))),
        )

    def final_exchange(self, tp, vec):
        x = lax.all_to_all(tp, "mp", split_axis=0, concat_axis=0, tiled=True)
        return (
            lax.all_gather(x, "dp", axis=0, tiled=False),
            lax.all_gather(lax.psum(vec, "mp"), "dp", axis=0, tiled=False),
        )


class Tuned:
    gather_all = staticmethod(gather_all)
    exchange = staticmethod(exchange)
    reduce_all = staticmethod(reduce_all)
    final_exchange = staticmethod(final_exchange)


def layer_norm(stream, gain, shift):
    average = jnp.mean(stream, axis=-1, keepdims=True)
    centered = stream - average
    variance = jnp.mean(centered * centered, axis=-1, keepdims=True)
    return centered * lax.rsqrt(variance + 1e-05) * gain + shift


def allowed_pairs(seg_query, segments, first_row):
    key_pos = jnp.arange(L)
    query_pos = first_row + jnp.arange(QBLK)
    same_text = seg_query[:, None] == segments[None, :]
    self_or_text = (seg_query[:, None] != 0) | (query_pos[:, None] == key_pos[None, :])
    return same_text & self_or_text


def attend_forward(queries, key_rows, value_rows, segments):
    outputs = []
    log_parts = []
    for block_index in range(L // QBLK):
        first_row = block_index * QBLK
        query_block = queries[first_row : first_row + QBLK]
        allowed = allowed_pairs(segments[first_row : first_row + QBLK], segments, first_row)
        scores = jnp.einsum("qhd,khd->hqk", query_block, key_rows, preferred_element_type=F32) * 0.125
        masked = jnp.where(allowed[None], scores, -1e30)
        highest = jnp.max(masked, axis=-1, keepdims=True)
        exponents = jnp.exp(masked - highest)
        totals = jnp.sum(exponents, axis=-1, keepdims=True)
        weights = (exponents / totals).astype(BF)
        outputs.append(jnp.einsum("hqk,khd->qhd", weights, value_rows, preferred_element_type=F32).astype(BF))
        log_parts.append((highest + jnp.log(totals))[..., 0])
    return (jnp.concatenate(outputs, axis=0), jnp.concatenate(log_parts, axis=1))


def attend_backward(queries, key_rows, value_rows, segments, log_sums, grad_heads):
    grad_keys = jnp.zeros(key_rows.shape, F32)
    grad_values = jnp.zeros(value_rows.shape, F32)
    grad_queries = []
    for block_index in range(L // QBLK):
        first_row = block_index * QBLK
        query_block = queries[first_row : first_row + QBLK]
        grad_block = grad_heads[first_row : first_row + QBLK]
        allowed = allowed_pairs(segments[first_row : first_row + QBLK], segments, first_row)
        scores = jnp.einsum("qhd,khd->hqk", query_block, key_rows, preferred_element_type=F32) * 0.125
        masked = jnp.where(allowed[None], scores, -1e30)
        probs = jnp.exp(masked - log_sums[:, first_row : first_row + QBLK, None])
        rounded = probs.astype(BF)
        grad_probs = jnp.einsum("qhd,khd->hqk", grad_block, value_rows, preferred_element_type=F32)
        inner = jnp.sum(probs * grad_probs, axis=-1, keepdims=True)
        grad_scores = (probs * (grad_probs - inner)).astype(BF)
        grad_queries.append(
            jnp.einsum("hqk,khd->qhd", grad_scores, key_rows, preferred_element_type=F32) * 0.125
        )
        grad_keys = (
            grad_keys
            + jnp.einsum("hqk,qhd->khd", grad_scores, query_block, preferred_element_type=F32) * 0.125
        )
        grad_values = grad_values + jnp.einsum("hqk,qhd->khd", rounded, grad_block, preferred_element_type=F32)
    return (
        jnp.concatenate(grad_queries, axis=0).astype(BF),
        grad_keys.astype(BF),
        grad_values.astype(BF),
    )


def dot(a, b):
    return jnp.dot(a, b, preferred_element_type=F32)


def contract_rows(left, right):
    return lax.dot_general(left, right, (((0,), (0,)), ((), ())), preferred_element_type=F32)


def contract_cols(left, right):
    return lax.dot_general(left, right, (((1,), (1,)), ((), ())), preferred_element_type=F32)


def fold(rows):
    half = rows.shape[-2] // 2
    return jnp.concatenate((rows[..., :half, :], rows[..., half:, :]), axis=-1)


def unfold(packed):
    width = packed.shape[-1] // 2
    return jnp.concatenate((packed[..., :width], packed[..., width:]), axis=-2)


def on_device(
    comm,
    token_ids,
    segment_ids,
    timesteps,
    token_table,
    time_table,
    ln1_gain,
    ln1_bias,
    w_qkv,
    w_out,
    attn_bias,
    ln2_gain,
    ln2_bias,
    w_up,
    w_down,
    mlp_bias,
    cotangent,
):
    group = lax.axis_size("mp")
    ndp = lax.axis_size("dp")
    member = lax.axis_index("mp")
    own_rows = L // group
    width = token_table.shape[1]
    heads_local = width // HD

    emb = fold(token_table[token_ids])
    time_row = lax.dynamic_slice_in_dim(time_table, timesteps[0], 1, 0)
    trow = jnp.broadcast_to(jnp.pad(time_row, ((0, 0), (0, 256 - width))), (16, 256))
    ids = token_ids.reshape(8, 128)
    w2 = jnp.stack((w_up, w_down))
    wo = w_out.reshape(width, 6, 128).transpose(1, 0, 2).reshape(6 * width, 128)
    E, TR, IDS, W2, WO = comm.gather_all(emb, trow, ids, w2, wo)

    time_full = TR[:, 0, :width].reshape(1, D).astype(F32)
    tokens = unfold(E).transpose(1, 0, 2).reshape(L, D)
    stream_all = tokens.astype(F32) + time_full
    stream_in = lax.dynamic_slice_in_dim(stream_all, member * own_rows, own_rows, 0)
    normed_one = layer_norm(stream_all, ln1_gain, ln1_bias).astype(BF)
    wq = w_qkv.transpose(1, 2, 0).reshape(3 * width, D)
    packed = contract_cols(normed_one, wq).astype(BF).reshape(L, 3, heads_local, HD)
    queries, key_rows, value_rows = packed[:, 0], packed[:, 1], packed[:, 2]
    attended, log_sums = attend_forward(queries, key_rows, value_rows, segment_ids)
    sent = fold(attended.reshape(group, own_rows, width))
    got = comm.exchange(sent, 1, "to_rows")

    att_own = unfold(got).transpose(1, 0, 2).reshape(own_rows, D)
    w_out_full = WO.reshape(group, 6, width, 128).transpose(0, 2, 1, 3).reshape(D, D)
    stream_mid = stream_in + dot(att_own, w_out_full) + attn_bias
    normed_two = layer_norm(stream_mid, ln2_gain, ln2_bias).astype(BF)
    own_segments = lax.dynamic_slice_in_dim(segment_ids, member * own_rows, own_rows, 0)
    grad_out = cotangent.astype(F32) * (own_segments != 0).astype(F32)[:, None]
    grad_mlp = grad_out.astype(BF)
    out = stream_mid + mlp_bias
    grad_norm_two = jnp.zeros((own_rows, D), F32)
    grads_up, grads_down = [], []
    for q in range(group):
        pre = dot(normed_two, W2[q, 0])
        act, back = jax.vjp(lambda v: jax.nn.gelu(v, approximate=True), pre)
        act = act.astype(BF)
        out = out + dot(act, W2[q, 1])
        grad_pre = back(contract_cols(grad_mlp, W2[q, 1]))[0].astype(BF)
        grad_norm_two = grad_norm_two + contract_cols(grad_pre, W2[q, 0])
        grads_up.append(contract_rows(normed_two, grad_pre).astype(BF))
        grads_down.append(contract_rows(grad_mlp, act).astype(BF))
    dw = jnp.stack((jnp.stack(grads_up), jnp.stack(grads_down)))
    norm_back_two = jax.vjp(layer_norm, stream_mid, ln2_gain, ln2_bias)[1]
    grad_mid_norm, grad_ln2_gain, grad_ln2_bias = norm_back_two(grad_norm_two)
    grad_mid = grad_out + grad_mid_norm
    grad_attn = grad_mid.astype(BF)
    dwo = contract_rows(grad_attn, att_own).astype(BF).reshape(D, group, width).transpose(1, 0, 2)
    dwo = jnp.pad(dwo, ((0, 0), (0, 0), (0, 256 - width)))
    grad_attended = contract_cols(grad_attn, w_out_full).astype(BF)
    sent = fold(grad_attended.reshape(own_rows, group, width).transpose(1, 0, 2))
    got = comm.exchange(sent, 2, "to_heads")

    grad_heads = unfold(got).reshape(L, heads_local, HD)
    grad_q, grad_k, grad_v = attend_backward(
        queries, key_rows, value_rows, segment_ids, log_sums, grad_heads
    )
    grad_packed = jnp.stack((grad_q, grad_k, grad_v), axis=1).reshape(L, 3 * width)
    dqkv = jnp.pad(contract_rows(normed_one, grad_packed).astype(BF), ((0, 0), (0, 640 - 3 * width)))
    gn = dot(grad_packed, wq).astype(BF).reshape(group, own_rows, D)

    pieces = lambda a: a.reshape(a.shape[:-2] + (ndp // 2, 2, D // ndp, a.shape[-1]))
    grad_norm_one, g_up, g_down, g_out, g_qkv = comm.reduce_all(
        gn, pieces(dw), pieces(dwo), pieces(dqkv)[None]
    )
    norm_back_one = jax.vjp(layer_norm, stream_in, ln1_gain, ln1_bias)[1]
    grad_in_norm, grad_ln1_gain, grad_ln1_bias = norm_back_one(grad_norm_one)
    input_grad = grad_mid + grad_in_norm
    tp = fold(input_grad.astype(BF).reshape(own_rows, group, width).transpose(1, 0, 2))
    step_row = jnp.where(member == 0, timesteps[0], 0).astype(F32)
    vec = jnp.stack(
        (
            grad_ln1_gain,
            grad_ln1_bias,
            jnp.sum(grad_mid, axis=0),
            grad_ln2_gain,
            grad_ln2_bias,
            jnp.sum(grad_out, axis=0),
            jnp.sum(input_grad, axis=0),
            jnp.broadcast_to(step_row, (D,)),
        )
    )
    X, SP = comm.final_exchange(tp, vec)
    rows_table = token_table.shape[0] // ndp
    columns = unfold(X).reshape(ndp * L, width)
    first = lax.axis_index("dp") * rows_table
    hot = (first + jnp.arange(rows_table))[:, None] == IDS.reshape(1, ndp * L)
    grad_token_table = dot(hot.astype(BF), columns)
    steps = SP[:, 7, 0].astype(jnp.int32)
    grad_time_table = jnp.zeros(time_table.shape[:1] + (D,), F32)
    at_row = jnp.arange(time_table.shape[0])[:, None]
    if ndp <= 8:
        for i in range(ndp):
            grad_time_table = grad_time_table + jnp.where(at_row == steps[i], SP[i, 6][None], 0.0)
    else:
        grad_time_table = grad_time_table.at[steps].add(SP[:, 6])
    sums = jnp.sum(SP[:, :6], axis=0)
    return (
        out.astype(BF),
        input_grad,
        grad_token_table,
        grad_time_table,
        sums[0],
        sums[1],
        g_qkv[:, : 3 * width].reshape(-1, 3, width),
        g_out[:, :width].T,
        sums[2],
        sums[3],
        sums[4],
        g_up,
        g_down.T,
        sums[5],
    )


def solution(mesh):
    placed = (
        P("dp"),
        P("dp"),
        P("dp"),
        P(None, "mp"),
        P(None, "mp"),
        P(),
        P(),
        P(None, None, "mp"),
        P("mp", None),
        P(),
        P(),
        P(),
        P(None, "mp"),
        P("mp", None),
        P(),
        P(("dp", "mp"), None),
    )
    ndp, nmp = mesh.shape["dp"], mesh.shape["mp"]
    comm = Tuned if (ndp, nmp) == (8, 4) else Native(ndp, nmp)
    return jax.shard_map(
        functools.partial(on_device, comm),
        mesh=mesh,
        in_specs=placed,
        out_specs=(
            P(("dp", "mp"), None),
            P(("dp", "mp"), None),
            P("dp", "mp"),
            P(),
            P(),
            P(),
            P("dp", None, "mp"),
            P("mp", "dp"),
            P(),
            P(),
            P(),
            P("dp", "mp"),
            P("mp", "dp"),
            P(),
        ),
        check_vma=False,
    )
```

```python
import functools

import jax
import jax.numpy as jnp
from jax import lax
from jax.experimental import pallas as pl
from jax.experimental.pallas import tpu as pltpu
from jax.sharding import PartitionSpec as P

D = 768
HD = 64
L = 1024
QBLK = 512
BF = jnp.bfloat16
F32 = jnp.float32
MESH = pl.DeviceIdType.MESH
ANY = pl.BlockSpec(memory_space=pl.ANY)
VM = pl.BlockSpec(memory_space=pltpu.VMEM)
DMA = pltpu.SemaphoreType.DMA
EPS = 1e-05


def shape(dims, dtype):
    return jax.ShapeDtypeStruct(dims, dtype)


def dot(a, b):
    return jnp.dot(a, b, preferred_element_type=F32)


def contract_rows(left, right):
    return lax.dot_general(left, right, (((0,), (0,)), ((), ())), preferred_element_type=F32)


def contract_cols(left, right):
    return lax.dot_general(left, right, (((1,), (1,)), ((), ())), preferred_element_type=F32)


class Place:
    def __init__(self):
        self.p = p = lax.axis_index("dp")
        self.j = lax.axis_index("mp")
        core, x, y = p % 2, (p // 2) % 2, p // 4
        self.core, self.m = core, p // 2
        self.px = p + 2 - 4 * x
        self.py = p + 4 - 8 * y
        self.pd = self.px + 4 - 8 * y
        self.pc = p + 1 - 2 * core
        self.mx = self.px // 2
        self.my = self.py // 2
        self.md = self.pd // 2

    def z(self, hop):
        return (self.p, (self.j + hop) % 4)

    def at(self, dp):
        return (dp, self.j)


def meet(devices):
    barrier = pltpu.get_barrier_semaphore()
    for device in devices:
        pl.semaphore_signal(barrier, inc=1, device_id=device, device_id_type=MESH)
    pl.semaphore_wait(barrier, len(devices))


def push(src, dst, send, recv, device):
    return pltpu.make_async_remote_copy(
        src_ref=src, dst_ref=dst, send_sem=send, recv_sem=recv, device_id=device, device_id_type=MESH
    )


def params(cid):
    return pltpu.CompilerParams(collective_id=cid, has_side_effects=True, vmem_limit_bytes=60 << 20)


def head_mask(width, h):
    lane = lax.broadcasted_iota(jnp.int32, (1, width), 1)
    return ((lane >= HD * h) & (lane < HD * h + HD)).astype(F32)


def fold(rows):
    half = rows.shape[-2] // 2
    return jnp.concatenate((rows[..., :half, :], rows[..., half:, :]), axis=-1)


def unfold(packed):
    width = packed.shape[-1] // 2
    return jnp.concatenate((packed[..., :width], packed[..., width:]), axis=-2)


CH = 32


def allowed(segc, sq, b, c):
    key = CH * c + lax.broadcasted_iota(jnp.int32, (CH, 256), 0)
    query = 256 * b + lax.broadcasted_iota(jnp.int32, (CH, 256), 1)
    return ((segc[CH * c : CH * c + CH, :] == sq) & (sq != 0)) | (key == query)


def lanes(b):
    return pl.ds(pl.multiple_of(256 * b, 256), 256)


def groups(x):
    return x.reshape(CH // 8, 8, 256)


class Weights:
    def __init__(self, me, shards, W2, WO, zs, zr, ps, pr):
        self.me, self.shards, self.W2, self.WO = me, shards, W2, WO
        self.zs, self.zr, self.ps, self.pr = zs, zr, ps, pr

    def zpart(self, a, q, piece, ref=None):
        if a < 2:
            rows = pl.ds(96 * piece, 96)
            return self.W2.at[q, a, rows, :] if ref is None else ref.at[rows, :]
        base = 192 * q if ref is None else 0
        return (self.WO if ref is None else ref).at[
            pl.ds(base + 48 * (piece // 2), 48), pl.ds(384 * (piece % 2), 384)
        ]

    def part(self, a, q, piece, half=None):
        if a == 0:
            lo, n = (0, 96) if half is None else (48 * half, 48)
            return self.W2.at[q, :, pl.ds(96 * piece + lo, n), :]
        lo, n = (0, 48) if half is None else ((0, 32), (32, 16))[half]
        return self.WO.at[pl.ds(192 * q + 48 * (piece // 2) + lo, n), pl.ds(384 * (piece % 2), 384)]

    def quarter(self, d, k):
        j = self.me.j
        return (j - k + 4) % 4 if d == 0 else (j + k) % 4

    def sends(self, d, k):
        j = self.me.j
        return (j < 3) & (j >= k) if d == 0 else (j > 0) & (j + k <= 3)

    def gets(self, d, k):
        j = self.me.j
        return j >= k + 1 if d == 0 else j + k + 1 <= 3

    def zcopy(self, d, k, a):
        p, q = self.me.p, self.quarter(d, k)
        src = self.zpart(a, q, p, self.shards[a]) if k == 0 else self.zpart(a, q, p)
        return push(src, self.zpart(a, q, p), self.zs.at[d, k, a], self.zr.at[d, k, a], self.me.z(1 if d == 0 else 3))

    def zgot(self, d, k, a):
        dst = self.zpart(a, self.quarter(d, k + 1), self.me.p)
        return push(dst, dst, self.zs.at[d, k, a], self.zr.at[d, k, a], self.me.z(1))

    def zstart(self, k, arrays):
        for d in (0, 1):

            @pl.when(self.sends(d, k))
            def _():
                for a in arrays:
                    self.zcopy(d, k, a).start()

    def zwait(self, k, arrays):
        for d in (0, 1):

            @pl.when(self.gets(d, k))
            def _():
                for a in arrays:
                    self.zgot(d, k, a).wait_recv()

    def routes(self, d, k, a, stage):
        me, q = self.me, self.quarter(d, k + 1)
        if stage == 0:
            return [(self.part(a, q, me.p), me.px), (self.part(a, q, me.p), me.py), (self.part(a, q, me.p), me.pc)]
        if stage == 1:
            return [
                (self.part(a, q, me.py, 0), me.px),
                (self.part(a, q, me.px, 1), me.py),
                (self.part(a, q, me.px), me.pc),
                (self.part(a, q, me.py), me.pc),
            ]
        return [(self.part(a, q, me.pd), me.pc)]

    def arrivals(self, d, k, a, stage):
        me, q = self.me, self.quarter(d, k + 1)
        c = me.pc - me.p
        if stage == 0:
            return [self.part(a, q, me.px), self.part(a, q, me.py), self.part(a, q, me.pc)]
        if stage == 1:
            return [
                self.part(a, q, me.pd, 0),
                self.part(a, q, me.pd, 1),
                self.part(a, q, me.px + c),
                self.part(a, q, me.py + c),
            ]
        return [self.part(a, q, me.pd + c)]

    def pstart(self, k, stage):
        for d in (0, 1):

            @pl.when(self.gets(d, k))
            def _():
                for a in (0, 1):
                    for i, (ref, dp) in enumerate(self.routes(d, k, a, stage)):
                        s = 3 * stage + i if stage < 2 else 7
                        push(ref, ref, self.ps.at[d, k, a, s], self.pr.at[d, k, a, s], self.me.at(dp)).start()

    def pwait(self, k, stage, which, send=False):
        for d in (0, 1):

            @pl.when(self.gets(d, k))
            def _():
                for a in (0, 1):
                    if send:
                        refs = [r for r, _ in self.routes(d, k, a, stage)]
                    else:
                        refs = self.arrivals(d, k, a, stage)
                    for i in which:
                        s = 3 * stage + i if stage < 2 else 7
                        c = push(refs[i], refs[i], self.ps.at[d, k, a, s], self.pr.at[d, k, a, s], self.me.at(self.me.pc))
                        c.wait_send() if send else c.wait_recv()

    def finish(self):
        for k in range(3):
            self.pwait(k, 0, (2,))
            self.pwait(k, 1, (2, 3))
            self.pwait(k, 2, (0,))
            self.pwait(k, 0, (0, 1, 2), send=True)
            self.pwait(k, 1, (0, 1, 2, 3), send=True)
            self.pwait(k, 2, (0,), send=True)
            for d in (0, 1):

                @pl.when(self.sends(d, k))
                def _():
                    for a in (0, 1, 2):
                        self.zcopy(d, k, a).wait_send()


def front_kernel(
    emb, trow, ids, segc, segr, par, wq, w_up, w_down, w_out,
    qm_o, k_o, v_o, kt_o, n1_o, x_o, lse_o, att_o, IDS, W2, WO,
    E, TR, vt, s, pb, ot, sendb, attg, own2, own_o,
    es, er, ts, tr, is_, ir, zs, zr, ps, pr, as_, ar, ls,
):
    me = Place()
    p, j = me.p, me.j
    meet([me.z(1), me.z(2), me.z(3)] + [me.at((p + k) % 8) for k in range(1, 8)])
    w = Weights(me, (own2.at[0], own2.at[1], own_o), W2, WO, zs, zr, ps, pr)

    def ecopy(d, k):
        q = w.quarter(d, k)
        return (emb if k == 0 else E.at[q], E.at[q], es.at[d, k], er.at[d, k], me.z(1 if d == 0 else 3))

    def estart(k):
        for d in (0, 1):

            @pl.when(w.sends(d, k))
            def _():
                push(*ecopy(d, k)).start()

    def ewait(k):
        for d in (0, 1):

            @pl.when(w.gets(d, k))
            def _():
                dst = E.at[w.quarter(d, k + 1)]
                push(dst, dst, es.at[d, k], er.at[d, k], me.z(1)).wait_recv()

    here = [
        pltpu.make_async_copy(emb, E.at[j], ls.at[0]),
        pltpu.make_async_copy(trow, TR.at[j], ls.at[1]),
        pltpu.make_async_copy(ids, IDS.at[p], ls.at[2]),
    ]
    load = [
        pltpu.make_async_copy(w_up, own2.at[0], ls.at[3]),
        pltpu.make_async_copy(w_down, own2.at[1], ls.at[4]),
        pltpu.make_async_copy(w_out, own_o, ls.at[5]),
    ]
    keep = [
        pltpu.make_async_copy(own2, W2.at[j], ls.at[3]),
        pltpu.make_async_copy(own_o, WO.at[pl.ds(192 * j, 192), :], ls.at[5]),
    ]
    small = [push(trow, TR.at[j], ts.at[k - 1], tr.at[k - 1], me.z(k)) for k in (1, 2, 3)]
    small_ids = [push(ids, IDS.at[p], is_.at[k - 1], ir.at[k - 1], me.at((p + k) % 8)) for k in range(1, 8)]

    estart(0)
    for c in load + small + here + small_ids:
        c.start()
    for c in load:
        c.wait()
    for c in keep:
        c.start()
    w.zstart(0, (0,))
    ewait(0)
    estart(1)
    w.zstart(0, (1,))
    ewait(1)
    estart(2)
    w.zstart(0, (2,))
    w.zwait(0, (0,))
    w.zstart(1, (0,))
    w.zwait(0, (1, 2))
    w.zstart(1, (1, 2))
    w.pstart(0, 0)
    ewait(2)
    for c in small:
        c.wait()
    here[0].wait()
    here[1].wait()

    time_row = jnp.concatenate([TR[q].astype(F32)[0:1, 0:192] for q in range(4)], axis=1)
    gain, shift = par[0:1, :], par[1:2, :]
    for r in range(4):
        h, o = r // 2, 256 * (r % 2)
        rows = slice(256 * r, 256 * r + 256)
        x = jnp.concatenate([E[q, o : o + 256, 192 * h : 192 * h + 192] for q in range(4)], axis=1)
        x = x.astype(F32) + time_row
        centered = x - jnp.mean(x, axis=1, keepdims=True)
        variance = jnp.mean(centered * centered, axis=1, keepdims=True)
        normed = (centered * lax.rsqrt(variance + EPS) * gain + shift).astype(BF)
        n1_o[rows, :] = normed

        @pl.when(j == r)
        def _():
            x_o[...] = x

        q = contract_cols(normed, wq[0:192, :]).astype(BF).astype(F32) * 0.125
        for i in range(3):
            qm_o[i, rows, :] = (q * head_mask(192, i)).astype(BF)
        k_o[rows, :] = contract_cols(normed, wq[192:384, :]).astype(BF)
        v_o[rows, :] = contract_cols(normed, wq[384:576, :]).astype(BF)
        kt_o[:, rows] = contract_cols(wq[192:384, :], normed).astype(BF)
        vt[:, rows] = contract_cols(wq[384:576, :], normed).astype(BF)

    def att_copy(b):
        return push(sendb.at[b], attg.at[j], as_.at[b], ar.at[j], (p, b))

    def step0():
        w.zwait(1, (0,))
        w.zstart(2, (0,))

    def step1():
        w.pwait(0, 0, (0, 1))
        w.pstart(0, 1)

    def step2():
        w.zwait(1, (1, 2))
        w.zstart(2, (1, 2))
        w.pstart(1, 0)

    def step3():
        w.pwait(0, 1, (0, 1))
        w.pstart(0, 2)

    def step4():
        w.pwait(1, 0, (0, 1))
        w.pstart(1, 1)

    def step5():
        w.zwait(2, (0, 1, 2))
        w.pstart(2, 0)

    steps = {0: step0, 2: step1, 4: step2, 6: step3, 10: step4, 11: step5}

    def slot(i, n):
        for k, step in {k: v for k, v in steps.items() if k % 3 == n}.items():
            pl.when(i == k // 3)(step)

    @pl.loop(0, 4)
    def _(i):
        b = (j + 1 + i) % 4
        sq = segr[0:1, lanes(b)]
        for h in range(3):
            s[h] = contract_cols(k_o[...], qm_o[h, lanes(b), :])
        slot(i, 0)
        top = [jnp.full((8, 256), -jnp.inf, F32)] * 3
        for c in range(L // CH):
            rows = slice(CH * c, CH * c + CH)
            ok = allowed(segc, sq, b, c)
            for h in range(3):
                x = jnp.where(ok, s[h, rows, :], -1e30)
                s[h, rows, :] = x
                top[h] = jnp.maximum(top[h], jnp.max(groups(x), axis=0))
        top = [jnp.max(m, axis=0, keepdims=True) for m in top]
        slot(i, 1)
        total = [jnp.zeros((8, 256), F32)] * 3
        for c in range(L // CH):
            rows = slice(CH * c, CH * c + CH)
            for h in range(3):
                e = jnp.exp(s[h, rows, :] - top[h])
                pb[h, rows, :] = e.astype(BF)
                total[h] = total[h] + jnp.sum(groups(e), axis=0)
        for h in range(3):
            t = jnp.sum(total[h], axis=0, keepdims=True)
            lse_o[3 * b + h] = top[h] + jnp.log(t)
            part = slice(64 * h, 64 * h + 64)
            ot[part, :] = dot(vt[part, :], pb[h]) * (1.0 / t)
        sendb[b] = fold(ot[...].T.astype(BF))

        @pl.when(b != j)
        def _():
            att_copy(b).start()

        slot(i, 2)

    attg[j] = sendb[j]
    w.pwait(1, 1, (0, 1))
    w.pstart(1, 2)
    for q in range(4):

        @pl.when(j != q)
        def _():
            push(attg.at[q], attg.at[q], as_.at[q], ar.at[q], me.z(1)).wait_recv()

    att_o[...] = jnp.concatenate([unfold(attg[q]) for q in range(4)], axis=1)
    w.pwait(2, 0, (0, 1))
    w.pstart(2, 1)
    w.pwait(2, 1, (0, 1))
    w.pstart(2, 2)
    for b in range(4):

        @pl.when(j != b)
        def _():
            att_copy(b).wait_send()

    for k in range(3):
        for d in (0, 1):

            @pl.when(w.sends(d, k))
            def _():
                push(*ecopy(d, k)).wait_send()

    w.finish()
    for c in small_ids + here[2:] + keep:
        c.wait()


def front(emb, trow, ids, segc, segr, par, wq, w_up, w_down, w_out):
    return pl.pallas_call(
        front_kernel,
        out_shape=(
            shape((3, L, 192), BF),
            shape((L, 192), BF),
            shape((L, 192), BF),
            shape((192, L), BF),
            shape((L, D), BF),
            shape((256, D), F32),
            shape((12, 1, 256), F32),
            shape((256, D), BF),
            shape((8, 8, 128), jnp.int32),
            shape((4, 2, D, D), BF),
            shape((D, D), BF),
        ),
        in_specs=[ANY] * 3 + [VM] * 4 + [ANY] * 3,
        out_specs=(VM,) * 8 + (ANY,) * 3,
        scratch_shapes=[
            pltpu.VMEM((4, 512, 384), BF),
            pltpu.VMEM((4, 16, 256), BF),
            pltpu.VMEM((192, L), BF),
            pltpu.VMEM((3, L, 256), F32),
            pltpu.VMEM((3, L, 256), BF),
            pltpu.VMEM((192, 256), F32),
            pltpu.VMEM((4, 128, 384), BF),
            pltpu.VMEM((4, 128, 384), BF),
            pltpu.VMEM((2, D, D), BF),
            pltpu.VMEM((192, D), BF),
            DMA((2, 3)),
            DMA((2, 3)),
            DMA((3,)),
            DMA((3,)),
            DMA((7,)),
            DMA((7,)),
            DMA((2, 3, 3)),
            DMA((2, 3, 3)),
            DMA((2, 3, 2, 8)),
            DMA((2, 3, 2, 8)),
            DMA((4,)),
            DMA((4,)),
            DMA((6,)),
        ],
        compiler_params=params(0),
        name="front",
    )(emb, trow, ids, segc, segr, par, wq, w_up, w_down, w_out)


def norm_stats(x):
    centered = x - jnp.mean(x, axis=1, keepdims=True)
    scale = lax.rsqrt(jnp.mean(centered * centered, axis=1, keepdims=True) + EPS)
    return centered * scale, scale


def norm_back(grad, gain, hat, scale):
    t = grad * gain
    return scale * (t - jnp.mean(t, axis=1, keepdims=True) - hat * jnp.mean(t * hat, axis=1, keepdims=True))


def rows_sum(x):
    return jnp.sum(x, axis=0, keepdims=True)


def mid_kernel(
    att, x, wo, w2, cot, segc, par,
    out_o, gmid_o, gatt_o, dw_o, dwo_o, vec_o,
    sm, hat, sc, n2, n2t, gmt, gm, acc, gn2,
):
    q = pl.program_id(0)

    @pl.when(q == 0)
    def _():
        mid = x[...] + dot(att[...], wo[...]) + par[2:3, :]
        sm[...] = mid
        h, scale = norm_stats(mid)
        hat[...] = h
        sc[...] = scale
        normed = (h * par[3:4, :] + par[4:5, :]).astype(BF)
        n2[...] = normed
        n2t[...] = normed.astype(F32).T.astype(BF)
        valid = (segc[...] != 0).astype(F32)
        grad = cot[...].astype(F32) * valid
        gm[...] = grad.astype(BF)
        gmt[...] = grad.T.astype(BF)
        acc[...] = mid + par[5:6, :]
        gn2[...] = jnp.zeros_like(gn2)

    up, down = w2[0, 0], w2[0, 1]
    pre = dot(n2[...], up)
    c = 0.7978845608028654
    cubic = c * (pre + 0.044715 * pre * pre * pre)
    t = jnp.tanh(cubic)
    act = (0.5 * pre * (1.0 + t)).astype(BF)
    slope = 0.5 * (1.0 + t) + 0.5 * pre * (1.0 - t * t) * (c * (1.0 + 3 * 0.044715 * pre * pre))
    acc[...] += dot(act, down)
    grad_pre = (contract_cols(gm[...], down) * slope).astype(BF)
    gn2[...] += contract_cols(grad_pre, up)
    dw_o[0, 0] = dot(n2t[...], grad_pre).astype(BF)
    dw_o[1, 0] = dot(gmt[...], act).astype(BF)

    @pl.when(q == 3)
    def _():
        out_o[...] = acc[...].astype(BF)
        grad = cot[...].astype(F32) * (segc[...] != 0).astype(F32)
        gn, h = gn2[...], hat[...]
        gmid = grad + norm_back(gn, par[3:4, :], h, sc[...])
        gmid_o[...] = gmid
        vec_o[...] = jnp.zeros_like(vec_o)
        vec_o[2:3, :] = rows_sum(gmid)
        vec_o[3:4, :] = rows_sum(gn * h)
        vec_o[4:5, :] = rows_sum(gn)
        vec_o[5:6, :] = rows_sum(grad)
        ga = gmid.astype(BF)
        gatt_o[...] = contract_cols(ga, wo[...]).astype(BF)
        full = dot(gmid.T.astype(BF), att[...]).astype(BF)
        for i in range(4):
            dwo_o[i, :, 0:192] = full[:, 192 * i : 192 * i + 192]
            dwo_o[i, :, 192:256] = jnp.zeros((D, 64), BF)


def mid(att, x, wo, w2, cot, segc, par):
    whole = lambda a: pl.BlockSpec(a.shape, lambda q: (0,) * a.ndim)
    keep = lambda *dims: pl.BlockSpec(dims, lambda q: (0,) * len(dims))
    return pl.pallas_call(
        mid_kernel,
        grid=(4,),
        out_shape=(
            shape((256, D), BF),
            shape((256, D), F32),
            shape((256, D), BF),
            shape((2, 4, D, D), BF),
            shape((4, D, 256), BF),
            shape((8, D), F32),
        ),
        in_specs=[
            whole(att),
            whole(x),
            whole(wo),
            pl.BlockSpec((1, 2, D, D), lambda q: (q, 0, 0, 0)),
            whole(cot),
            whole(segc),
            whole(par),
        ],
        out_specs=(
            keep(256, D),
            keep(256, D),
            keep(256, D),
            pl.BlockSpec((2, 1, D, D), lambda q: (0, q, 0, 0)),
            keep(4, D, 256),
            keep(8, D),
        ),
        scratch_shapes=[
            pltpu.VMEM((256, D), F32),
            pltpu.VMEM((256, D), F32),
            pltpu.VMEM((256, 1), F32),
            pltpu.VMEM((256, D), BF),
            pltpu.VMEM((D, 256), BF),
            pltpu.VMEM((D, 256), BF),
            pltpu.VMEM((256, D), BF),
            pltpu.VMEM((256, D), F32),
            pltpu.VMEM((256, D), F32),
        ],
        compiler_params=pltpu.CompilerParams(vmem_limit_bytes=60 << 20, dimension_semantics=("arbitrary",)),
        name="mid",
    )(att, x, wo, w2, cot, segc, par)


class Line:
    def __init__(self, me, acc, up, down, sems):
        self.me, self.acc, self.up, self.down = me, acc, up, down
        self.us, self.ur, self.ds, self.dr = (sems.at[i] for i in range(4))

    def send(self, q, d):
        if d == 0:
            return push(self.acc(q), self.up.at[q], self.us.at[q], self.ur.at[q], self.me.z(1))
        return push(self.acc(q), self.down.at[q], self.ds.at[q], self.dr.at[q], self.me.z(3))

    def end(self, q, d):
        @pl.when(self.me.j == (0 if d == 0 else 3))
        def _():
            self.send(q, d).start()

    def first(self):
        for q in (3, 2, 1):
            self.end(q, 0)
        for q in (0, 1, 2):
            self.end(q, 1)

    def inner(self, steps):
        for q, d, j in steps:

            @pl.when(self.me.j == j)
            def _():
                c = self.send(q, d)
                c.wait_recv()
                ref = self.acc(q)
                ref[...] = ref[...] + (self.up if d == 0 else self.down)[q]
                c.start()

    def finish(self, out):
        j = self.me.j
        for q in range(4):

            @pl.when(j == q)
            def _():
                total = self.acc(q)[...].astype(F32)
                if q > 0:
                    self.send(q, 0).wait_recv()
                    total = total + self.up[q].astype(F32)
                if q < 3:
                    self.send(q, 1).wait_recv()
                    total = total + self.down[q].astype(F32)
                out[...] = total

    def close(self):
        j = self.me.j
        for q in range(4):

            @pl.when(j < q)
            def _():
                self.send(q, 0).wait_send()

            @pl.when(j > q)
            def _():
                self.send(q, 1).wait_send()


NEAR = ((3, 0, 1), (0, 1, 2))
FAR = ((3, 0, 2), (0, 1, 1), (2, 0, 1), (1, 1, 2))


class Unit:
    def __init__(self, me, src, acc, rc, rx, ry, rx2, ry2, sems, lsem):
        self.me, self.src, self.acc = me, src, acc
        self.rc, self.rx, self.ry, self.rx2, self.ry2 = rc, rx, ry, rx2, ry2
        self.s, self.r, self.lsem = sems.at[0], sems.at[1], lsem
        self.nq = acc.shape[0]

    def copies(self, stage):
        me, acc, s, r = self.me, self.acc, self.s, self.r
        lo, hi = pl.ds(0, 48), pl.ds(48, 48)
        if stage == 0:
            return [push(self.src.at[:, :, 1 - me.core], self.rc, s.at[0], r.at[0], me.at(me.pc))]
        if stage == 1:
            return [
                push(acc.at[:, me.md, lo], self.rx.at[:, 1], s.at[1], r.at[1], me.at(me.px)),
                push(acc.at[:, me.md, hi], self.ry.at[:, 1], s.at[2], r.at[2], me.at(me.py)),
                push(acc.at[:, me.mx, lo], self.rx.at[:, 0], s.at[3], r.at[3], me.at(me.px)),
                push(acc.at[:, me.my, hi], self.ry.at[:, 0], s.at[4], r.at[4], me.at(me.py)),
            ]
        return [
            push(acc.at[:, me.my, lo], self.ry2, s.at[5], r.at[5], me.at(me.py)),
            push(acc.at[:, me.mx, hi], self.rx2, s.at[6], r.at[6], me.at(me.px)),
        ]

    def load(self):
        return pltpu.make_async_copy(self.src.at[:, :, self.me.core], self.acc, self.lsem)

    def begin(self):
        self.copies(0)[0].start()
        self.load().start()

    def chip(self):
        self.load().wait()
        self.copies(0)[0].wait_recv()

        @pl.loop(0, self.nq)
        def _(q):
            for m in range(4):
                self.acc[q, m] = self.acc[q, m] + self.rc[q, m]

    def cross(self):
        for c in self.copies(1):
            c.start()

    def turn(self):
        me = self.me
        first = self.copies(1)
        for c in first[:2]:
            c.wait()
        second = self.copies(2)

        @pl.loop(0, self.nq)
        def _(q):
            self.acc[q, me.my, 0:48] = self.acc[q, me.my, 0:48] + self.rx[q, 1]
            self.acc[q, me.mx, 48:96] = self.acc[q, me.mx, 48:96] + self.ry[q, 1]

        for c in second:
            c.start()
        for c in first[2:]:
            c.wait()

        @pl.loop(0, self.nq)
        def _(q):
            self.acc[q, me.m, 0:48] = self.acc[q, me.m, 0:48] + self.rx[q, 0]
            self.acc[q, me.m, 48:96] = self.acc[q, me.m, 48:96] + self.ry[q, 0]

    def settle(self):
        me = self.me
        for c in self.copies(2):
            c.wait()

        @pl.loop(0, self.nq)
        def _(q):
            self.acc[q, me.m, 0:48] = self.acc[q, me.m, 0:48] + self.ry2[q]
            self.acc[q, me.m, 48:96] = self.acc[q, me.m, 48:96] + self.rx2[q]

        self.copies(0)[0].wait_send()

    def own(self, q):
        return self.acc.at[q, self.me.m]


SHAPES = ((4, 768), (4, 768), (4, 256), (3, 256))


def back_kernel(
    gatt, qm, k, v, kt, lse, n1, wq, x, gmid, segc, segr, par, vec, IDS, step, dw, dwo,
    o_in, o_tok, o_up, o_down, o_out, o_qkv, o_sp,
    *scratch,
):
    me = Place()
    p, j = me.p, me.j
    meet([me.z(1), me.z(2), me.z(3)] + [me.at((p + i) % 8) for i in range(1, 8)])
    it = iter(scratch)
    take = lambda n: [next(it) for _ in range(n)]
    sendb, gbuf, dom, s, dp, pb, dsb, dqt, dqn, dk, dv, gn = take(12)
    as_, ar = take(2)
    gacc, gup, gdown, gsem = take(4)
    qk, tb, X, hot, vbuf, SZ, vs = take(7)
    vzs, vzr, ts, tr, ps, pr, vps, vpr, ls = take(9)
    sources = (dw.at[1], dw.at[0], dwo, qk)
    units, lines = [], []
    for i, src in enumerate(sources):
        acc, rc, rx, ry, rx2, ry2, sems, lsem = take(8)
        unit = Unit(me, src, acc, rc, rx, ry, rx2, ry2, sems, lsem)
        units.append(unit)
        if i < 3:
            up, down, sem = take(3)
            lines.append(Line(me, unit.own, up, down, sem))
    own = Line(me, lambda q: gacc.at[q], gup, gdown, gsem)

    def to_heads(d):
        return push(sendb.at[d], gbuf.at[j], as_.at[d], ar.at[j], (p, d))

    for d in range(4):
        sendb[d] = fold(gatt[:, 192 * d : 192 * d + 192])

        @pl.when(j != d)
        def _():
            to_heads(d).start()

    gbuf[j] = sendb[j]
    for u in units[:3]:
        u.begin()
    dk[...] = jnp.zeros_like(dk)
    dv[...] = jnp.zeros_like(dv)

    def step0():
        units[0].chip()
        units[0].cross()

    def step1():
        units[1].chip()

    def step2():
        units[2].chip()

    def step3():
        units[0].turn()
        units[1].cross()

    steps = {0: step0, 1: step1, 2: step2, 11: step3}

    def slot(i, n):
        for c, fn in {c: fn for c, fn in steps.items() if c % 3 == n}.items():
            pl.when(i == c // 3)(fn)

    @pl.loop(0, 4)
    def _(i):
        b = (j + i) % 4
        sq = segr[0:1, lanes(b)]

        @pl.when(i > 0)
        def _():
            push(gbuf.at[b], gbuf.at[b], as_.at[b], ar.at[b], me.z(1)).wait_recv()

        do = unfold(gbuf[b]).astype(F32)
        for h in range(3):
            dom[h] = (do * head_mask(192, h)).astype(BF)
            s[h] = contract_cols(k[...], qm[h, lanes(b), :])
            dp[h] = contract_cols(v[...], dom[h])
        slot(i, 0)
        ls_ = [lse[3 * b + h] for h in range(3)]
        inner = [jnp.zeros((8, 256), F32)] * 3
        for c in range(L // CH):
            rows = slice(CH * c, CH * c + CH)
            ok = allowed(segc, sq, b, c)
            for h in range(3):
                e = jnp.exp(jnp.where(ok, s[h, rows, :], -1e30) - ls_[h])
                s[h, rows, :] = e
                pb[rows, 256 * h : 256 * h + 256] = e.astype(BF)
                inner[h] = inner[h] + jnp.sum(groups(e * dp[h, rows, :]), axis=0)
        inner = [jnp.sum(a, axis=0, keepdims=True) for a in inner]
        slot(i, 1)
        for c in range(L // CH):
            rows = slice(CH * c, CH * c + CH)
            for h in range(3):
                grad = s[h, rows, :] * (dp[h, rows, :] - inner[h])
                dsb[rows, 256 * h : 256 * h + 256] = grad.astype(BF)
        dv[...] += dot(pb[...], dom[...].reshape(768, 192))
        dk[...] += dot(dsb[...], qm[:, lanes(b), :].reshape(768, 192))
        for h in range(3):
            part = slice(64 * h, 64 * h + 64)
            dqt[part, lanes(b)] = dot(kt[part, :], dsb[:, 256 * h : 256 * h + 256]) * 0.125
        slot(i, 2)

    for q, starts in ((3, ((3, 0),)), (0, ((0, 1),)), (2, ((2, 0),)), (1, ((1, 1), (1, 0), (2, 1)))):
        rows = slice(256 * q, 256 * q + 256)
        dq = dqt[:, rows].T.astype(BF)
        dqn[rows, :] = dq
        total = dot(dq, wq[0:192, :]) + dot(dk[rows, :].astype(BF), wq[192:384, :])
        gacc[q] = (total + dot(dv[rows, :].astype(BF), wq[384:576, :])).astype(BF)
        for block, d in starts:
            own.end(block, d)
    for i, grad in enumerate((dqn[...], dk[...].astype(BF), dv[...].astype(BF))):
        full = contract_rows(n1[...], grad).astype(BF)
        for piece in range(8):
            qk[i, piece // 2, piece % 2, :, 0:192] = full[96 * piece : 96 * piece + 96, :]
            qk[i, piece // 2, piece % 2, :, 192:256] = jnp.zeros((96, 64), BF)
    units[3].begin()
    own.inner(NEAR)
    units[3].chip()
    units[0].settle()
    own.inner(FAR)
    units[1].turn()
    units[2].cross()
    units[3].cross()
    own.finish(gn)
    lines[0].first()

    hat, scale = norm_stats(x[...])
    grad = gn[...]
    dx = gmid[...] + norm_back(grad, par[0:1, :], hat, scale)
    o_in[...] = dx
    dxb = dx.astype(BF)

    def to_columns(d):
        return push(tb.at[d], X.at[p, j], ts.at[d], tr.at[j], (p, d))

    for d in range(4):
        tb[d] = fold(dxb[:, 192 * d : 192 * d + 192])

        @pl.when(j != d)
        def _():
            to_columns(d).start()

    X[p, j] = tb[j]
    vbuf[...] = vec[...]
    vbuf[0:1, :] = rows_sum(grad * hat)
    vbuf[1:2, :] = rows_sum(grad)
    vbuf[6:7, :] = rows_sum(dx)
    first = jnp.where(j == 0, step[0], 0).astype(F32)
    vbuf[7:8, :] = jnp.full((1, D), 1.0, F32) * first
    small = [push(vbuf, SZ.at[j], vzs.at[i - 1], vzr.at[i - 1], me.z(i)) for i in (1, 2, 3)]
    for c in small:
        c.start()
    SZ[j] = vbuf[...]
    units[1].settle()
    lines[1].first()
    lines[0].inner(NEAR)
    for c in small:
        c.wait()
    vs[...] = SZ[0] + SZ[1] + SZ[2] + SZ[3]
    out_v = [push(vs, o_sp.at[p], vps.at[i - 1], vpr.at[i - 1], me.at((p + i) % 8)) for i in range(1, 8)]
    for c in out_v:
        c.start()
    o_sp[p] = vs[...]

    for q in range(4):

        @pl.when(j != q)
        def _():
            push(X.at[p, q], X.at[p, q], ts.at[q], tr.at[q], me.z(1)).wait_recv()

    half = (pl.ds(0, 2), pl.ds(2, 2))

    def to(ref, i, dev):
        return push(ref, ref, ps.at[i], pr.at[i], me.at(dev))

    first_hop = [to(X.at[p], 0, me.px), to(X.at[p], 1, me.py), to(X.at[p], 2, me.pc)]
    for c in first_hop:
        c.start()

    def table(d, start=False):
        vocab = 1024 * p + lax.broadcasted_iota(jnp.int32, (1024, 128), 0)
        for g in range(8):
            hot[:, 128 * g : 128 * g + 128] = (vocab == IDS[d, g : g + 1, :]).astype(F32).astype(BF)
        rows = jnp.concatenate([unfold(X[d, q]) for q in range(4)], axis=0)
        part = dot(hot[...], rows)
        if start:
            o_tok[...] = part
        else:
            o_tok[...] += part

    here = me.pc - p
    table(p, start=True)
    to(X.at[me.pc], 2, me.pc).wait_recv()
    to(X.at[me.px], 0, me.px).wait_recv()
    to(X.at[me.py], 1, me.py).wait_recv()
    second = [
        to(X.at[me.py, half[0]], 3, me.px),
        to(X.at[me.px, half[1]], 4, me.py),
        to(X.at[me.px], 5, me.pc),
        to(X.at[me.py], 6, me.pc),
    ]
    for c in second:
        c.start()
    table(me.pc)
    units[2].turn()
    units[3].turn()
    table(me.px)
    lines[0].inner(FAR)
    lines[1].inner(NEAR)
    table(me.py)
    to(X.at[me.pd, half[0]], 3, me.px).wait_recv()
    to(X.at[me.pd, half[1]], 4, me.px).wait_recv()
    third = to(X.at[me.pd], 7, me.pc)
    third.start()
    units[2].settle()
    lines[2].first()
    units[3].settle()
    table(me.pd)
    to(X.at[me.px + here], 5, me.pc).wait_recv()
    table(me.px + here)
    lines[1].inner(FAR)
    lines[2].inner(NEAR)
    to(X.at[me.py + here], 6, me.pc).wait_recv()
    table(me.py + here)
    lines[2].inner(FAR)
    to(X.at[me.pd + here], 7, me.pc).wait_recv()
    table(me.pd + here)
    lines[0].finish(o_down)
    lines[1].finish(o_up)
    lines[2].finish(o_out)
    for i in range(3):
        o_qkv[i] = units[3].acc[i, me.m].astype(F32)
    for c in out_v:
        c.wait()
    for c in first_hop + second + [third]:
        c.wait_send()
    for d in range(4):

        @pl.when(j != d)
        def _():
            to_heads(d).wait_send()
            to_columns(d).wait_send()

    for line in lines + [own]:
        line.close()


def back(gatt, qm, k, v, kt, lse, n1, wq, x, gmid, segc, segr, par, vec, ids, step, dw, dwo):
    scratch = [
        pltpu.VMEM((4, 128, 384), BF),
        pltpu.VMEM((4, 128, 384), BF),
        pltpu.VMEM((3, 256, 192), BF),
        pltpu.VMEM((3, L, 256), F32),
        pltpu.VMEM((3, L, 256), F32),
        pltpu.VMEM((L, 768), BF),
        pltpu.VMEM((L, 768), BF),
        pltpu.VMEM((192, L), F32),
        pltpu.VMEM((L, 192), BF),
        pltpu.VMEM((L, 192), F32),
        pltpu.VMEM((L, 192), F32),
        pltpu.VMEM((256, D), F32),
        DMA((4,)),
        DMA((4,)),
        pltpu.VMEM((4, 256, D), BF),
        pltpu.VMEM((4, 256, D), BF),
        pltpu.VMEM((4, 256, D), BF),
        DMA((4, 4)),
        pltpu.VMEM((3, 4, 2, 96, 256), BF),
        pltpu.VMEM((4, 128, 384), BF),
        pltpu.VMEM((8, 4, 128, 384), BF),
        pltpu.VMEM((1024, 1024), BF),
        pltpu.VMEM((8, D), F32),
        pltpu.VMEM((4, 8, D), F32),
        pltpu.VMEM((8, D), F32),
        DMA((3,)),
        DMA((3,)),
        DMA((4,)),
        DMA((4,)),
        DMA((8,)),
        DMA((8,)),
        DMA((7,)),
        DMA((7,)),
        DMA((2,)),
    ]
    for i, (nq, w) in enumerate(SHAPES):
        scratch += [
            pltpu.VMEM((nq, 4, 96, w), BF),
            pltpu.VMEM((nq, 4, 96, w), BF),
            pltpu.VMEM((nq, 2, 48, w), BF),
            pltpu.VMEM((nq, 2, 48, w), BF),
            pltpu.VMEM((nq, 48, w), BF),
            pltpu.VMEM((nq, 48, w), BF),
            DMA((2, 7)),
            DMA,
        ]
        if i < 3:
            scratch += [pltpu.VMEM((4, 96, w), BF), pltpu.VMEM((4, 96, w), BF), DMA((4, 4))]
    return pl.pallas_call(
        back_kernel,
        out_shape=(
            shape((256, D), F32),
            shape((1024, 192), F32),
            shape((96, D), F32),
            shape((96, D), F32),
            shape((96, 256), F32),
            shape((3, 96, 256), F32),
            shape((8, 8, D), F32),
        ),
        in_specs=[VM] * 15 + [pl.BlockSpec(memory_space=pltpu.SMEM)] + [ANY] * 2,
        out_specs=(VM,) * 7,
        scratch_shapes=scratch,
        compiler_params=params(1),
        name="back",
    )(gatt, qm, k, v, kt, lse, n1, wq, x, gmid, segc, segr, par, vec, ids, step, dw, dwo)

class Native:
    def __init__(self, ndp, nmp):
        self.ndp, self.nmp = ndp, nmp

    def gather_all(self, emb, trow, ids, w2, wo):
        over_mp = lambda a: lax.all_gather(a, "mp", axis=0, tiled=False)
        return (
            over_mp(emb),
            over_mp(trow),
            lax.all_gather(ids, "dp", axis=0, tiled=False),
            over_mp(w2),
            over_mp(wo),
        )

    def exchange(self, x, cid, name):
        return lax.all_to_all(x, "mp", split_axis=0, concat_axis=0, tiled=True)

    def reduce_all(self, gn, dw, dwo, dqkv):
        sum_mp = lambda a: lax.psum_scatter(a.astype(F32), "mp", scatter_dimension=0, tiled=True)
        sum_dp = lambda a: lax.psum_scatter(a, "dp", scatter_dimension=0, tiled=True)
        flat = lambda a: a.reshape(D, a.shape[-1])
        return (
            sum_mp(gn).reshape(gn.shape[1:]),
            sum_dp(flat(sum_mp(dw[0]))),
            sum_dp(flat(sum_mp(dw[1]))),
            sum_dp(flat(sum_mp(dwo[..., : D // self.nmp]))),
            sum_dp(flat(dqkv[..., : 3 * D // self.nmp].astype(F32))),
        )

    def final_exchange(self, tp, vec):
        x = lax.all_to_all(tp, "mp", split_axis=0, concat_axis=0, tiled=True)
        return (
            lax.all_gather(x, "dp", axis=0, tiled=False),
            lax.all_gather(lax.psum(vec, "mp"), "dp", axis=0, tiled=False),
        )


def layer_norm(stream, gain, shift):
    average = jnp.mean(stream, axis=-1, keepdims=True)
    centered = stream - average
    variance = jnp.mean(centered * centered, axis=-1, keepdims=True)
    return centered * lax.rsqrt(variance + 1e-05) * gain + shift


def allowed_pairs(seg_query, segments, first_row):
    key_pos = jnp.arange(L)
    query_pos = first_row + jnp.arange(QBLK)
    same_text = seg_query[:, None] == segments[None, :]
    self_or_text = (seg_query[:, None] != 0) | (query_pos[:, None] == key_pos[None, :])
    return same_text & self_or_text


def attend_forward(queries, key_rows, value_rows, segments):
    outputs = []
    log_parts = []
    for block_index in range(L // QBLK):
        first_row = block_index * QBLK
        query_block = queries[first_row : first_row + QBLK]
        allowed = allowed_pairs(segments[first_row : first_row + QBLK], segments, first_row)
        scores = jnp.einsum("qhd,khd->hqk", query_block, key_rows, preferred_element_type=F32) * 0.125
        masked = jnp.where(allowed[None], scores, -1e30)
        highest = jnp.max(masked, axis=-1, keepdims=True)
        exponents = jnp.exp(masked - highest)
        totals = jnp.sum(exponents, axis=-1, keepdims=True)
        weights = (exponents / totals).astype(BF)
        outputs.append(jnp.einsum("hqk,khd->qhd", weights, value_rows, preferred_element_type=F32).astype(BF))
        log_parts.append((highest + jnp.log(totals))[..., 0])
    return (jnp.concatenate(outputs, axis=0), jnp.concatenate(log_parts, axis=1))


def attend_backward(queries, key_rows, value_rows, segments, log_sums, grad_heads):
    grad_keys = jnp.zeros(key_rows.shape, F32)
    grad_values = jnp.zeros(value_rows.shape, F32)
    grad_queries = []
    for block_index in range(L // QBLK):
        first_row = block_index * QBLK
        query_block = queries[first_row : first_row + QBLK]
        grad_block = grad_heads[first_row : first_row + QBLK]
        allowed = allowed_pairs(segments[first_row : first_row + QBLK], segments, first_row)
        scores = jnp.einsum("qhd,khd->hqk", query_block, key_rows, preferred_element_type=F32) * 0.125
        masked = jnp.where(allowed[None], scores, -1e30)
        probs = jnp.exp(masked - log_sums[:, first_row : first_row + QBLK, None])
        rounded = probs.astype(BF)
        grad_probs = jnp.einsum("qhd,khd->hqk", grad_block, value_rows, preferred_element_type=F32)
        inner = jnp.sum(probs * grad_probs, axis=-1, keepdims=True)
        grad_scores = (probs * (grad_probs - inner)).astype(BF)
        grad_queries.append(
            jnp.einsum("hqk,khd->qhd", grad_scores, key_rows, preferred_element_type=F32) * 0.125
        )
        grad_keys = (
            grad_keys
            + jnp.einsum("hqk,qhd->khd", grad_scores, query_block, preferred_element_type=F32) * 0.125
        )
        grad_values = grad_values + jnp.einsum("hqk,qhd->khd", rounded, grad_block, preferred_element_type=F32)
    return (
        jnp.concatenate(grad_queries, axis=0).astype(BF),
        grad_keys.astype(BF),
        grad_values.astype(BF),
    )


def on_device_native(
    comm,
    token_ids,
    segment_ids,
    timesteps,
    token_table,
    time_table,
    ln1_gain,
    ln1_bias,
    w_qkv,
    w_out,
    attn_bias,
    ln2_gain,
    ln2_bias,
    w_up,
    w_down,
    mlp_bias,
    cotangent,
):
    group = lax.axis_size("mp")
    ndp = lax.axis_size("dp")
    member = lax.axis_index("mp")
    own_rows = L // group
    width = token_table.shape[1]
    heads_local = width // HD

    emb = fold(token_table[token_ids])
    time_row = lax.dynamic_slice_in_dim(time_table, timesteps[0], 1, 0)
    trow = jnp.broadcast_to(jnp.pad(time_row, ((0, 0), (0, 256 - width))), (16, 256))
    ids = token_ids.reshape(8, 128)
    w2 = jnp.stack((w_up, w_down))
    wo = w_out.reshape(width, 6, 128).transpose(1, 0, 2).reshape(6 * width, 128)
    E, TR, IDS, W2, WO = comm.gather_all(emb, trow, ids, w2, wo)

    time_full = TR[:, 0, :width].reshape(1, D).astype(F32)
    tokens = unfold(E).transpose(1, 0, 2).reshape(L, D)
    stream_all = tokens.astype(F32) + time_full
    stream_in = lax.dynamic_slice_in_dim(stream_all, member * own_rows, own_rows, 0)
    normed_one = layer_norm(stream_all, ln1_gain, ln1_bias).astype(BF)
    wq = w_qkv.transpose(1, 2, 0).reshape(3 * width, D)
    packed = contract_cols(normed_one, wq).astype(BF).reshape(L, 3, heads_local, HD)
    queries, key_rows, value_rows = packed[:, 0], packed[:, 1], packed[:, 2]
    attended, log_sums = attend_forward(queries, key_rows, value_rows, segment_ids)
    sent = fold(attended.reshape(group, own_rows, width))
    got = comm.exchange(sent, 1, "to_rows")

    att_own = unfold(got).transpose(1, 0, 2).reshape(own_rows, D)
    w_out_full = WO.reshape(group, 6, width, 128).transpose(0, 2, 1, 3).reshape(D, D)
    stream_mid = stream_in + dot(att_own, w_out_full) + attn_bias
    normed_two = layer_norm(stream_mid, ln2_gain, ln2_bias).astype(BF)
    own_segments = lax.dynamic_slice_in_dim(segment_ids, member * own_rows, own_rows, 0)
    grad_out = cotangent.astype(F32) * (own_segments != 0).astype(F32)[:, None]
    grad_mlp = grad_out.astype(BF)
    out = stream_mid + mlp_bias
    grad_norm_two = jnp.zeros((own_rows, D), F32)
    grads_up, grads_down = [], []
    for q in range(group):
        pre = dot(normed_two, W2[q, 0])
        act, back = jax.vjp(lambda v: jax.nn.gelu(v, approximate=True), pre)
        act = act.astype(BF)
        out = out + dot(act, W2[q, 1])
        grad_pre = back(contract_cols(grad_mlp, W2[q, 1]))[0].astype(BF)
        grad_norm_two = grad_norm_two + contract_cols(grad_pre, W2[q, 0])
        grads_up.append(contract_rows(normed_two, grad_pre).astype(BF))
        grads_down.append(contract_rows(grad_mlp, act).astype(BF))
    dw = jnp.stack((jnp.stack(grads_up), jnp.stack(grads_down)))
    norm_back_two = jax.vjp(layer_norm, stream_mid, ln2_gain, ln2_bias)[1]
    grad_mid_norm, grad_ln2_gain, grad_ln2_bias = norm_back_two(grad_norm_two)
    grad_mid = grad_out + grad_mid_norm
    grad_attn = grad_mid.astype(BF)
    dwo = contract_rows(grad_attn, att_own).astype(BF).reshape(D, group, width).transpose(1, 0, 2)
    dwo = jnp.pad(dwo, ((0, 0), (0, 0), (0, 256 - width)))
    grad_attended = contract_cols(grad_attn, w_out_full).astype(BF)
    sent = fold(grad_attended.reshape(own_rows, group, width).transpose(1, 0, 2))
    got = comm.exchange(sent, 2, "to_heads")

    grad_heads = unfold(got).reshape(L, heads_local, HD)
    grad_q, grad_k, grad_v = attend_backward(
        queries, key_rows, value_rows, segment_ids, log_sums, grad_heads
    )
    grad_packed = jnp.stack((grad_q, grad_k, grad_v), axis=1).reshape(L, 3 * width)
    dqkv = jnp.pad(contract_rows(normed_one, grad_packed).astype(BF), ((0, 0), (0, 640 - 3 * width)))
    gn = dot(grad_packed, wq).astype(BF).reshape(group, own_rows, D)

    pieces = lambda a: a.reshape(a.shape[:-2] + (ndp // 2, 2, D // ndp, a.shape[-1]))
    grad_norm_one, g_up, g_down, g_out, g_qkv = comm.reduce_all(
        gn, pieces(dw), pieces(dwo), pieces(dqkv)[None]
    )
    norm_back_one = jax.vjp(layer_norm, stream_in, ln1_gain, ln1_bias)[1]
    grad_in_norm, grad_ln1_gain, grad_ln1_bias = norm_back_one(grad_norm_one)
    input_grad = grad_mid + grad_in_norm
    tp = fold(input_grad.astype(BF).reshape(own_rows, group, width).transpose(1, 0, 2))
    step_row = jnp.where(member == 0, timesteps[0], 0).astype(F32)
    vec = jnp.stack(
        (
            grad_ln1_gain,
            grad_ln1_bias,
            jnp.sum(grad_mid, axis=0),
            grad_ln2_gain,
            grad_ln2_bias,
            jnp.sum(grad_out, axis=0),
            jnp.sum(input_grad, axis=0),
            jnp.broadcast_to(step_row, (D,)),
        )
    )
    X, SP = comm.final_exchange(tp, vec)
    rows_table = token_table.shape[0] // ndp
    columns = unfold(X).reshape(ndp * L, width)
    first = lax.axis_index("dp") * rows_table
    hot = (first + jnp.arange(rows_table))[:, None] == IDS.reshape(1, ndp * L)
    grad_token_table = dot(hot.astype(BF), columns)
    steps = SP[:, 7, 0].astype(jnp.int32)
    grad_time_table = jnp.zeros(time_table.shape[:1] + (D,), F32)
    at_row = jnp.arange(time_table.shape[0])[:, None]
    if ndp <= 8:
        for i in range(ndp):
            grad_time_table = grad_time_table + jnp.where(at_row == steps[i], SP[i, 6][None], 0.0)
    else:
        grad_time_table = grad_time_table.at[steps].add(SP[:, 6])
    sums = jnp.sum(SP[:, :6], axis=0)
    return (
        out.astype(BF),
        input_grad,
        grad_token_table,
        grad_time_table,
        sums[0],
        sums[1],
        g_qkv[:, : 3 * width].reshape(-1, 3, width),
        g_out[:, :width].T,
        sums[2],
        sums[3],
        sums[4],
        g_up,
        g_down.T,
        sums[5],
    )


def on_device_tuned(
    token_ids, segment_ids, timesteps, token_table, time_table, ln1_gain, ln1_bias, w_qkv, w_out, attn_bias,
    ln2_gain, ln2_bias, w_up, w_down, mlp_bias, cotangent,
):
    group, ndp = 4, 8
    member = lax.axis_index("mp")
    own_rows, width = 256, 192
    emb = fold(token_table[token_ids])
    time_row = lax.dynamic_slice_in_dim(time_table, timesteps[0], 1, 0)
    trow = jnp.broadcast_to(jnp.pad(time_row, ((0, 0), (0, 256 - width))), (16, 256))
    ids = token_ids.reshape(8, 128)
    wq = w_qkv.transpose(1, 2, 0).reshape(3 * width, D)
    segc, segr = segment_ids.reshape(L, 1), segment_ids.reshape(1, L)
    par = jnp.stack((ln1_gain, ln1_bias, attn_bias, ln2_gain, ln2_bias, mlp_bias))
    qm, k, v, kt, normed_one, stream_in, lse, att_own, IDS, W2, WO = front(
        emb, trow, ids, segc, segr, par, wq, w_up, w_down, w_out
    )
    segc_own = lax.dynamic_slice_in_dim(segc, member * own_rows, own_rows, 0)
    out, grad_mid, grad_attended, dw, dwo, vec = mid(att_own, stream_in, WO, W2, cotangent, segc_own, par)
    pieces = lambda a: a.reshape(a.shape[:-2] + (ndp // 2, 2, D // ndp, a.shape[-1]))
    input_grad, grad_token_table, g_up, g_down, g_out, g_qkv, SP = back(
        grad_attended, qm, k, v, kt, lse, normed_one, wq, stream_in, grad_mid, segc, segr, par, vec, IDS, timesteps,
        pieces(dw), pieces(dwo),
    )
    steps = SP[:, 7, 0].astype(jnp.int32)
    grad_time_table = jnp.zeros(time_table.shape[:1] + (D,), F32)
    at_row = jnp.arange(time_table.shape[0])[:, None]
    for i in range(ndp):
        grad_time_table = grad_time_table + jnp.where(at_row == steps[i], SP[i, 6][None], 0.0)
    sums = jnp.sum(SP[:, :6], axis=0)
    return (
        out, input_grad, grad_token_table, grad_time_table, sums[0], sums[1],
        g_qkv[:, :, :width].transpose(1, 0, 2), g_out[:, :width].T, sums[2], sums[3], sums[4], g_up, g_down.T,
        sums[5],
    )


def solution(mesh):
    placed = (
        P("dp"),
        P("dp"),
        P("dp"),
        P(None, "mp"),
        P(None, "mp"),
        P(),
        P(),
        P(None, None, "mp"),
        P("mp", None),
        P(),
        P(),
        P(),
        P(None, "mp"),
        P("mp", None),
        P(),
        P(("dp", "mp"), None),
    )
    ndp, nmp = mesh.shape["dp"], mesh.shape["mp"]
    return jax.shard_map(
        on_device_tuned if (ndp, nmp) == (8, 4) else functools.partial(on_device_native, Native(ndp, nmp)),
        mesh=mesh,
        in_specs=placed,
        out_specs=(
            P(("dp", "mp"), None),
            P(("dp", "mp"), None),
            P("dp", "mp"),
            P(),
            P(),
            P(),
            P("dp", None, "mp"),
            P("mp", "dp"),
            P(),
            P(),
            P(),
            P("dp", "mp"),
            P("mp", "dp"),
            P(),
        ),
        check_vma=False,
    )
```

```python
import functools

import jax
import jax.numpy as jnp
from jax import lax
from jax.experimental import pallas as pl
from jax.experimental.pallas import tpu as pltpu
from jax.sharding import PartitionSpec as P

D = 768
HD = 64
L = 1024
QBLK = 512
BF = jnp.bfloat16
F32 = jnp.float32
MESH = pl.DeviceIdType.MESH
ANY = pl.BlockSpec(memory_space=pl.ANY)
VM = pl.BlockSpec(memory_space=pltpu.VMEM)
DMA = pltpu.SemaphoreType.DMA
EPS = 1e-05


def shape(dims, dtype):
    return jax.ShapeDtypeStruct(dims, dtype)


def dot(a, b):
    return jnp.dot(a, b, preferred_element_type=F32)


def contract_rows(left, right):
    return lax.dot_general(left, right, (((0,), (0,)), ((), ())), preferred_element_type=F32)


def contract_cols(left, right):
    return lax.dot_general(left, right, (((1,), (1,)), ((), ())), preferred_element_type=F32)


class Place:
    def __init__(self):
        self.p = p = lax.axis_index("dp")
        self.j = lax.axis_index("mp")
        core, x, y = p % 2, (p // 2) % 2, p // 4
        self.core, self.m = core, p // 2
        self.px = p + 2 - 4 * x
        self.py = p + 4 - 8 * y
        self.pd = self.px + 4 - 8 * y
        self.pc = p + 1 - 2 * core
        self.mx = self.px // 2
        self.my = self.py // 2
        self.md = self.pd // 2

    def z(self, hop):
        return (self.p, (self.j + hop) % 4)

    def at(self, dp):
        return (dp, self.j)


def meet(devices):
    barrier = pltpu.get_barrier_semaphore()
    for device in devices:
        pl.semaphore_signal(barrier, inc=1, device_id=device, device_id_type=MESH)
    pl.semaphore_wait(barrier, len(devices))


def push(src, dst, send, recv, device):
    return pltpu.make_async_remote_copy(
        src_ref=src, dst_ref=dst, send_sem=send, recv_sem=recv, device_id=device, device_id_type=MESH
    )


def params(cid):
    return pltpu.CompilerParams(collective_id=cid, has_side_effects=True, vmem_limit_bytes=60 << 20)


def head_mask(width, h):
    lane = lax.broadcasted_iota(jnp.int32, (1, width), 1)
    return ((lane >= HD * h) & (lane < HD * h + HD)).astype(F32)


def fold(rows):
    half = rows.shape[-2] // 2
    return jnp.concatenate((rows[..., :half, :], rows[..., half:, :]), axis=-1)


def unfold(packed):
    width = packed.shape[-1] // 2
    return jnp.concatenate((packed[..., :width], packed[..., width:]), axis=-2)


CH = 32


def line_of(ref):
    return ref[...].reshape(1, ref.shape[0])


def across(row):
    return jnp.broadcast_to(row, (128, row.shape[1])).T


def allowed(segc, sq, b, c):
    key = CH * c + lax.broadcasted_iota(jnp.int32, (CH, 256), 0)
    query = 256 * b + lax.broadcasted_iota(jnp.int32, (CH, 256), 1)
    return ((segc[CH * c : CH * c + CH, :] == sq) & (sq != 0.0)) | (key == query)


def lanes(b):
    return pl.ds(pl.multiple_of(256 * b, 256), 256)


def groups(x):
    return x.reshape(CH // 8, 8, 256)


def write_segments(seg, segr, segc):
    row = line_of(seg).astype(F32)
    segr[...] = row
    for i in range(8):
        segc[128 * i : 128 * i + 128, :] = across(row[:, 128 * i : 128 * i + 128])[:, 0:1]


class Weights:
    def __init__(self, me, shards, W2, WO, zs, zr, ps, pr):
        self.me, self.shards, self.W2, self.WO = me, shards, W2, WO
        self.zs, self.zr, self.ps, self.pr = zs, zr, ps, pr

    def zpart(self, a, q, piece, ref=None):
        if a < 2:
            rows = pl.ds(96 * piece, 96)
            return self.W2.at[q, a, rows, :] if ref is None else ref.at[rows, :]
        base = 192 * q if ref is None else 0
        return (self.WO if ref is None else ref).at[
            pl.ds(base + 48 * (piece // 2), 48), pl.ds(384 * (piece % 2), 384)
        ]

    def part(self, a, q, piece, half=None):
        if a == 0:
            lo, n = (0, 96) if half is None else (48 * half, 48)
            return self.W2.at[q, :, pl.ds(96 * piece + lo, n), :]
        lo, n = (0, 48) if half is None else ((0, 32), (32, 16))[half]
        return self.WO.at[pl.ds(192 * q + 48 * (piece // 2) + lo, n), pl.ds(384 * (piece % 2), 384)]

    def quarter(self, d, k):
        j = self.me.j
        return (j - k + 4) % 4 if d == 0 else (j + k) % 4

    def sends(self, d, k):
        j = self.me.j
        return (j < 3) & (j >= k) if d == 0 else (j > 0) & (j + k <= 3)

    def gets(self, d, k):
        j = self.me.j
        return j >= k + 1 if d == 0 else j + k + 1 <= 3

    def zcopy(self, d, k, a):
        p, q = self.me.p, self.quarter(d, k)
        src = self.zpart(a, q, p, self.shards[a]) if k == 0 else self.zpart(a, q, p)
        return push(src, self.zpart(a, q, p), self.zs.at[d, k, a], self.zr.at[d, k, a], self.me.z(1 if d == 0 else 3))

    def zgot(self, d, k, a):
        dst = self.zpart(a, self.quarter(d, k + 1), self.me.p)
        return push(dst, dst, self.zs.at[d, k, a], self.zr.at[d, k, a], self.me.z(1))

    def zstart(self, k, arrays):
        for d in (0, 1):

            @pl.when(self.sends(d, k))
            def _():
                for a in arrays:
                    self.zcopy(d, k, a).start()

    def zwait(self, k, arrays):
        for d in (0, 1):

            @pl.when(self.gets(d, k))
            def _():
                for a in arrays:
                    self.zgot(d, k, a).wait_recv()

    def routes(self, d, k, a, stage):
        me, q = self.me, self.quarter(d, k + 1)
        if stage == 0:
            return [(self.part(a, q, me.p), me.px), (self.part(a, q, me.p), me.py), (self.part(a, q, me.p), me.pc)]
        if stage == 1:
            return [
                (self.part(a, q, me.py, 0), me.px),
                (self.part(a, q, me.px, 1), me.py),
                (self.part(a, q, me.px), me.pc),
                (self.part(a, q, me.py), me.pc),
            ]
        return [(self.part(a, q, me.pd), me.pc)]

    def arrivals(self, d, k, a, stage):
        me, q = self.me, self.quarter(d, k + 1)
        c = me.pc - me.p
        if stage == 0:
            return [self.part(a, q, me.px), self.part(a, q, me.py), self.part(a, q, me.pc)]
        if stage == 1:
            return [
                self.part(a, q, me.pd, 0),
                self.part(a, q, me.pd, 1),
                self.part(a, q, me.px + c),
                self.part(a, q, me.py + c),
            ]
        return [self.part(a, q, me.pd + c)]

    def pstart(self, k, stage):
        for d in (0, 1):

            @pl.when(self.gets(d, k))
            def _():
                for a in (0, 1):
                    for i, (ref, dp) in enumerate(self.routes(d, k, a, stage)):
                        s = 3 * stage + i if stage < 2 else 7
                        push(ref, ref, self.ps.at[d, k, a, s], self.pr.at[d, k, a, s], self.me.at(dp)).start()

    def pwait(self, k, stage, which, send=False):
        for d in (0, 1):

            @pl.when(self.gets(d, k))
            def _():
                for a in (0, 1):
                    if send:
                        refs = [r for r, _ in self.routes(d, k, a, stage)]
                    else:
                        refs = self.arrivals(d, k, a, stage)
                    for i in which:
                        s = 3 * stage + i if stage < 2 else 7
                        c = push(refs[i], refs[i], self.ps.at[d, k, a, s], self.pr.at[d, k, a, s], self.me.at(self.me.pc))
                        c.wait_send() if send else c.wait_recv()

    def finish(self):
        for k in range(3):
            self.pwait(k, 0, (2,))
            self.pwait(k, 1, (2, 3))
            self.pwait(k, 2, (0,))
            self.pwait(k, 0, (0, 1, 2), send=True)
            self.pwait(k, 1, (0, 1, 2, 3), send=True)
            self.pwait(k, 2, (0,), send=True)
            for d in (0, 1):

                @pl.when(self.sends(d, k))
                def _():
                    for a in (0, 1, 2):
                        self.zcopy(d, k, a).wait_send()


def front_kernel(
    ids, seg, step, ids8, tabt, timet, g1, b1, wq, w_up, w_down, w_out,
    qm_o, k_o, v_o, kt_o, n1_o, x_o, lse_o, att_o, segr, segc, IDS, W2, WO,
    tab, hot, eb, E, tb, TR, vt, s, pb, ot, sendb, attg, own2, own_o,
    es, er, ts, tr, is_, ir, zs, zr, ps, pr, as_, ar, ls,
):
    me = Place()
    p, j = me.p, me.j
    fetch = pltpu.make_async_copy(tabt, tab, ls.at[0])
    fetch.start()
    load = [
        pltpu.make_async_copy(w_up, own2.at[0], ls.at[3]),
        pltpu.make_async_copy(w_down, own2.at[1], ls.at[4]),
        pltpu.make_async_copy(w_out, own_o, ls.at[5]),
    ]
    for c in load:
        c.start()
    write_segments(seg, segr, segc)
    lane = lax.broadcasted_iota(jnp.int32, (192, 1000), 1)
    column = jnp.sum(jnp.where(lane == step[0], timet[...].astype(F32), 0.0), axis=1, keepdims=True)
    tb[:, 0:192] = jnp.broadcast_to(column, (192, 128)).T[0:16, :].astype(BF)
    meet([me.z(1), me.z(2), me.z(3)] + [me.at((p + k) % 8) for k in range(1, 8)])
    w = Weights(me, (own2.at[0], own2.at[1], own_o), W2, WO, zs, zr, ps, pr)

    def ecopy(d, k, c):
        q = w.quarter(d, k)
        dev = me.z(1 if d == 0 else 3)
        return push(eb.at[c] if k == 0 else E.at[q, c], E.at[q, c], es.at[d, k, c], er.at[d, k, c], dev)

    def estart(k, c):
        for d in (0, 1):

            @pl.when(w.sends(d, k))
            def _():
                ecopy(d, k, c).start()

    def ewait(k, c):
        for d in (0, 1):

            @pl.when(w.gets(d, k))
            def _():
                dst = E.at[w.quarter(d, k + 1), c]
                push(dst, dst, es.at[d, k, c], er.at[d, k, c], me.z(1)).wait_recv()

    here = [pltpu.make_async_copy(ids8, IDS.at[p], ls.at[2])]
    keep = [
        pltpu.make_async_copy(own2, W2.at[j], ls.at[3]),
        pltpu.make_async_copy(own_o, WO.at[pl.ds(192 * j, 192), :], ls.at[5]),
    ]
    small = [push(tb, TR.at[j], ts.at[k - 1], tr.at[k - 1], me.z(k)) for k in (1, 2, 3)]
    small_ids = [push(ids8, IDS.at[p], is_.at[k - 1], ir.at[k - 1], me.at((p + k) % 8)) for k in range(1, 8)]
    ids_row = line_of(ids).astype(F32)

    def embed(c):
        token = across(ids_row[:, 256 * c : 256 * c + 256])
        s[0, 0:256, 0:192] = jnp.zeros((256, 192), F32)

        @pl.loop(0, 4)
        def _(v):
            base = (2048 * v).astype(F32)
            for i in range(16):
                word = lax.broadcasted_iota(jnp.int32, (256, 128), 1).astype(F32) + (base + 128.0 * i)
                hot[:, 128 * i : 128 * i + 128] = (token == word).astype(F32).astype(BF)
            s[0, 0:256, 0:192] += contract_cols(hot[...], tab[:, pl.ds(pl.multiple_of(2048 * v, 2048), 2048)])

        eb[c] = fold(s[0, 0:256, 0:192].astype(BF))
        estart(0, c)

    fetch.wait()
    for c in load:
        c.wait()
    w.zstart(0, (0,))
    embed(0)
    for c in small + here + small_ids + keep:
        c.start()
    embed(1)
    embed(2)
    ewait(0, 0)
    estart(1, 0)
    embed(3)
    w.zstart(0, (1,))
    ewait(0, 1)
    estart(1, 1)
    ewait(0, 2)
    estart(1, 2)
    ewait(1, 0)
    estart(2, 0)
    ewait(0, 3)
    estart(1, 3)
    ewait(1, 1)
    estart(2, 1)
    w.zwait(0, (0,))
    w.zstart(0, (2,))
    ewait(1, 2)
    estart(2, 2)
    w.zstart(1, (0,))
    for c in small:
        c.wait()
    E[j] = eb[...]
    TR[j] = tb[...]
    time_row = jnp.concatenate([TR[q].astype(F32)[0:1, 0:192] for q in range(4)], axis=1)
    gain, shift = line_of(g1), line_of(b1)

    def norm_qkv(r):
        rows = slice(256 * r, 256 * r + 256)
        x = jnp.concatenate([unfold(E[q, r]) for q in range(4)], axis=1)
        x = x.astype(F32) + time_row
        centered = x - jnp.mean(x, axis=1, keepdims=True)
        variance = jnp.mean(centered * centered, axis=1, keepdims=True)
        normed = (centered * lax.rsqrt(variance + EPS) * gain + shift).astype(BF)
        n1_o[rows, :] = normed

        @pl.when(j == r)
        def _():
            x_o[...] = x

        q = contract_cols(normed, wq[0:192, :]).astype(BF).astype(F32) * 0.125
        for i in range(3):
            qm_o[i, rows, :] = (q * head_mask(192, i)).astype(BF)
        k_o[rows, :] = contract_cols(normed, wq[192:384, :]).astype(BF)
        v_o[rows, :] = contract_cols(normed, wq[384:576, :]).astype(BF)
        kt_o[:, rows] = contract_cols(wq[192:384, :], normed).astype(BF)
        vt[:, rows] = contract_cols(wq[384:576, :], normed).astype(BF)

    ewait(2, 0)
    norm_qkv(0)
    ewait(1, 3)
    estart(2, 3)
    w.zwait(0, (1, 2))
    w.zstart(1, (1, 2))
    w.pstart(0, 0)
    ewait(2, 1)
    norm_qkv(1)
    ewait(2, 2)
    norm_qkv(2)
    ewait(2, 3)
    norm_qkv(3)

    def att_copy(b):
        return push(sendb.at[b], attg.at[j], as_.at[b], ar.at[j], (p, b))

    def step0():
        w.zwait(1, (0,))
        w.zstart(2, (0,))

    def step1():
        w.pwait(0, 0, (0, 1))
        w.pstart(0, 1)

    def step2():
        w.zwait(1, (1, 2))
        w.zstart(2, (1, 2))
        w.pstart(1, 0)

    def step3():
        w.pwait(0, 1, (0, 1))
        w.pstart(0, 2)

    def step4():
        w.pwait(1, 0, (0, 1))
        w.pstart(1, 1)

    def step5():
        w.zwait(2, (0, 1, 2))
        w.pstart(2, 0)

    steps = {0: step0, 2: step1, 4: step2, 6: step3, 10: step4, 11: step5}

    def slot(i, n):
        for k, step in {k: v for k, v in steps.items() if k % 3 == n}.items():
            pl.when(i == k // 3)(step)

    @pl.loop(0, 4)
    def _(i):
        b = (j + 1 + i) % 4
        sq = segr[0:1, lanes(b)]
        for h in range(3):
            s[h] = contract_cols(k_o[...], qm_o[h, lanes(b), :])
        slot(i, 0)
        top = [jnp.full((8, 256), -jnp.inf, F32)] * 3
        for c in range(L // CH):
            rows = slice(CH * c, CH * c + CH)
            ok = allowed(segc, sq, b, c)
            for h in range(3):
                x = jnp.where(ok, s[h, rows, :], -1e30)
                s[h, rows, :] = x
                top[h] = jnp.maximum(top[h], jnp.max(groups(x), axis=0))
        top = [jnp.max(m, axis=0, keepdims=True) for m in top]
        slot(i, 1)
        total = [jnp.zeros((8, 256), F32)] * 3
        for c in range(L // CH):
            rows = slice(CH * c, CH * c + CH)
            for h in range(3):
                e = jnp.exp(s[h, rows, :] - top[h])
                pb[h, rows, :] = e.astype(BF)
                total[h] = total[h] + jnp.sum(groups(e), axis=0)
        for h in range(3):
            t = jnp.sum(total[h], axis=0, keepdims=True)
            lse_o[3 * b + h] = top[h] + jnp.log(t)
            part = slice(64 * h, 64 * h + 64)
            ot[part, :] = dot(vt[part, :], pb[h]) * (1.0 / t)
        sendb[b] = fold(ot[...].T.astype(BF))

        @pl.when(b != j)
        def _():
            att_copy(b).start()

        slot(i, 2)

    attg[j] = sendb[j]
    w.pwait(1, 1, (0, 1))
    w.pstart(1, 2)
    for q in range(4):

        @pl.when(j != q)
        def _():
            push(attg.at[q], attg.at[q], as_.at[q], ar.at[q], me.z(1)).wait_recv()

    att_o[...] = jnp.concatenate([unfold(attg[q]) for q in range(4)], axis=1)
    w.pwait(2, 0, (0, 1))
    w.pstart(2, 1)
    w.pwait(2, 1, (0, 1))
    w.pstart(2, 2)
    for b in range(4):

        @pl.when(j != b)
        def _():
            att_copy(b).wait_send()

    for k in range(3):
        for d in (0, 1):

            @pl.when(w.sends(d, k))
            def _():
                for c in range(4):
                    ecopy(d, k, c).wait_send()

    w.finish()
    for c in small_ids + here + keep:
        c.wait()


def front(ids, seg, step, ids8, tabt, timet, g1, b1, wq, w_up, w_down, w_out):
    return pl.pallas_call(
        front_kernel,
        out_shape=(
            shape((3, L, 192), BF),
            shape((L, 192), BF),
            shape((L, 192), BF),
            shape((192, L), BF),
            shape((L, D), BF),
            shape((256, D), F32),
            shape((12, 1, 256), F32),
            shape((256, D), BF),
            shape((1, L), F32),
            shape((L, 1), F32),
            shape((8, 8, 128), jnp.int32),
            shape((4, 2, D, D), BF),
            shape((D, D), BF),
        ),
        in_specs=[VM] * 2 + [pl.BlockSpec(memory_space=pltpu.SMEM)] + [ANY] * 2 + [VM] * 4 + [ANY] * 3,
        out_specs=(VM,) * 10 + (ANY,) * 3,
        scratch_shapes=[
            pltpu.VMEM((192, 8192), BF),
            pltpu.VMEM((256, 2048), BF),
            pltpu.VMEM((4, 128, 384), BF),
            pltpu.VMEM((4, 4, 128, 384), BF),
            pltpu.VMEM((16, 256), BF),
            pltpu.VMEM((4, 16, 256), BF),
            pltpu.VMEM((192, L), BF),
            pltpu.VMEM((3, L, 256), F32),
            pltpu.VMEM((3, L, 256), BF),
            pltpu.VMEM((192, 256), F32),
            pltpu.VMEM((4, 128, 384), BF),
            pltpu.VMEM((4, 128, 384), BF),
            pltpu.VMEM((2, D, D), BF),
            pltpu.VMEM((192, D), BF),
            DMA((2, 3, 4)),
            DMA((2, 3, 4)),
            DMA((3,)),
            DMA((3,)),
            DMA((7,)),
            DMA((7,)),
            DMA((2, 3, 3)),
            DMA((2, 3, 3)),
            DMA((2, 3, 2, 8)),
            DMA((2, 3, 2, 8)),
            DMA((4,)),
            DMA((4,)),
            DMA((6,)),
        ],
        compiler_params=params(0),
        name="front",
    )(ids, seg, step, ids8, tabt, timet, g1, b1, wq, w_up, w_down, w_out)


def norm_stats(x):
    centered = x - jnp.mean(x, axis=1, keepdims=True)
    scale = lax.rsqrt(jnp.mean(centered * centered, axis=1, keepdims=True) + EPS)
    return centered * scale, scale


def norm_back(grad, gain, hat, scale):
    t = grad * gain
    return scale * (t - jnp.mean(t, axis=1, keepdims=True) - hat * jnp.mean(t * hat, axis=1, keepdims=True))


def rows_sum(x):
    return jnp.sum(x, axis=0, keepdims=True)


def mid_kernel(
    att, x, wo, w2, cot, segr, pa, pg, pb, pm,
    out_o, gmid_o, gatt_o, dw_o, dwo_o, vec_o,
    sm, hat, sc, n2, n2t, gmt, gm, acc, gn2,
):
    q = pl.program_id(0)
    own = pl.ds(pl.multiple_of(256 * lax.axis_index("mp"), 256), 256)

    def masked():
        valid = across((segr[:, own] != 0.0).astype(F32))[:, 0:1]
        return cot[...].astype(F32) * valid


    @pl.when(q == 0)
    def _():
        mid = x[...] + dot(att[...], wo[...]) + line_of(pa)
        sm[...] = mid
        h, scale = norm_stats(mid)
        hat[...] = h
        sc[...] = scale
        normed = (h * line_of(pg) + line_of(pb)).astype(BF)
        n2[...] = normed
        n2t[...] = normed.astype(F32).T.astype(BF)
        grad = masked()
        gm[...] = grad.astype(BF)
        gmt[...] = grad.T.astype(BF)
        acc[...] = mid + line_of(pm)
        gn2[...] = jnp.zeros_like(gn2)

    up, down = w2[0, 0], w2[0, 1]
    pre = dot(n2[...], up)
    c = 0.7978845608028654
    cubic = c * (pre + 0.044715 * pre * pre * pre)
    t = jnp.tanh(cubic)
    act = (0.5 * pre * (1.0 + t)).astype(BF)
    slope = 0.5 * (1.0 + t) + 0.5 * pre * (1.0 - t * t) * (c * (1.0 + 3 * 0.044715 * pre * pre))
    acc[...] += dot(act, down)
    grad_pre = (contract_cols(gm[...], down) * slope).astype(BF)
    gn2[...] += contract_cols(grad_pre, up)
    dw_o[0, 0] = dot(n2t[...], grad_pre).astype(BF)
    dw_o[1, 0] = dot(gmt[...], act).astype(BF)

    @pl.when(q == 3)
    def _():
        out_o[...] = acc[...].astype(BF)
        grad = masked()
        gn, h = gn2[...], hat[...]
        gmid = grad + norm_back(gn, line_of(pg), h, sc[...])
        gmid_o[...] = gmid
        vec_o[...] = jnp.zeros_like(vec_o)
        vec_o[2:3, :] = rows_sum(gmid)
        vec_o[3:4, :] = rows_sum(gn * h)
        vec_o[4:5, :] = rows_sum(gn)
        vec_o[5:6, :] = rows_sum(grad)
        ga = gmid.astype(BF)
        gatt_o[...] = contract_cols(ga, wo[...]).astype(BF)
        full = dot(gmid.T.astype(BF), att[...]).astype(BF)
        for i in range(4):
            dwo_o[i, :, 0:192] = full[:, 192 * i : 192 * i + 192]
            dwo_o[i, :, 192:256] = jnp.zeros((D, 64), BF)


def mid(att, x, wo, w2, cot, segr, pa, pg, pb, pm):
    whole = lambda a: pl.BlockSpec(a.shape, lambda q: (0,) * a.ndim)
    keep = lambda *dims: pl.BlockSpec(dims, lambda q: (0,) * len(dims))
    return pl.pallas_call(
        mid_kernel,
        grid=(4,),
        out_shape=(
            shape((256, D), BF),
            shape((256, D), F32),
            shape((256, D), BF),
            shape((2, 4, D, D), BF),
            shape((4, D, 256), BF),
            shape((8, D), F32),
        ),
        in_specs=[
            whole(att),
            whole(x),
            whole(wo),
            pl.BlockSpec((1, 2, D, D), lambda q: (q, 0, 0, 0)),
            whole(cot),
            whole(segr),
            whole(pa),
            whole(pg),
            whole(pb),
            whole(pm),
        ],
        out_specs=(
            keep(256, D),
            keep(256, D),
            keep(256, D),
            pl.BlockSpec((2, 1, D, D), lambda q: (0, q, 0, 0)),
            keep(4, D, 256),
            keep(8, D),
        ),
        scratch_shapes=[
            pltpu.VMEM((256, D), F32),
            pltpu.VMEM((256, D), F32),
            pltpu.VMEM((256, 1), F32),
            pltpu.VMEM((256, D), BF),
            pltpu.VMEM((D, 256), BF),
            pltpu.VMEM((D, 256), BF),
            pltpu.VMEM((256, D), BF),
            pltpu.VMEM((256, D), F32),
            pltpu.VMEM((256, D), F32),
        ],
        compiler_params=pltpu.CompilerParams(vmem_limit_bytes=60 << 20, dimension_semantics=("arbitrary",)),
        name="mid",
    )(att, x, wo, w2, cot, segr, pa, pg, pb, pm)


class Line:
    def __init__(self, me, acc, up, down, sems):
        self.me, self.acc, self.up, self.down = me, acc, up, down
        self.us, self.ur, self.ds, self.dr = (sems.at[i] for i in range(4))

    def send(self, q, d):
        if d == 0:
            return push(self.acc(q), self.up.at[q], self.us.at[q], self.ur.at[q], self.me.z(1))
        return push(self.acc(q), self.down.at[q], self.ds.at[q], self.dr.at[q], self.me.z(3))

    def end(self, q, d):
        @pl.when(self.me.j == (0 if d == 0 else 3))
        def _():
            self.send(q, d).start()

    def first(self):
        for q in (3, 2, 1):
            self.end(q, 0)
        for q in (0, 1, 2):
            self.end(q, 1)

    def inner(self, steps):
        for q, d, j in steps:

            @pl.when(self.me.j == j)
            def _():
                c = self.send(q, d)
                c.wait_recv()
                ref = self.acc(q)
                ref[...] = ref[...] + (self.up if d == 0 else self.down)[q]
                c.start()

    def finish(self, out):
        j = self.me.j
        for q in range(4):

            @pl.when(j == q)
            def _():
                total = self.acc(q)[...].astype(F32)
                if q > 0:
                    self.send(q, 0).wait_recv()
                    total = total + self.up[q].astype(F32)
                if q < 3:
                    self.send(q, 1).wait_recv()
                    total = total + self.down[q].astype(F32)
                out[...] = total

    def close(self):
        j = self.me.j
        for q in range(4):

            @pl.when(j < q)
            def _():
                self.send(q, 0).wait_send()

            @pl.when(j > q)
            def _():
                self.send(q, 1).wait_send()


NEAR = ((3, 0, 1), (0, 1, 2))
FAR = ((3, 0, 2), (0, 1, 1), (2, 0, 1), (1, 1, 2))


class Unit:
    def __init__(self, me, src, acc, rc, rx, ry, rx2, ry2, sems, lsem):
        self.me, self.src, self.acc = me, src, acc
        self.rc, self.rx, self.ry, self.rx2, self.ry2 = rc, rx, ry, rx2, ry2
        self.s, self.r, self.lsem = sems.at[0], sems.at[1], lsem
        self.nq = acc.shape[0]

    def copies(self, stage):
        me, acc, s, r = self.me, self.acc, self.s, self.r
        lo, hi = pl.ds(0, 48), pl.ds(48, 48)
        if stage == 0:
            return [push(self.src.at[:, :, 1 - me.core], self.rc, s.at[0], r.at[0], me.at(me.pc))]
        if stage == 1:
            return [
                push(acc.at[:, me.md, lo], self.rx.at[:, 1], s.at[1], r.at[1], me.at(me.px)),
                push(acc.at[:, me.md, hi], self.ry.at[:, 1], s.at[2], r.at[2], me.at(me.py)),
                push(acc.at[:, me.mx, lo], self.rx.at[:, 0], s.at[3], r.at[3], me.at(me.px)),
                push(acc.at[:, me.my, hi], self.ry.at[:, 0], s.at[4], r.at[4], me.at(me.py)),
            ]
        return [
            push(acc.at[:, me.my, lo], self.ry2, s.at[5], r.at[5], me.at(me.py)),
            push(acc.at[:, me.mx, hi], self.rx2, s.at[6], r.at[6], me.at(me.px)),
        ]

    def load(self):
        return pltpu.make_async_copy(self.src.at[:, :, self.me.core], self.acc, self.lsem)

    def begin(self):
        self.copies(0)[0].start()
        self.load().start()

    def chip(self):
        self.load().wait()
        self.copies(0)[0].wait_recv()

        @pl.loop(0, self.nq)
        def _(q):
            for m in range(4):
                self.acc[q, m] = self.acc[q, m] + self.rc[q, m]

    def cross(self):
        for c in self.copies(1):
            c.start()

    def turn(self):
        me = self.me
        first = self.copies(1)
        for c in first[:2]:
            c.wait()
        second = self.copies(2)

        @pl.loop(0, self.nq)
        def _(q):
            self.acc[q, me.my, 0:48] = self.acc[q, me.my, 0:48] + self.rx[q, 1]
            self.acc[q, me.mx, 48:96] = self.acc[q, me.mx, 48:96] + self.ry[q, 1]

        for c in second:
            c.start()
        for c in first[2:]:
            c.wait()

        @pl.loop(0, self.nq)
        def _(q):
            self.acc[q, me.m, 0:48] = self.acc[q, me.m, 0:48] + self.rx[q, 0]
            self.acc[q, me.m, 48:96] = self.acc[q, me.m, 48:96] + self.ry[q, 0]

    def settle(self):
        me = self.me
        for c in self.copies(2):
            c.wait()

        @pl.loop(0, self.nq)
        def _(q):
            self.acc[q, me.m, 0:48] = self.acc[q, me.m, 0:48] + self.ry2[q]
            self.acc[q, me.m, 48:96] = self.acc[q, me.m, 48:96] + self.rx2[q]

        self.copies(0)[0].wait_send()

    def own(self, q):
        return self.acc.at[q, self.me.m]


SHAPES = ((4, 768), (4, 768), (4, 256), (3, 256))


def back_kernel(
    gatt, qm, k, v, kt, lse, n1, wq, x, gmid, segc, segr, g1, vec, IDS, step, dw, dwo,
    h_in, h_tok, h_up, h_down, h_out, h_qkv, h_sp,
    *scratch,
):
    me = Place()
    p, j = me.p, me.j
    meet([me.z(1), me.z(2), me.z(3)] + [me.at((p + i) % 8) for i in range(1, 8)])
    it = iter(scratch)
    take = lambda n: [next(it) for _ in range(n)]
    sendb, gbuf, dom, s, dp, pb, dsb, dqt, dqn, dk, dv, gn = take(12)
    o_in, o_tok, o_up, o_down, o_out, o_qkv, o_sp, hs = take(8)
    as_, ar = take(2)
    gacc, gup, gdown, gsem = take(4)
    qk, tb, X, hot, vbuf, SZ, vs = take(7)
    vzs, vzr, ts, tr, ps, pr, vps, vpr, ls = take(9)
    sources = (dw.at[1], dw.at[0], dwo, qk)
    units, lines = [], []
    for i, src in enumerate(sources):
        acc, rc, rx, ry, rx2, ry2, sems, lsem = take(8)
        unit = Unit(me, src, acc, rc, rx, ry, rx2, ry2, sems, lsem)
        units.append(unit)
        if i < 3:
            up, down, sem = take(3)
            lines.append(Line(me, unit.own, up, down, sem))
    own = Line(me, lambda q: gacc.at[q], gup, gdown, gsem)

    homes = [
        pltpu.make_async_copy(src, dst, hs.at[i])
        for i, (src, dst) in enumerate(
            ((o_in, h_in), (o_tok, h_tok), (o_up, h_up), (o_down, h_down), (o_out, h_out), (o_qkv, h_qkv), (o_sp, h_sp))
        )
    ]

    def to_heads(d):
        return push(sendb.at[d], gbuf.at[j], as_.at[d], ar.at[j], (p, d))

    for d in range(4):
        sendb[d] = fold(gatt[:, 192 * d : 192 * d + 192])

        @pl.when(j != d)
        def _():
            to_heads(d).start()

    gbuf[j] = sendb[j]
    for u in units[:3]:
        u.begin()
    dk[...] = jnp.zeros_like(dk)
    dv[...] = jnp.zeros_like(dv)

    def step0():
        units[0].chip()
        units[0].cross()

    def step1():
        units[2].chip()
        units[2].cross()

    def step2():
        units[1].chip()

    steps = {0: step0, 2: step1, 4: step2}

    def slot(i, n):
        for c, fn in {c: fn for c, fn in steps.items() if c % 3 == n}.items():
            pl.when(i == c // 3)(fn)

    @pl.loop(0, 4)
    def _(i):
        b = (j + i) % 4
        sq = segr[0:1, lanes(b)]

        @pl.when(i > 0)
        def _():
            push(gbuf.at[b], gbuf.at[b], as_.at[b], ar.at[b], me.z(1)).wait_recv()

        do = unfold(gbuf[b]).astype(F32)
        for h in range(3):
            dom[h] = (do * head_mask(192, h)).astype(BF)
            s[h] = contract_cols(k[...], qm[h, lanes(b), :])
            dp[h] = contract_cols(v[...], dom[h])
        slot(i, 0)
        ls_ = [lse[3 * b + h] for h in range(3)]
        inner = [jnp.zeros((8, 256), F32)] * 3
        for c in range(L // CH):
            rows = slice(CH * c, CH * c + CH)
            ok = allowed(segc, sq, b, c)
            for h in range(3):
                e = jnp.exp(jnp.where(ok, s[h, rows, :], -1e30) - ls_[h])
                s[h, rows, :] = e
                pb[rows, 256 * h : 256 * h + 256] = e.astype(BF)
                inner[h] = inner[h] + jnp.sum(groups(e * dp[h, rows, :]), axis=0)
        inner = [jnp.sum(a, axis=0, keepdims=True) for a in inner]
        slot(i, 1)
        for c in range(L // CH):
            rows = slice(CH * c, CH * c + CH)
            for h in range(3):
                grad = s[h, rows, :] * (dp[h, rows, :] - inner[h])
                dsb[rows, 256 * h : 256 * h + 256] = grad.astype(BF)
        dv[...] += dot(pb[...], dom[...].reshape(768, 192))
        dk[...] += dot(dsb[...], qm[:, lanes(b), :].reshape(768, 192))
        for h in range(3):
            part = slice(64 * h, 64 * h + 64)
            dqt[part, lanes(b)] = dot(kt[part, :], dsb[:, 256 * h : 256 * h + 256]) * 0.125
        slot(i, 2)

    for q, starts in ((3, ((3, 0),)), (0, ((0, 1),)), (2, ((2, 0),)), (1, ((1, 1), (1, 0), (2, 1)))):
        rows = slice(256 * q, 256 * q + 256)
        dq = dqt[:, rows].T.astype(BF)
        dqn[rows, :] = dq
        total = dot(dq, wq[0:192, :]) + dot(dk[rows, :].astype(BF), wq[192:384, :])
        gacc[q] = (total + dot(dv[rows, :].astype(BF), wq[384:576, :])).astype(BF)
        for block, d in starts:
            own.end(block, d)
    units[0].turn()
    units[2].turn()
    units[1].cross()
    for i, grad in enumerate((dqn[...], dk[...].astype(BF), dv[...].astype(BF))):
        full = contract_rows(n1[...], grad).astype(BF)
        for piece in range(8):
            qk[i, piece // 2, piece % 2, :, 0:192] = full[96 * piece : 96 * piece + 96, :]
            qk[i, piece // 2, piece % 2, :, 192:256] = jnp.zeros((96, 64), BF)
    units[3].begin()
    own.inner(NEAR)
    units[3].chip()
    units[3].cross()
    units[0].settle()
    lines[0].first()
    own.inner(FAR)
    units[2].settle()
    units[1].turn()
    units[3].turn()
    own.finish(gn)

    hat, scale = norm_stats(x[...])
    grad = gn[...]
    dx = gmid[...] + norm_back(grad, line_of(g1), hat, scale)
    o_in[...] = dx
    homes[0].start()
    dxb = dx.astype(BF)

    def to_columns(d):
        return push(tb.at[d], X.at[p, j], ts.at[d], tr.at[j], (p, d))

    for d in range(4):
        tb[d] = fold(dxb[:, 192 * d : 192 * d + 192])

        @pl.when(j != d)
        def _():
            to_columns(d).start()

    X[p, j] = tb[j]
    vbuf[...] = vec[...]
    vbuf[0:1, :] = rows_sum(grad * hat)
    vbuf[1:2, :] = rows_sum(grad)
    vbuf[6:7, :] = rows_sum(dx)
    first = jnp.where(j == 0, step[0], 0).astype(F32)
    vbuf[7:8, :] = jnp.full((1, D), 1.0, F32) * first
    small = [push(vbuf, SZ.at[j], vzs.at[i - 1], vzr.at[i - 1], me.z(i)) for i in (1, 2, 3)]
    for c in small:
        c.start()
    SZ[j] = vbuf[...]

    def hop(ref, i, dev):
        return push(ref, ref, ps.at[i], pr.at[i], me.at(dev))

    def table(d, start=False):
        vocab = 1024 * p + lax.broadcasted_iota(jnp.int32, (1024, 128), 0)
        for g in range(8):
            hot[:, 128 * g : 128 * g + 128] = (vocab == IDS[d, g : g + 1, :]).astype(F32).astype(BF)
        rows = jnp.concatenate([unfold(X[d, q]) for q in range(4)], axis=0)
        part = dot(hot[...], rows)
        if start:
            o_tok[...] = part
        else:
            o_tok[...] += part

    sent = []
    here = me.pc - p

    def spread(i):
        q = (j + i) % 4
        if i > 0:
            push(X.at[p, q], X.at[p, q], ts.at[q], tr.at[q], me.z(1)).wait_recv()
        for c in (hop(X.at[p, q], 2 * q, me.px), hop(X.at[p, q], 2 * q + 1, me.py)):
            c.start()
            sent.append(c)

    def on_x(q):
        return hop(X.at[me.py, q], 8 + q, me.px)

    def on_y(q):
        return hop(X.at[me.px, q], 8 + q, me.py)

    def corner(i):
        q = (j + i) % 4
        hop(X.at[me.px, q], 2 * q, me.px).wait_recv()
        hop(X.at[me.py, q], 2 * q + 1, me.py).wait_recv()

        @pl.when(q < 2)
        def _():
            on_x(q).start()

        @pl.when(q >= 2)
        def _():
            on_y(q).start()

    def to_core(d, i):
        c = hop(X.at[d], i, me.pc)
        c.start()
        sent.append(c)

    spread(0)
    lines[0].inner(NEAR)
    units[1].settle()
    lines[1].first()
    spread(1)
    spread(3)
    lines[2].first()
    corner(0)
    for c in small:
        c.wait()
    vs[...] = SZ[0] + SZ[1] + SZ[2] + SZ[3]
    out_v = [push(vs, o_sp.at[p], vps.at[i - 1], vpr.at[i - 1], me.at((p + i) % 8)) for i in range(1, 8)]
    for c in out_v:
        c.start()
    o_sp[p] = vs[...]
    lines[0].inner(FAR)
    spread(2)
    to_core(p, 12)
    corner(1)
    corner(3)
    table(p, start=True)
    lines[1].inner(NEAR)
    corner(2)
    to_core(me.px, 13)
    to_core(me.py, 14)
    units[3].settle()
    lines[2].inner(NEAR)
    hop(X.at[me.pc], 12, me.pc).wait_recv()
    table(me.pc)
    lines[1].inner(FAR)
    table(me.px)
    for q in range(4):
        hop(X.at[me.pd, q], 8 + q, me.px).wait_recv()
    to_core(me.pd, 15)
    lines[2].inner(FAR)
    table(me.py)
    table(me.pd)
    hop(X.at[me.px + here], 13, me.pc).wait_recv()
    table(me.px + here)
    hop(X.at[me.py + here], 14, me.pc).wait_recv()
    table(me.py + here)
    hop(X.at[me.pd + here], 15, me.pc).wait_recv()
    table(me.pd + here)
    homes[1].start()
    lines[0].finish(o_down)
    homes[3].start()
    lines[2].finish(o_out)
    homes[4].start()
    lines[1].finish(o_up)
    homes[2].start()
    for i in range(3):
        o_qkv[i] = units[3].acc[i, me.m].astype(F32)
    homes[5].start()
    for c in out_v:
        c.wait()
    homes[6].start()
    for c in homes:
        c.wait()
    for c in sent:
        c.wait_send()
    for q in range(4):
        on_x(q).wait_send() if q < 2 else on_y(q).wait_send()
    for d in range(4):

        @pl.when(j != d)
        def _():
            to_heads(d).wait_send()
            to_columns(d).wait_send()

    for line in lines + [own]:
        line.close()


def back(gatt, qm, k, v, kt, lse, n1, wq, x, gmid, segc, segr, g1, vec, ids, step, dw, dwo):
    scratch = [
        pltpu.VMEM((4, 128, 384), BF),
        pltpu.VMEM((4, 128, 384), BF),
        pltpu.VMEM((3, 256, 192), BF),
        pltpu.VMEM((3, L, 256), F32),
        pltpu.VMEM((3, L, 256), F32),
        pltpu.VMEM((L, 768), BF),
        pltpu.VMEM((L, 768), BF),
        pltpu.VMEM((192, L), F32),
        pltpu.VMEM((L, 192), BF),
        pltpu.VMEM((L, 192), F32),
        pltpu.VMEM((L, 192), F32),
        pltpu.VMEM((256, D), F32),
        pltpu.VMEM((256, D), F32),
        pltpu.VMEM((1024, 192), F32),
        pltpu.VMEM((96, D), F32),
        pltpu.VMEM((96, D), F32),
        pltpu.VMEM((96, 256), F32),
        pltpu.VMEM((3, 96, 256), F32),
        pltpu.VMEM((8, 8, D), F32),
        DMA((7,)),
        DMA((4,)),
        DMA((4,)),
        pltpu.VMEM((4, 256, D), BF),
        pltpu.VMEM((4, 256, D), BF),
        pltpu.VMEM((4, 256, D), BF),
        DMA((4, 4)),
        pltpu.VMEM((3, 4, 2, 96, 256), BF),
        pltpu.VMEM((4, 128, 384), BF),
        pltpu.VMEM((8, 4, 128, 384), BF),
        pltpu.VMEM((1024, 1024), BF),
        pltpu.VMEM((8, D), F32),
        pltpu.VMEM((4, 8, D), F32),
        pltpu.VMEM((8, D), F32),
        DMA((3,)),
        DMA((3,)),
        DMA((4,)),
        DMA((4,)),
        DMA((16,)),
        DMA((16,)),
        DMA((7,)),
        DMA((7,)),
        DMA((2,)),
    ]
    for i, (nq, w) in enumerate(SHAPES):
        scratch += [
            pltpu.VMEM((nq, 4, 96, w), BF),
            pltpu.VMEM((nq, 4, 96, w), BF),
            pltpu.VMEM((nq, 2, 48, w), BF),
            pltpu.VMEM((nq, 2, 48, w), BF),
            pltpu.VMEM((nq, 48, w), BF),
            pltpu.VMEM((nq, 48, w), BF),
            DMA((2, 7)),
            DMA,
        ]
        if i < 3:
            scratch += [pltpu.VMEM((4, 96, w), BF), pltpu.VMEM((4, 96, w), BF), DMA((4, 4))]
    return pl.pallas_call(
        back_kernel,
        out_shape=(
            shape((256, D), F32),
            shape((1024, 192), F32),
            shape((96, D), F32),
            shape((96, D), F32),
            shape((96, 256), F32),
            shape((3, 96, 256), F32),
            shape((8, 8, D), F32),
        ),
        in_specs=[VM] * 15 + [pl.BlockSpec(memory_space=pltpu.SMEM)] + [ANY] * 2,
        out_specs=(ANY,) * 7,
        scratch_shapes=scratch,
        compiler_params=params(1),
        name="back",
    )(gatt, qm, k, v, kt, lse, n1, wq, x, gmid, segc, segr, g1, vec, ids, step, dw, dwo)


def tail_kernel(sp, din, tok, up, down, wout, qkv, *outs):
    o_time, o_din, o_tok, o_up, o_down, o_out, o_qkv = outs[:7]
    i = pl.program_id(0)
    row = (200 * i + lax.broadcasted_iota(jnp.int32, (200, D), 0)).astype(F32)
    total = jnp.zeros((200, D), F32)
    for d in range(8):
        total = total + jnp.where(row == sp[d, 7:8, :], sp[d, 6:7, :], 0.0)
    o_time[...] = total

    @pl.when(i == 0)
    def _():
        sums = sp[0]
        for d in range(1, 8):
            sums = sums + sp[d]
        for n, ref in enumerate(outs[7:]):
            ref[...] = sums[n : n + 1, :].reshape(D)
        o_din[...] = din[...]
        o_tok[...] = tok[...].T
        o_up[...] = up[...]
        o_down[...] = down[...]
        o_out[...] = wout[...].T[0:192, :]
        o_qkv[...] = qkv[:, :, 0:192]


def tail(*args):
    whole = lambda a: pl.BlockSpec(a.shape, lambda i: (0,) * len(a.shape))
    outs = (
        shape((256, D), F32),
        shape((192, 1024), F32),
        shape((96, D), F32),
        shape((96, D), F32),
        shape((192, 96), F32),
        shape((3, 96, 192), F32),
    ) + (shape((D,), F32),) * 6
    return pl.pallas_call(
        tail_kernel,
        grid=(5,),
        out_shape=(shape((1000, D), F32),) + outs,
        in_specs=[whole(a) for a in args],
        out_specs=(pl.BlockSpec((200, D), lambda i: (i, 0)),) + tuple(whole(a) for a in outs),
        compiler_params=pltpu.CompilerParams(vmem_limit_bytes=63 << 20, dimension_semantics=("arbitrary",)),
        name="tail",
    )(*args)


class Native:
    def __init__(self, ndp, nmp):
        self.ndp, self.nmp = ndp, nmp

    def gather_all(self, emb, trow, ids, w2, wo):
        over_mp = lambda a: lax.all_gather(a, "mp", axis=0, tiled=False)
        return (
            over_mp(emb),
            over_mp(trow),
            lax.all_gather(ids, "dp", axis=0, tiled=False),
            over_mp(w2),
            over_mp(wo),
        )

    def exchange(self, x, cid, name):
        return lax.all_to_all(x, "mp", split_axis=0, concat_axis=0, tiled=True)

    def reduce_all(self, gn, dw, dwo, dqkv):
        sum_mp = lambda a: lax.psum_scatter(a.astype(F32), "mp", scatter_dimension=0, tiled=True)
        sum_dp = lambda a: lax.psum_scatter(a, "dp", scatter_dimension=0, tiled=True)
        flat = lambda a: a.reshape(D, a.shape[-1])
        return (
            sum_mp(gn).reshape(gn.shape[1:]),
            sum_dp(flat(sum_mp(dw[0]))),
            sum_dp(flat(sum_mp(dw[1]))),
            sum_dp(flat(sum_mp(dwo[..., : D // self.nmp]))),
            sum_dp(flat(dqkv[..., : 3 * D // self.nmp].astype(F32))),
        )

    def final_exchange(self, tp, vec):
        x = lax.all_to_all(tp, "mp", split_axis=0, concat_axis=0, tiled=True)
        return (
            lax.all_gather(x, "dp", axis=0, tiled=False),
            lax.all_gather(lax.psum(vec, "mp"), "dp", axis=0, tiled=False),
        )


def layer_norm(stream, gain, shift):
    average = jnp.mean(stream, axis=-1, keepdims=True)
    centered = stream - average
    variance = jnp.mean(centered * centered, axis=-1, keepdims=True)
    return centered * lax.rsqrt(variance + 1e-05) * gain + shift


def allowed_pairs(seg_query, segments, first_row):
    key_pos = jnp.arange(L)
    query_pos = first_row + jnp.arange(QBLK)
    same_text = seg_query[:, None] == segments[None, :]
    self_or_text = (seg_query[:, None] != 0) | (query_pos[:, None] == key_pos[None, :])
    return same_text & self_or_text


def attend_forward(queries, key_rows, value_rows, segments):
    outputs = []
    log_parts = []
    for block_index in range(L // QBLK):
        first_row = block_index * QBLK
        query_block = queries[first_row : first_row + QBLK]
        allowed = allowed_pairs(segments[first_row : first_row + QBLK], segments, first_row)
        scores = jnp.einsum("qhd,khd->hqk", query_block, key_rows, preferred_element_type=F32) * 0.125
        masked = jnp.where(allowed[None], scores, -1e30)
        highest = jnp.max(masked, axis=-1, keepdims=True)
        exponents = jnp.exp(masked - highest)
        totals = jnp.sum(exponents, axis=-1, keepdims=True)
        weights = (exponents / totals).astype(BF)
        outputs.append(jnp.einsum("hqk,khd->qhd", weights, value_rows, preferred_element_type=F32).astype(BF))
        log_parts.append((highest + jnp.log(totals))[..., 0])
    return (jnp.concatenate(outputs, axis=0), jnp.concatenate(log_parts, axis=1))


def attend_backward(queries, key_rows, value_rows, segments, log_sums, grad_heads):
    grad_keys = jnp.zeros(key_rows.shape, F32)
    grad_values = jnp.zeros(value_rows.shape, F32)
    grad_queries = []
    for block_index in range(L // QBLK):
        first_row = block_index * QBLK
        query_block = queries[first_row : first_row + QBLK]
        grad_block = grad_heads[first_row : first_row + QBLK]
        allowed = allowed_pairs(segments[first_row : first_row + QBLK], segments, first_row)
        scores = jnp.einsum("qhd,khd->hqk", query_block, key_rows, preferred_element_type=F32) * 0.125
        masked = jnp.where(allowed[None], scores, -1e30)
        probs = jnp.exp(masked - log_sums[:, first_row : first_row + QBLK, None])
        rounded = probs.astype(BF)
        grad_probs = jnp.einsum("qhd,khd->hqk", grad_block, value_rows, preferred_element_type=F32)
        inner = jnp.sum(probs * grad_probs, axis=-1, keepdims=True)
        grad_scores = (probs * (grad_probs - inner)).astype(BF)
        grad_queries.append(
            jnp.einsum("hqk,khd->qhd", grad_scores, key_rows, preferred_element_type=F32) * 0.125
        )
        grad_keys = (
            grad_keys
            + jnp.einsum("hqk,qhd->khd", grad_scores, query_block, preferred_element_type=F32) * 0.125
        )
        grad_values = grad_values + jnp.einsum("hqk,qhd->khd", rounded, grad_block, preferred_element_type=F32)
    return (
        jnp.concatenate(grad_queries, axis=0).astype(BF),
        grad_keys.astype(BF),
        grad_values.astype(BF),
    )


def on_device_native(
    comm,
    token_ids,
    segment_ids,
    timesteps,
    token_table,
    time_table,
    ln1_gain,
    ln1_bias,
    w_qkv,
    w_out,
    attn_bias,
    ln2_gain,
    ln2_bias,
    w_up,
    w_down,
    mlp_bias,
    cotangent,
):
    group = lax.axis_size("mp")
    ndp = lax.axis_size("dp")
    member = lax.axis_index("mp")
    own_rows = L // group
    width = token_table.shape[1]
    heads_local = width // HD

    emb = fold(token_table[token_ids])
    time_row = lax.dynamic_slice_in_dim(time_table, timesteps[0], 1, 0)
    trow = jnp.broadcast_to(jnp.pad(time_row, ((0, 0), (0, 256 - width))), (16, 256))
    ids = token_ids.reshape(8, 128)
    w2 = jnp.stack((w_up, w_down))
    wo = w_out.reshape(width, 6, 128).transpose(1, 0, 2).reshape(6 * width, 128)
    E, TR, IDS, W2, WO = comm.gather_all(emb, trow, ids, w2, wo)

    time_full = TR[:, 0, :width].reshape(1, D).astype(F32)
    tokens = unfold(E).transpose(1, 0, 2).reshape(L, D)
    stream_all = tokens.astype(F32) + time_full
    stream_in = lax.dynamic_slice_in_dim(stream_all, member * own_rows, own_rows, 0)
    normed_one = layer_norm(stream_all, ln1_gain, ln1_bias).astype(BF)
    wq = w_qkv.transpose(1, 2, 0).reshape(3 * width, D)
    packed = contract_cols(normed_one, wq).astype(BF).reshape(L, 3, heads_local, HD)
    queries, key_rows, value_rows = packed[:, 0], packed[:, 1], packed[:, 2]
    attended, log_sums = attend_forward(queries, key_rows, value_rows, segment_ids)
    sent = fold(attended.reshape(group, own_rows, width))
    got = comm.exchange(sent, 1, "to_rows")

    att_own = unfold(got).transpose(1, 0, 2).reshape(own_rows, D)
    w_out_full = WO.reshape(group, 6, width, 128).transpose(0, 2, 1, 3).reshape(D, D)
    stream_mid = stream_in + dot(att_own, w_out_full) + attn_bias
    normed_two = layer_norm(stream_mid, ln2_gain, ln2_bias).astype(BF)
    own_segments = lax.dynamic_slice_in_dim(segment_ids, member * own_rows, own_rows, 0)
    grad_out = cotangent.astype(F32) * (own_segments != 0).astype(F32)[:, None]
    grad_mlp = grad_out.astype(BF)
    out = stream_mid + mlp_bias
    grad_norm_two = jnp.zeros((own_rows, D), F32)
    grads_up, grads_down = [], []
    for q in range(group):
        pre = dot(normed_two, W2[q, 0])
        act, back = jax.vjp(lambda v: jax.nn.gelu(v, approximate=True), pre)
        act = act.astype(BF)
        out = out + dot(act, W2[q, 1])
        grad_pre = back(contract_cols(grad_mlp, W2[q, 1]))[0].astype(BF)
        grad_norm_two = grad_norm_two + contract_cols(grad_pre, W2[q, 0])
        grads_up.append(contract_rows(normed_two, grad_pre).astype(BF))
        grads_down.append(contract_rows(grad_mlp, act).astype(BF))
    dw = jnp.stack((jnp.stack(grads_up), jnp.stack(grads_down)))
    norm_back_two = jax.vjp(layer_norm, stream_mid, ln2_gain, ln2_bias)[1]
    grad_mid_norm, grad_ln2_gain, grad_ln2_bias = norm_back_two(grad_norm_two)
    grad_mid = grad_out + grad_mid_norm
    grad_attn = grad_mid.astype(BF)
    dwo = contract_rows(grad_attn, att_own).astype(BF).reshape(D, group, width).transpose(1, 0, 2)
    dwo = jnp.pad(dwo, ((0, 0), (0, 0), (0, 256 - width)))
    grad_attended = contract_cols(grad_attn, w_out_full).astype(BF)
    sent = fold(grad_attended.reshape(own_rows, group, width).transpose(1, 0, 2))
    got = comm.exchange(sent, 2, "to_heads")

    grad_heads = unfold(got).reshape(L, heads_local, HD)
    grad_q, grad_k, grad_v = attend_backward(
        queries, key_rows, value_rows, segment_ids, log_sums, grad_heads
    )
    grad_packed = jnp.stack((grad_q, grad_k, grad_v), axis=1).reshape(L, 3 * width)
    dqkv = jnp.pad(contract_rows(normed_one, grad_packed).astype(BF), ((0, 0), (0, 640 - 3 * width)))
    gn = dot(grad_packed, wq).astype(BF).reshape(group, own_rows, D)

    pieces = lambda a: a.reshape(a.shape[:-2] + (ndp // 2, 2, D // ndp, a.shape[-1]))
    grad_norm_one, g_up, g_down, g_out, g_qkv = comm.reduce_all(
        gn, pieces(dw), pieces(dwo), pieces(dqkv)[None]
    )
    norm_back_one = jax.vjp(layer_norm, stream_in, ln1_gain, ln1_bias)[1]
    grad_in_norm, grad_ln1_gain, grad_ln1_bias = norm_back_one(grad_norm_one)
    input_grad = grad_mid + grad_in_norm
    tp = fold(input_grad.astype(BF).reshape(own_rows, group, width).transpose(1, 0, 2))
    step_row = jnp.where(member == 0, timesteps[0], 0).astype(F32)
    vec = jnp.stack(
        (
            grad_ln1_gain,
            grad_ln1_bias,
            jnp.sum(grad_mid, axis=0),
            grad_ln2_gain,
            grad_ln2_bias,
            jnp.sum(grad_out, axis=0),
            jnp.sum(input_grad, axis=0),
            jnp.broadcast_to(step_row, (D,)),
        )
    )
    X, SP = comm.final_exchange(tp, vec)
    rows_table = token_table.shape[0] // ndp
    columns = unfold(X).reshape(ndp * L, width)
    first = lax.axis_index("dp") * rows_table
    hot = (first + jnp.arange(rows_table))[:, None] == IDS.reshape(1, ndp * L)
    grad_token_table = dot(hot.astype(BF), columns)
    steps = SP[:, 7, 0].astype(jnp.int32)
    grad_time_table = jnp.zeros(time_table.shape[:1] + (D,), F32)
    at_row = jnp.arange(time_table.shape[0])[:, None]
    if ndp <= 8:
        for i in range(ndp):
            grad_time_table = grad_time_table + jnp.where(at_row == steps[i], SP[i, 6][None], 0.0)
    else:
        grad_time_table = grad_time_table.at[steps].add(SP[:, 6])
    sums = jnp.sum(SP[:, :6], axis=0)
    return (
        out.astype(BF),
        input_grad,
        grad_token_table,
        grad_time_table,
        sums[0],
        sums[1],
        g_qkv[:, : 3 * width].reshape(-1, 3, width),
        g_out[:, :width].T,
        sums[2],
        sums[3],
        sums[4],
        g_up,
        g_down.T,
        sums[5],
    )


def on_device_tuned(
    token_ids, segment_ids, timesteps, token_table, time_table, ln1_gain, ln1_bias, w_qkv, w_out, attn_bias,
    ln2_gain, ln2_bias, w_up, w_down, mlp_bias, cotangent,
):
    ndp, width = 8, 192
    ids8 = token_ids.reshape(8, 128)
    wq = w_qkv.transpose(1, 2, 0).reshape(3 * width, D)
    qm, k, v, kt, normed_one, stream_in, lse, att_own, segr, segc, IDS, W2, WO = front(
        token_ids, segment_ids, timesteps, ids8, token_table.T, time_table.T, ln1_gain, ln1_bias, wq, w_up, w_down, w_out
    )
    out, grad_mid, grad_attended, dw, dwo, vec = mid(
        att_own, stream_in, WO, W2, cotangent, segr, attn_bias, ln2_gain, ln2_bias, mlp_bias
    )
    pieces = lambda a: a.reshape(a.shape[:-2] + (ndp // 2, 2, D // ndp, a.shape[-1]))
    input_grad, grad_token_table, g_up, g_down, g_out, g_qkv, SP = back(
        grad_attended, qm, k, v, kt, lse, normed_one, wq, stream_in, grad_mid, segc, segr, ln1_gain, vec, IDS, timesteps,
        pieces(dw), pieces(dwo),
    )
    o_time, o_in, o_tok, o_up, o_down, o_out, o_qkv, *sums = tail(
        SP, input_grad, grad_token_table, g_up, g_down, g_out, g_qkv
    )
    return (
        out, o_in, o_tok.T, o_time, sums[0], sums[1], o_qkv.transpose(1, 0, 2), o_out, sums[2], sums[3], sums[4],
        o_up, o_down.T, sums[5],
    )


def solution(mesh):
    placed = (
        P("dp"),
        P("dp"),
        P("dp"),
        P(None, "mp"),
        P(None, "mp"),
        P(),
        P(),
        P(None, None, "mp"),
        P("mp", None),
        P(),
        P(),
        P(),
        P(None, "mp"),
        P("mp", None),
        P(),
        P(("dp", "mp"), None),
    )
    ndp, nmp = mesh.shape["dp"], mesh.shape["mp"]
    return jax.shard_map(
        on_device_tuned if (ndp, nmp) == (8, 4) else functools.partial(on_device_native, Native(ndp, nmp)),
        mesh=mesh,
        in_specs=placed,
        out_specs=(
            P(("dp", "mp"), None),
            P(("dp", "mp"), None),
            P("dp", "mp"),
            P(),
            P(),
            P(),
            P("dp", None, "mp"),
            P("mp", "dp"),
            P(),
            P(),
            P(),
            P("dp", "mp"),
            P("mp", "dp"),
            P(),
        ),
        check_vma=False,
    )
```

```python
import functools

import jax
import jax.numpy as jnp
from jax import lax
from jax.experimental import pallas as pl
from jax.experimental.pallas import tpu as pltpu
from jax.sharding import PartitionSpec as P

D = 768
HD = 64
L = 1024
QBLK = 512
BF = jnp.bfloat16
F32 = jnp.float32
MESH = pl.DeviceIdType.MESH
ANY = pl.BlockSpec(memory_space=pl.ANY)
VM = pl.BlockSpec(memory_space=pltpu.VMEM)
DMA = pltpu.SemaphoreType.DMA
EPS = 1e-05


def shape(dims, dtype):
    return jax.ShapeDtypeStruct(dims, dtype)


def dot(a, b):
    return jnp.dot(a, b, preferred_element_type=F32)


def contract_rows(left, right):
    return lax.dot_general(left, right, (((0,), (0,)), ((), ())), preferred_element_type=F32)


def contract_cols(left, right):
    return lax.dot_general(left, right, (((1,), (1,)), ((), ())), preferred_element_type=F32)


class Place:
    def __init__(self):
        self.p = p = lax.axis_index("dp")
        self.j = lax.axis_index("mp")
        core, x, y = p % 2, (p // 2) % 2, p // 4
        self.core, self.m = core, p // 2
        self.px = p + 2 - 4 * x
        self.py = p + 4 - 8 * y
        self.pd = self.px + 4 - 8 * y
        self.pc = p + 1 - 2 * core
        self.mx = self.px // 2
        self.my = self.py // 2
        self.md = self.pd // 2

    def z(self, hop):
        return (self.p, (self.j + hop) % 4)

    def at(self, dp):
        return (dp, self.j)


def meet(devices):
    barrier = pltpu.get_barrier_semaphore()
    for device in devices:
        pl.semaphore_signal(barrier, inc=1, device_id=device, device_id_type=MESH)
    pl.semaphore_wait(barrier, len(devices))


def push(src, dst, send, recv, device):
    return pltpu.make_async_remote_copy(
        src_ref=src, dst_ref=dst, send_sem=send, recv_sem=recv, device_id=device, device_id_type=MESH
    )


def params(cid):
    return pltpu.CompilerParams(collective_id=cid, has_side_effects=True, vmem_limit_bytes=60 << 20)


def head_mask(width, h):
    lane = lax.broadcasted_iota(jnp.int32, (1, width), 1)
    return ((lane >= HD * h) & (lane < HD * h + HD)).astype(F32)


def fold(rows):
    half = rows.shape[-2] // 2
    return jnp.concatenate((rows[..., :half, :], rows[..., half:, :]), axis=-1)


def unfold(packed):
    width = packed.shape[-1] // 2
    return jnp.concatenate((packed[..., :width], packed[..., width:]), axis=-2)


CH = 32


def line_of(ref):
    return ref[...].reshape(1, ref.shape[0])


def across(row):
    return jnp.broadcast_to(row, (128, row.shape[1])).T


def allowed(segc, sq, b, c):
    key = CH * c + lax.broadcasted_iota(jnp.int32, (CH, 256), 0)
    query = 256 * b + lax.broadcasted_iota(jnp.int32, (CH, 256), 1)
    return ((segc[CH * c : CH * c + CH, :] == sq) & (sq != 0.0)) | (key == query)


def lanes(b):
    return pl.ds(pl.multiple_of(256 * b, 256), 256)


def groups(x):
    return x.reshape(CH // 8, 8, 256)


def write_segments(seg, segr, segc):
    row = line_of(seg).astype(F32)
    segr[...] = row
    for i in range(8):
        segc[128 * i : 128 * i + 128, :] = across(row[:, 128 * i : 128 * i + 128])[:, 0:1]


class Weights:
    def __init__(self, me, W2, WO, zs, zr, ps, pr):
        self.me, self.W2, self.WO = me, W2, WO
        self.zs, self.zr, self.ps, self.pr = zs, zr, ps, pr

    def zpart(self, a, q, piece):
        if a < 2:
            return self.W2.at[q, a, pl.ds(96 * piece, 96), :]
        return self.WO.at[pl.ds(192 * q + 48 * (piece // 2), 48), pl.ds(384 * (piece % 2), 384)]

    def part(self, a, q, piece, half=None):
        if a < 2:
            lo, n = (0, 96) if half is None else (48 * half, 48)
            return self.W2.at[q, a, pl.ds(96 * piece + lo, n), :]
        lo, n = (0, 48) if half is None else ((0, 32), (32, 16))[half]
        return self.WO.at[pl.ds(192 * q + 48 * (piece // 2) + lo, n), pl.ds(384 * (piece % 2), 384)]

    def quarter(self, d, k):
        j = self.me.j
        return (j - k + 4) % 4 if d == 0 else (j + k) % 4

    def sends(self, d, k):
        j = self.me.j
        return (j < 3) & (j >= k) if d == 0 else (j > 0) & (j + k <= 3)

    def gets(self, d, k):
        j = self.me.j
        return j >= k + 1 if d == 0 else j + k + 1 <= 3

    def zcopy(self, d, k, a):
        p, q = self.me.p, self.quarter(d, k)
        part = self.zpart(a, q, p)
        return push(part, part, self.zs.at[d, k, a], self.zr.at[d, k, a], self.me.z(1 if d == 0 else 3))

    def zgot(self, d, k, a):
        dst = self.zpart(a, self.quarter(d, k + 1), self.me.p)
        return push(dst, dst, self.zs.at[d, k, a], self.zr.at[d, k, a], self.me.z(1))

    def zstart(self, k, arrays):
        for d in (0, 1):

            @pl.when(self.sends(d, k))
            def _():
                for a in arrays:
                    self.zcopy(d, k, a).start()

    def spread(self, k, a):
        self.zwait(k, (a,))
        self.pstart(k, 0, (a,))

    def turn(self, k, a):
        self.pwait(k, 0, (0, 1), (a,))
        self.pstart(k, 1, (a,))

    def last(self, k, a):
        self.pwait(k, 1, (0, 1), (a,))
        self.pstart(k, 2, (a,))

    def zown(self, k):
        for d in (0, 1):
            last = self.me.j == (k if d == 0 else 3 - k)

            @pl.when(self.sends(d, 0) & last)
            def _():
                self.zcopy(d, 0, 1).start()

    def zwait(self, k, arrays):
        for d in (0, 1):

            @pl.when(self.gets(d, k))
            def _():
                for a in arrays:
                    self.zgot(d, k, a).wait_recv()

    def routes(self, d, k, a, stage):
        me, q = self.me, self.quarter(d, k + 1)
        if stage == 0:
            return [(self.part(a, q, me.p), me.px), (self.part(a, q, me.p), me.py), (self.part(a, q, me.p), me.pc)]
        if stage == 1:
            return [
                (self.part(a, q, me.py, 0), me.px),
                (self.part(a, q, me.px, 1), me.py),
                (self.part(a, q, me.px), me.pc),
                (self.part(a, q, me.py), me.pc),
            ]
        return [(self.part(a, q, me.pd), me.pc)]

    def arrivals(self, d, k, a, stage):
        me, q = self.me, self.quarter(d, k + 1)
        c = me.pc - me.p
        if stage == 0:
            return [self.part(a, q, me.px), self.part(a, q, me.py), self.part(a, q, me.pc)]
        if stage == 1:
            return [
                self.part(a, q, me.pd, 0),
                self.part(a, q, me.pd, 1),
                self.part(a, q, me.px + c),
                self.part(a, q, me.py + c),
            ]
        return [self.part(a, q, me.pd + c)]

    def pstart(self, k, stage, arrays):
        for d in (0, 1):

            @pl.when(self.gets(d, k))
            def _():
                for a in arrays:
                    for i, (ref, dp) in enumerate(self.routes(d, k, a, stage)):
                        s = 3 * stage + i if stage < 2 else 7
                        push(ref, ref, self.ps.at[d, k, a, s], self.pr.at[d, k, a, s], self.me.at(dp)).start()

    def pwait(self, k, stage, which, arrays, send=False):
        for d in (0, 1):

            @pl.when(self.gets(d, k))
            def _():
                for a in arrays:
                    self.one(d, k, stage, which, a, send)

    def one(self, d, k, stage, which, a, send=False):
        if send:
            refs = [r for r, _ in self.routes(d, k, a, stage)]
        else:
            refs = self.arrivals(d, k, a, stage)
        for i in which:
            s = 3 * stage + i if stage < 2 else 7
            c = push(refs[i], refs[i], self.ps.at[d, k, a, s], self.pr.at[d, k, a, s], self.me.at(self.me.pc))
            c.wait_send() if send else c.wait_recv()

    def rest(self, step):
        for d, k, devices in NEEDS[step]:
            here = self.me.j == devices[0]
            for other in devices[1:]:
                here = here | (self.me.j == other)

            @pl.when(here)
            def _():
                for a in (0, 1):
                    self.one(d, k, 0, (2,), a)
                    self.one(d, k, 1, (2, 3), a)
                    self.one(d, k, 2, (0,), a)

    def out_rest(self):
        for k in range(3):
            self.pwait(k, 0, (2,), (2,))
            self.pwait(k, 1, (2, 3), (2,))
            self.pwait(k, 2, (0,), (2,))

    def finish(self):
        for k in range(3):
            self.pwait(k, 0, (0, 1, 2), (0, 1, 2), send=True)
            self.pwait(k, 1, (0, 1, 2, 3), (0, 1, 2), send=True)
            self.pwait(k, 2, (0,), (0, 1, 2), send=True)
            for d in (0, 1):

                @pl.when(self.sends(d, k))
                def _():
                    for a in (0, 1, 2):
                        self.zcopy(d, k, a).wait_send()


NEEDS = {
    1: ((0, 0, (1, 2, 3)), (1, 0, (0,))),
    2: ((1, 1, (0,)), (1, 0, (1, 2)), (0, 1, (3,))),
    3: ((1, 2, (0,)), (1, 1, (1,)), (0, 1, (2,)), (0, 2, (3,))),
}
ORDER = ((0, 1, 2, 3), (1, 0, 2, 3), (2, 1, 3, 0), (3, 2, 1, 0))


def quarter_at(j, i):
    total = 0
    for n in range(4):
        for m in range(4):
            total = total + ORDER[n][m] * ((j == n) & (i == m)).astype(jnp.int32)
    return total


def front_kernel(
    ids, seg, step, ids8, tabt, h_timet, g1, b1, h_wq, w_up, w_down, w_out, h_cot, pa, pg, pb2, pm,
    h_qm, h_k, h_v, h_kt, h_n1, h_x, h_lse, h_segr, h_segc, h_gmid, h_gatt, h_vec, h_out, IDS, dw_o, dwo_o,
    qm_o, k_o, v_o, kt_o, n1_o, x_o, lse_o, segr, segc, gmid_o, gatt_o, vec_o, out_o, wq, cot, timet,
    W2, WO, tab, hot, eb, E, tb, TR, vt, s, pb, ot, sendb, attg,
    att, hat, n2, n2t, gmt, gm, acc, gn2, stage, rc, accb, wst, wrc, wacc,
    es, er, ts, tr, is_, ir, zs, zr, ps, pr, as_, ar, ls, cs, cr, ws, wr, hs, os,
):
    me = Place()
    p, j = me.p, me.j
    fetch = pltpu.make_async_copy(tabt, tab, ls.at[0])
    fetch_time = pltpu.make_async_copy(h_timet, timet, ls.at[1])
    later = [pltpu.make_async_copy(h_wq, wq, ls.at[6]), pltpu.make_async_copy(h_cot, cot, ls.at[7])]
    fetch_time.start()
    fetch.start()
    pairs = (
        (qm_o, h_qm), (k_o, h_k), (v_o, h_v), (kt_o, h_kt), (n1_o, h_n1), (x_o, h_x), (lse_o, h_lse), (segr, h_segr),
        (segc, h_segc), (gmid_o, h_gmid), (gatt_o, h_gatt), (vec_o, h_vec), (out_o, h_out),
    )
    homes = [pltpu.make_async_copy(src, dst, os.at[i]) for i, (src, dst) in enumerate(pairs)]
    load = [
        pltpu.make_async_copy(w_up, W2.at[j, 0], ls.at[3]),
        pltpu.make_async_copy(w_down, W2.at[j, 1], ls.at[4]),
        pltpu.make_async_copy(w_out, WO.at[pl.ds(192 * j, 192), :], ls.at[5]),
    ]
    for c in load:
        c.start()
    for c in later:
        c.start()
    write_segments(seg, segr, segc)
    homes[7].start()
    homes[8].start()
    fetch_time.wait()
    lane = lax.broadcasted_iota(jnp.int32, (192, 1000), 1)
    column = jnp.sum(jnp.where(lane == step[0], timet[...].astype(F32), 0.0), axis=1, keepdims=True)
    tb[:, 0:192] = jnp.broadcast_to(column, (192, 128)).T[0:16, :].astype(BF)
    meet([me.z(1), me.z(2), me.z(3)] + [me.at((p + k) % 8) for k in range(1, 8)])
    w = Weights(me, W2, WO, zs, zr, ps, pr)

    def ecopy(d, k, c):
        q = w.quarter(d, k)
        dev = me.z(1 if d == 0 else 3)
        return push(eb.at[c] if k == 0 else E.at[q, c], E.at[q, c], es.at[d, k, c], er.at[d, k, c], dev)

    def estart(k, c):
        for d in (0, 1):

            @pl.when(w.sends(d, k))
            def _():
                ecopy(d, k, c).start()

    def ewait(k, c):
        for d in (0, 1):

            @pl.when(w.gets(d, k))
            def _():
                dst = E.at[w.quarter(d, k + 1), c]
                push(dst, dst, es.at[d, k, c], er.at[d, k, c], me.z(1)).wait_recv()

    here = [pltpu.make_async_copy(ids8, IDS.at[p], ls.at[2])]
    small = [push(tb, TR.at[j], ts.at[k - 1], tr.at[k - 1], me.z(k)) for k in (1, 2, 3)]
    small_ids = [push(ids8, IDS.at[p], is_.at[k - 1], ir.at[k - 1], me.at((p + k) % 8)) for k in range(1, 8)]
    ids_row = line_of(ids).astype(F32)

    def embed(c):
        token = across(ids_row[:, 256 * c : 256 * c + 256])
        s[0, 0:256, 0:192] = jnp.zeros((256, 192), F32)

        @pl.loop(0, 4)
        def _(v):
            base = (2048 * v).astype(F32)
            for i in range(16):
                word = lax.broadcasted_iota(jnp.int32, (256, 128), 1).astype(F32) + (base + 128.0 * i)
                hot[:, 128 * i : 128 * i + 128] = (token == word).astype(F32).astype(BF)
            s[0, 0:256, 0:192] += contract_cols(hot[...], tab[:, pl.ds(pl.multiple_of(2048 * v, 2048), 2048)])

        eb[c] = fold(s[0, 0:256, 0:192].astype(BF))
        estart(0, c)

    fetch.wait()
    for c in load:
        c.wait()
    w.zstart(0, (2, 0))
    embed(0)
    for c in small + here + small_ids:
        c.start()
    embed(1)
    w.spread(0, 2)
    w.zstart(1, (2,))
    embed(2)
    ewait(0, 0)
    estart(1, 0)
    w.spread(0, 0)
    embed(3)
    w.zown(0)
    ewait(0, 1)
    estart(1, 1)
    w.spread(1, 2)
    w.zstart(2, (2,))
    ewait(0, 2)
    estart(1, 2)
    ewait(1, 0)
    estart(2, 0)
    ewait(0, 3)
    estart(1, 3)
    w.zown(1)
    ewait(1, 1)
    estart(2, 1)
    w.spread(2, 2)
    ewait(1, 2)
    estart(2, 2)
    for c in small:
        c.wait()
    E[j] = eb[...]
    TR[j] = tb[...]
    for c in later:
        c.wait()
    time_row = jnp.concatenate([TR[q].astype(F32)[0:1, 0:192] for q in range(4)], axis=1)
    gain, shift = line_of(g1), line_of(b1)

    def norm_qkv(r):
        rows = slice(256 * r, 256 * r + 256)
        x = jnp.concatenate([unfold(E[q, r]) for q in range(4)], axis=1)
        x = x.astype(F32) + time_row
        centered = x - jnp.mean(x, axis=1, keepdims=True)
        variance = jnp.mean(centered * centered, axis=1, keepdims=True)
        normed = (centered * lax.rsqrt(variance + EPS) * gain + shift).astype(BF)
        n1_o[rows, :] = normed

        @pl.when(j == r)
        def _():
            x_o[...] = x

        q = contract_cols(normed, wq[0:192, :]).astype(BF).astype(F32) * 0.125
        for i in range(3):
            qm_o[i, rows, :] = (q * head_mask(192, i)).astype(BF)
        k_o[rows, :] = contract_cols(normed, wq[192:384, :]).astype(BF)
        v_o[rows, :] = contract_cols(normed, wq[384:576, :]).astype(BF)
        kt_o[:, rows] = contract_cols(wq[192:384, :], normed).astype(BF)
        vt[:, rows] = contract_cols(wq[384:576, :], normed).astype(BF)

    ewait(1, 3)
    estart(2, 3)
    w.zown(2)
    w.zstart(1, (0,))
    ewait(2, 0)
    norm_qkv(0)
    for k in range(3):
        w.turn(k, 2)
    w.turn(0, 0)
    ewait(2, 1)
    norm_qkv(1)
    for k in range(3):
        w.last(k, 2)
    w.last(0, 0)
    ewait(2, 2)
    norm_qkv(2)
    ewait(2, 3)
    norm_qkv(3)
    for c in homes[:6]:
        c.start()
    w.spread(0, 1)
    w.zstart(1, (1,))

    def att_copy(b):
        return push(sendb.at[b], attg.at[j], as_.at[b], ar.at[j], (p, b))

    def step0():
        w.spread(1, 0)
        w.zstart(2, (0,))

    def step1():
        w.turn(0, 1)

    def step2():
        w.spread(1, 1)
        w.zstart(2, (1,))

    def step3():
        w.turn(1, 0)
        w.last(0, 1)

    def step4():
        w.spread(2, 0)

    def step5():
        w.turn(1, 1)
        w.last(1, 0)

    def step6():
        w.spread(2, 1)

    steps = {1: step0, 3: step1, 4: step2, 6: step3, 8: step4, 10: step5, 11: step6}

    def slot(i, n):
        for k, step in {k: v for k, v in steps.items() if k % 3 == n}.items():
            pl.when(i == k // 3)(step)

    @pl.loop(0, 4)
    def _(i):
        b = (j + 1 + i) % 4
        sq = segr[0:1, lanes(b)]
        for h in range(3):
            s[h] = contract_cols(k_o[...], qm_o[h, lanes(b), :])
        slot(i, 0)
        top = [jnp.full((8, 256), -jnp.inf, F32)] * 3
        for c in range(L // CH):
            rows = slice(CH * c, CH * c + CH)
            ok = allowed(segc, sq, b, c)
            for h in range(3):
                x = jnp.where(ok, s[h, rows, :], -1e30)
                s[h, rows, :] = x
                top[h] = jnp.maximum(top[h], jnp.max(groups(x), axis=0))
        top = [jnp.max(m, axis=0, keepdims=True) for m in top]
        slot(i, 1)
        total = [jnp.zeros((8, 256), F32)] * 3
        for c in range(L // CH):
            rows = slice(CH * c, CH * c + CH)
            for h in range(3):
                e = jnp.exp(s[h, rows, :] - top[h])
                pb[h, rows, :] = e.astype(BF)
                total[h] = total[h] + jnp.sum(groups(e), axis=0)
        for h in range(3):
            t = jnp.sum(total[h], axis=0, keepdims=True)
            lse_o[3 * b + h] = top[h] + jnp.log(t)
            part = slice(64 * h, 64 * h + 64)
            ot[part, :] = dot(vt[part, :], pb[h]) * (1.0 / t)
        sendb[b] = fold(ot[...].T.astype(BF))

        @pl.when(b != j)
        def _():
            att_copy(b).start()

        slot(i, 2)

    homes[6].start()
    attg[j] = sendb[j]
    w.out_rest()
    for q in range(4):

        @pl.when(j != q)
        def _():
            push(attg.at[q], attg.at[q], as_.at[q], ar.at[q], me.z(1)).wait_recv()

    w.last(1, 1)
    w.turn(2, 0)
    att[...] = jnp.concatenate([unfold(attg[q]) for q in range(4)], axis=1)
    mid = x_o[...] + dot(att[...], WO[...]) + line_of(pa)
    h0, scale = norm_stats(mid)
    hat[...] = h0
    normed = h0 * line_of(pg) + line_of(pb2)
    n2[...] = normed.astype(BF)
    n2t[...] = normed.T.astype(BF)
    valid = across((segr[:, lanes(j)] != 0.0).astype(F32))[:, 0:1]
    gmid_o[...] = cot[...].astype(F32) * valid
    gm[...] = gmid_o[...].astype(BF)
    gmt[...] = gmid_o[...].T.astype(BF)
    acc[...] = mid + line_of(pm)
    gn2[...] = jnp.zeros_like(gn2)

    def to_sibling(i):
        return push(stage.at[i % 2, :, :, 1 - me.core], rc.at[i], cs.at[i], cr.at[i], me.at(me.pc))

    def save(i):
        return pltpu.make_async_copy(accb.at[i % 2], dw_o.at[:, quarter_at(j, i)], hs.at[i % 2])

    def chip(i):
        to_sibling(i).wait_recv()
        for u in range(2):
            for m in range(4):
                accb[i % 2, u, m] = stage[i % 2, u, m, me.core] + rc[i, u, m]
        save(i).start()

    def pump1():
        w.last(2, 1)
        w.rest(1)

    def pump2():
        w.rest(2)

    def pump3():
        w.rest(3)

    w.last(2, 0)
    w.turn(2, 1)

    @pl.loop(0, 4)
    def _(i):
        q = quarter_at(j, i)
        pl.when(i == 1)(pump1)
        pl.when(i == 2)(pump2)
        pl.when(i == 3)(pump3)
        pre = dot(n2[...], W2[q, 0])
        c = 0.7978845608028654
        t = jnp.tanh(c * (pre + 0.044715 * pre * pre * pre))
        act = (0.5 * pre * (1.0 + t)).astype(BF)
        slope = 0.5 * (1.0 + t) + 0.5 * pre * (1.0 - t * t) * (c * (1.0 + 3 * 0.044715 * pre * pre))
        acc[...] += dot(act, W2[q, 1])
        grad_pre = (contract_cols(gm[...], W2[q, 1]) * slope).astype(BF)
        gn2[...] += contract_cols(grad_pre, W2[q, 0])

        @pl.when(i >= 2)
        def _():
            to_sibling(i - 2).wait_send()
            save(i - 2).wait()

        for u, full in ((0, dot(n2t[...], grad_pre)), (1, dot(gmt[...], act))):
            for n in range(8):
                stage[i % 2, u, n // 2, n % 2] = full[96 * n : 96 * n + 96, :].astype(BF)
        to_sibling(i).start()

        @pl.when(i >= 1)
        def _():
            chip(i - 1)

    out_o[...] = acc[...].astype(BF)
    homes[12].start()
    grad = gmid_o[...]
    gn, h0 = gn2[...], hat[...]
    vec_o[...] = jnp.zeros_like(vec_o)
    vec_o[3:4, :] = rows_sum(gn * h0)
    vec_o[4:5, :] = rows_sum(gn)
    vec_o[5:6, :] = rows_sum(grad)
    gmid = grad + norm_back(gn, line_of(pg), h0, scale)
    gmid_o[...] = gmid
    vec_o[2:3, :] = rows_sum(gmid)
    gatt_o[...] = contract_cols(gmid.astype(BF), WO[...]).astype(BF)
    for c in homes[9:12]:
        c.start()
    full = dot(gmid.T.astype(BF), att[...]).astype(BF)
    for q in range(4):
        for n in range(8):
            wst[q, n // 2, n % 2, :, 0:192] = full[96 * n : 96 * n + 96, 192 * q : 192 * q + 192]
            wst[q, n // 2, n % 2, :, 192:256] = jnp.zeros((96, 64), BF)
    wo_copy = push(wst.at[:, :, 1 - me.core], wrc, ws, wr, me.at(me.pc))
    wo_copy.start()
    save(2).wait()
    chip(3)
    wo_copy.wait_recv()
    for q in range(4):
        for m in range(4):
            wacc[q, m] = wst[q, m, me.core] + wrc[q, m]
    wsave = pltpu.make_async_copy(wacc, dwo_o, hs.at[0])
    to_sibling(2).wait_send()
    to_sibling(3).wait_send()
    wo_copy.wait_send()
    wsave.start()
    for b in range(4):

        @pl.when(j != b)
        def _():
            att_copy(b).wait_send()

    for k in range(3):
        for d in (0, 1):

            @pl.when(w.sends(d, k))
            def _():
                for c in range(4):
                    ecopy(d, k, c).wait_send()

    w.finish()
    for c in small_ids + here:
        c.wait()
    save(3).wait()
    wsave.wait()
    for c in homes:
        c.wait()


FRONT_KEPT = (
    ((3, L, 192), BF),
    ((L, 192), BF),
    ((L, 192), BF),
    ((192, L), BF),
    ((L, D), BF),
    ((256, D), F32),
    ((12, 1, 256), F32),
    ((1, L), F32),
    ((L, 1), F32),
    ((256, D), F32),
    ((256, D), BF),
    ((8, D), F32),
    ((256, D), BF),
)


def front(*args):
    return pl.pallas_call(
        front_kernel,
        out_shape=tuple(shape(*a) for a in FRONT_KEPT)
        + (
            shape((8, 8, 128), jnp.int32),
            shape((2, 4, 4, 96, D), BF),
            shape((4, 4, 96, 256), BF),
        ),
        in_specs=[VM] * 2 + [pl.BlockSpec(memory_space=pltpu.SMEM)] + [ANY] * 3 + [VM] * 2 + [ANY] * 5 + [VM] * 4,
        out_specs=(ANY,) * 16,
        scratch_shapes=[pltpu.VMEM(*a) for a in FRONT_KEPT]
        + [
            pltpu.VMEM((576, D), BF),
            pltpu.VMEM((256, D), BF),
            pltpu.VMEM((192, 1000), BF),
            pltpu.VMEM((4, 2, D, D), BF),
            pltpu.VMEM((D, D), BF),
            pltpu.VMEM((192, 8192), BF),
            pltpu.VMEM((256, 2048), BF),
            pltpu.VMEM((4, 128, 384), BF),
            pltpu.VMEM((4, 4, 128, 384), BF),
            pltpu.VMEM((16, 256), BF),
            pltpu.VMEM((4, 16, 256), BF),
            pltpu.VMEM((192, L), BF),
            pltpu.VMEM((3, L, 256), F32),
            pltpu.VMEM((3, L, 256), BF),
            pltpu.VMEM((192, 256), F32),
            pltpu.VMEM((4, 128, 384), BF),
            pltpu.VMEM((4, 128, 384), BF),
            pltpu.VMEM((256, D), BF),
            pltpu.VMEM((256, D), F32),
            pltpu.VMEM((256, D), BF),
            pltpu.VMEM((D, 256), BF),
            pltpu.VMEM((D, 256), BF),
            pltpu.VMEM((256, D), BF),
            pltpu.VMEM((256, D), F32),
            pltpu.VMEM((256, D), F32),
            pltpu.VMEM((2, 2, 4, 2, 96, D), BF),
            pltpu.VMEM((4, 2, 4, 96, D), BF),
            pltpu.VMEM((2, 2, 4, 96, D), BF),
            pltpu.VMEM((4, 4, 2, 96, 256), BF),
            pltpu.VMEM((4, 4, 96, 256), BF),
            pltpu.VMEM((4, 4, 96, 256), BF),
            DMA((2, 3, 4)),
            DMA((2, 3, 4)),
            DMA((3,)),
            DMA((3,)),
            DMA((7,)),
            DMA((7,)),
            DMA((2, 3, 3)),
            DMA((2, 3, 3)),
            DMA((2, 3, 3, 8)),
            DMA((2, 3, 3, 8)),
            DMA((4,)),
            DMA((4,)),
            DMA((8,)),
            DMA((4,)),
            DMA((4,)),
            DMA,
            DMA,
            DMA((2,)),
            DMA((13,)),
        ],
        compiler_params=params(0),
        name="front",
    )(*args)

def norm_stats(x):
    centered = x - jnp.mean(x, axis=1, keepdims=True)
    scale = lax.rsqrt(jnp.mean(centered * centered, axis=1, keepdims=True) + EPS)
    return centered * scale, scale


def norm_back(grad, gain, hat, scale):
    t = grad * gain
    return scale * (t - jnp.mean(t, axis=1, keepdims=True) - hat * jnp.mean(t * hat, axis=1, keepdims=True))


def rows_sum(x):
    return jnp.sum(x, axis=0, keepdims=True)


class Line:
    def __init__(self, me, acc, up, down, sems):
        self.me, self.acc, self.up, self.down = me, acc, up, down
        self.us, self.ur, self.ds, self.dr = (sems.at[i] for i in range(4))

    def send(self, q, d):
        if d == 0:
            return push(self.acc(q), self.up.at[q], self.us.at[q], self.ur.at[q], self.me.z(1))
        return push(self.acc(q), self.down.at[q], self.ds.at[q], self.dr.at[q], self.me.z(3))

    def end(self, q, d):
        @pl.when(self.me.j == (0 if d == 0 else 3))
        def _():
            self.send(q, d).start()

    def first(self):
        for q in (3, 2, 1):
            self.end(q, 0)
        for q in (0, 1, 2):
            self.end(q, 1)

    def inner(self, steps):
        for q, d, j in steps:

            @pl.when(self.me.j == j)
            def _():
                c = self.send(q, d)
                c.wait_recv()
                ref = self.acc(q)
                ref[...] = ref[...] + (self.up if d == 0 else self.down)[q]
                c.start()

    def finish(self, out):
        j = self.me.j
        for q in range(4):

            @pl.when(j == q)
            def _():
                total = self.acc(q)[...].astype(F32)
                if q > 0:
                    self.send(q, 0).wait_recv()
                    total = total + self.up[q].astype(F32)
                if q < 3:
                    self.send(q, 1).wait_recv()
                    total = total + self.down[q].astype(F32)
                out[...] = total

    def close(self):
        j = self.me.j
        for q in range(4):

            @pl.when(j < q)
            def _():
                self.send(q, 0).wait_send()

            @pl.when(j > q)
            def _():
                self.send(q, 1).wait_send()


NEAR = ((3, 0, 1), (0, 1, 2))
FAR = ((3, 0, 2), (0, 1, 1), (2, 0, 1), (1, 1, 2))


class Unit:
    def __init__(self, me, src, acc, rc, rx, ry, rx2, ry2, sems, lsem):
        self.me, self.src, self.acc = me, src, acc
        self.rc, self.rx, self.ry, self.rx2, self.ry2 = rc, rx, ry, rx2, ry2
        self.s, self.r, self.lsem = sems.at[0], sems.at[1], lsem
        self.nq = acc.shape[0]

    def copies(self, stage):
        me, acc, s, r = self.me, self.acc, self.s, self.r
        lo, hi = pl.ds(0, 48), pl.ds(48, 48)
        if stage == 0:
            return [push(self.src.at[:, :, 1 - me.core], self.rc, s.at[0], r.at[0], me.at(me.pc))]
        if stage == 1:
            return [
                push(acc.at[:, me.md, lo], self.rx.at[:, 1], s.at[1], r.at[1], me.at(me.px)),
                push(acc.at[:, me.md, hi], self.ry.at[:, 1], s.at[2], r.at[2], me.at(me.py)),
                push(acc.at[:, me.mx, lo], self.rx.at[:, 0], s.at[3], r.at[3], me.at(me.px)),
                push(acc.at[:, me.my, hi], self.ry.at[:, 0], s.at[4], r.at[4], me.at(me.py)),
            ]
        return [
            push(acc.at[:, me.my, lo], self.ry2, s.at[5], r.at[5], me.at(me.py)),
            push(acc.at[:, me.mx, hi], self.rx2, s.at[6], r.at[6], me.at(me.px)),
        ]

    def load(self):
        src = self.src if self.rc is None else self.src.at[:, :, self.me.core]
        return pltpu.make_async_copy(src, self.acc, self.lsem)

    def begin(self):
        self.load().start()
        if self.rc is not None:
            self.copies(0)[0].start()

    def chip(self):
        self.load().wait()
        if self.rc is None:
            return
        self.copies(0)[0].wait_recv()

        @pl.loop(0, self.nq)
        def _(q):
            for m in range(4):
                self.acc[q, m] = self.acc[q, m] + self.rc[q, m]

    def cross(self):
        for c in self.copies(1):
            c.start()

    def turn(self):
        me = self.me
        first = self.copies(1)
        for c in first[:2]:
            c.wait()
        second = self.copies(2)

        @pl.loop(0, self.nq)
        def _(q):
            self.acc[q, me.my, 0:48] = self.acc[q, me.my, 0:48] + self.rx[q, 1]
            self.acc[q, me.mx, 48:96] = self.acc[q, me.mx, 48:96] + self.ry[q, 1]

        for c in second:
            c.start()
        for c in first[2:]:
            c.wait()

        @pl.loop(0, self.nq)
        def _(q):
            self.acc[q, me.m, 0:48] = self.acc[q, me.m, 0:48] + self.rx[q, 0]
            self.acc[q, me.m, 48:96] = self.acc[q, me.m, 48:96] + self.ry[q, 0]

    def settle(self):
        me = self.me
        for c in self.copies(2):
            c.wait()

        @pl.loop(0, self.nq)
        def _(q):
            self.acc[q, me.m, 0:48] = self.acc[q, me.m, 0:48] + self.ry2[q]
            self.acc[q, me.m, 48:96] = self.acc[q, me.m, 48:96] + self.rx2[q]

        if self.rc is not None:
            self.copies(0)[0].wait_send()

    def own(self, q):
        return self.acc.at[q, self.me.m]


SHAPES = ((4, 768), (4, 768), (4, 256), (3, 256))


def back_kernel(
    h_gatt, h_qm, h_k, h_v, h_kt, h_lse, h_n1, h_wq, h_x, h_gmid, h_segc, h_segr, h_vec, h_ids, dw, dwo, g1, step,
    h_in, h_tok, h_up, h_down, h_out, h_qkv, h_sp,
    gatt, qm, k, v, kt, lse, n1, wq, x, gmid, segc, segr, vec, IDS, gs, *scratch,
):
    me = Place()
    p, j = me.p, me.j
    pairs = (
        (h_gatt, gatt), (h_k, k), (h_qm, qm), (h_v, v), (h_segc, segc), (h_segr, segr), (h_lse, lse), (h_kt, kt),
        (h_n1, n1), (h_wq, wq), (h_x, x), (h_gmid, gmid), (h_vec, vec), (h_ids, IDS),
    )
    loads = [pltpu.make_async_copy(src, dst, gs.at[i]) for i, (src, dst) in enumerate(pairs)]
    for c in loads[:8]:
        c.start()
    meet([me.z(1), me.z(2), me.z(3)] + [me.at((p + i) % 8) for i in range(1, 8)])
    it = iter(scratch)
    take = lambda n: [next(it) for _ in range(n)]
    sendb, gbuf, dom, s, dp, pb, dsb, dqt, dqn, dk, dv, gn = take(12)
    o_in, o_tok, o_up, o_down, o_out, o_qkv, o_sp, hs = take(8)
    as_, ar = take(2)
    gacc, gup, gdown, gsem = take(4)
    qk, tb, X, hot, vbuf, SZ, vs = take(7)
    vzs, vzr, ts, tr, ps, pr, vps, vpr, ls = take(9)
    sources = (dw.at[1], dw.at[0], dwo, qk)
    units, lines = [], []
    for i, src in enumerate(sources):
        acc, rx, ry, rx2, ry2, sems, lsem = take(7)
        rc = take(1)[0] if i == 3 else None
        unit = Unit(me, src, acc, rc, rx, ry, rx2, ry2, sems, lsem)
        units.append(unit)
        if i < 3:
            up, down, sem = take(3)
            lines.append(Line(me, unit.own, up, down, sem))
    own = Line(me, lambda q: gacc.at[q], gup, gdown, gsem)

    homes = [
        pltpu.make_async_copy(src, dst, hs.at[i])
        for i, (src, dst) in enumerate(
            ((o_in, h_in), (o_tok, h_tok), (o_up, h_up), (o_down, h_down), (o_out, h_out), (o_qkv, h_qkv), (o_sp, h_sp))
        )
    ]

    def to_heads(d):
        return push(sendb.at[d], gbuf.at[j], as_.at[d], ar.at[j], (p, d))

    loads[0].wait()
    for d in range(4):
        sendb[d] = fold(gatt[:, 192 * d : 192 * d + 192])

        @pl.when(j != d)
        def _():
            to_heads(d).start()

    gbuf[j] = sendb[j]
    for i in (0, 2, 1):
        units[i].begin()
    for c in loads[8:]:
        c.start()
    dk[...] = jnp.zeros_like(dk)
    dv[...] = jnp.zeros_like(dv)

    units[0].chip()
    units[0].cross()
    units[2].chip()
    units[2].cross()
    units[1].chip()
    steps = {}

    def slot(i, n):
        for c, fn in {c: fn for c, fn in steps.items() if c % 3 == n}.items():
            pl.when(i == c // 3)(fn)

    for c in loads[1:8]:
        c.wait()

    @pl.loop(0, 4)
    def _(i):
        b = (j + i) % 4
        sq = segr[0:1, lanes(b)]

        @pl.when(i > 0)
        def _():
            push(gbuf.at[b], gbuf.at[b], as_.at[b], ar.at[b], me.z(1)).wait_recv()

        do = unfold(gbuf[b]).astype(F32)
        for h in range(3):
            dom[h] = (do * head_mask(192, h)).astype(BF)
            s[h] = contract_cols(k[...], qm[h, lanes(b), :])
            dp[h] = contract_cols(v[...], dom[h])
        slot(i, 0)
        ls_ = [lse[3 * b + h] for h in range(3)]
        inner = [jnp.zeros((8, 256), F32)] * 3
        for c in range(L // CH):
            rows = slice(CH * c, CH * c + CH)
            ok = allowed(segc, sq, b, c)
            for h in range(3):
                e = jnp.exp(jnp.where(ok, s[h, rows, :], -1e30) - ls_[h])
                s[h, rows, :] = e
                pb[rows, 256 * h : 256 * h + 256] = e.astype(BF)
                inner[h] = inner[h] + jnp.sum(groups(e * dp[h, rows, :]), axis=0)
        inner = [jnp.sum(a, axis=0, keepdims=True) for a in inner]
        slot(i, 1)
        for c in range(L // CH):
            rows = slice(CH * c, CH * c + CH)
            for h in range(3):
                grad = s[h, rows, :] * (dp[h, rows, :] - inner[h])
                dsb[rows, 256 * h : 256 * h + 256] = grad.astype(BF)
        dv[...] += dot(pb[...], dom[...].reshape(768, 192))
        dk[...] += dot(dsb[...], qm[:, lanes(b), :].reshape(768, 192))
        for h in range(3):
            part = slice(64 * h, 64 * h + 64)
            dqt[part, lanes(b)] = dot(kt[part, :], dsb[:, 256 * h : 256 * h + 256]) * 0.125
        slot(i, 2)

    for c in loads[8:]:
        c.wait()
    for q, starts in ((3, ((3, 0),)), (0, ((0, 1),)), (2, ((2, 0),)), (1, ((1, 1), (1, 0), (2, 1)))):
        rows = slice(256 * q, 256 * q + 256)
        dq = dqt[:, rows].T.astype(BF)
        dqn[rows, :] = dq
        total = dot(dq, wq[0:192, :]) + dot(dk[rows, :].astype(BF), wq[192:384, :])
        gacc[q] = (total + dot(dv[rows, :].astype(BF), wq[384:576, :])).astype(BF)
        for block, d in starts:
            own.end(block, d)
    units[0].turn()
    units[2].turn()
    units[1].cross()
    for i, grad in enumerate((dqn[...], dk[...].astype(BF), dv[...].astype(BF))):
        full = contract_rows(n1[...], grad).astype(BF)
        for piece in range(8):
            qk[i, piece // 2, piece % 2, :, 0:192] = full[96 * piece : 96 * piece + 96, :]
            qk[i, piece // 2, piece % 2, :, 192:256] = jnp.zeros((96, 64), BF)
    units[3].begin()
    own.inner(NEAR)
    units[3].chip()
    units[3].cross()
    units[0].settle()
    lines[0].first()
    own.inner(FAR)
    units[2].settle()
    units[1].turn()
    units[3].turn()
    own.finish(gn)

    hat, scale = norm_stats(x[...])
    grad = gn[...]
    dx = gmid[...] + norm_back(grad, line_of(g1), hat, scale)
    o_in[...] = dx
    homes[0].start()
    dxb = dx.astype(BF)

    def to_columns(d):
        return push(tb.at[d], X.at[p, j], ts.at[d], tr.at[j], (p, d))

    for d in range(4):
        tb[d] = fold(dxb[:, 192 * d : 192 * d + 192])

        @pl.when(j != d)
        def _():
            to_columns(d).start()

    X[p, j] = tb[j]
    vbuf[...] = vec[...]
    vbuf[0:1, :] = rows_sum(grad * hat)
    vbuf[1:2, :] = rows_sum(grad)
    vbuf[6:7, :] = rows_sum(dx)
    first = jnp.where(j == 0, step[0], 0).astype(F32)
    vbuf[7:8, :] = jnp.full((1, D), 1.0, F32) * first
    small = [push(vbuf, SZ.at[j], vzs.at[i - 1], vzr.at[i - 1], me.z(i)) for i in (1, 2, 3)]
    for c in small:
        c.start()
    SZ[j] = vbuf[...]

    def hop(ref, i, dev):
        return push(ref, ref, ps.at[i], pr.at[i], me.at(dev))

    def table(d, start=False):
        vocab = 1024 * p + lax.broadcasted_iota(jnp.int32, (1024, 128), 0)
        for g in range(8):
            hot[:, 128 * g : 128 * g + 128] = (vocab == IDS[d, g : g + 1, :]).astype(F32).astype(BF)
        rows = jnp.concatenate([unfold(X[d, q]) for q in range(4)], axis=0)
        part = dot(hot[...], rows)
        if start:
            o_tok[...] = part
        else:
            o_tok[...] += part

    sent = []
    here = me.pc - p

    def spread(i):
        q = (j + i) % 4
        if i > 0:
            push(X.at[p, q], X.at[p, q], ts.at[q], tr.at[q], me.z(1)).wait_recv()
        for c in (hop(X.at[p, q], 2 * q, me.px), hop(X.at[p, q], 2 * q + 1, me.py)):
            c.start()
            sent.append(c)

    def on_x(q):
        return hop(X.at[me.py, q], 8 + q, me.px)

    def on_y(q):
        return hop(X.at[me.px, q], 8 + q, me.py)

    def corner(i):
        q = (j + i) % 4
        hop(X.at[me.px, q], 2 * q, me.px).wait_recv()
        hop(X.at[me.py, q], 2 * q + 1, me.py).wait_recv()

        @pl.when(q < 2)
        def _():
            on_x(q).start()

        @pl.when(q >= 2)
        def _():
            on_y(q).start()

    def to_core(d, i):
        c = hop(X.at[d], i, me.pc)
        c.start()
        sent.append(c)

    spread(0)
    lines[0].inner(NEAR)
    units[1].settle()
    lines[1].first()
    spread(1)
    spread(3)
    lines[2].first()
    corner(0)
    for c in small:
        c.wait()
    vs[...] = SZ[0] + SZ[1] + SZ[2] + SZ[3]
    out_v = [push(vs, o_sp.at[p], vps.at[i - 1], vpr.at[i - 1], me.at((p + i) % 8)) for i in range(1, 8)]
    for c in out_v:
        c.start()
    o_sp[p] = vs[...]
    lines[0].inner(FAR)
    spread(2)
    to_core(p, 12)
    corner(1)
    corner(3)
    table(p, start=True)
    lines[1].inner(NEAR)
    corner(2)
    to_core(me.px, 13)
    to_core(me.py, 14)
    units[3].settle()
    lines[2].inner(NEAR)
    hop(X.at[me.pc], 12, me.pc).wait_recv()
    table(me.pc)
    lines[1].inner(FAR)
    table(me.px)
    for q in range(4):
        hop(X.at[me.pd, q], 8 + q, me.px).wait_recv()
    to_core(me.pd, 15)
    lines[2].inner(FAR)
    table(me.py)
    table(me.pd)
    hop(X.at[me.px + here], 13, me.pc).wait_recv()
    table(me.px + here)
    hop(X.at[me.py + here], 14, me.pc).wait_recv()
    table(me.py + here)
    hop(X.at[me.pd + here], 15, me.pc).wait_recv()
    table(me.pd + here)
    homes[1].start()
    lines[0].finish(o_down)
    homes[3].start()
    lines[2].finish(o_out)
    homes[4].start()
    lines[1].finish(o_up)
    homes[2].start()
    for i in range(3):
        o_qkv[i] = units[3].acc[i, me.m].astype(F32)
    homes[5].start()
    for c in out_v:
        c.wait()
    homes[6].start()
    for c in homes:
        c.wait()
    for c in sent:
        c.wait_send()
    for q in range(4):
        on_x(q).wait_send() if q < 2 else on_y(q).wait_send()
    for d in range(4):

        @pl.when(j != d)
        def _():
            to_heads(d).wait_send()
            to_columns(d).wait_send()

    for line in lines + [own]:
        line.close()


BACK_KEPT = (
    ((256, D), BF),
    ((3, L, 192), BF),
    ((L, 192), BF),
    ((L, 192), BF),
    ((192, L), BF),
    ((12, 1, 256), F32),
    ((L, D), BF),
    ((576, D), BF),
    ((256, D), F32),
    ((256, D), F32),
    ((L, 1), F32),
    ((1, L), F32),
    ((8, D), F32),
    ((8, 8, 128), jnp.int32),
)


def back(*args):
    scratch = [pltpu.VMEM(*a) for a in BACK_KEPT] + [
        DMA((14,)),
        pltpu.VMEM((4, 128, 384), BF),
        pltpu.VMEM((4, 128, 384), BF),
        pltpu.VMEM((3, 256, 192), BF),
        pltpu.VMEM((3, L, 256), F32),
        pltpu.VMEM((3, L, 256), F32),
        pltpu.VMEM((L, 768), BF),
        pltpu.VMEM((L, 768), BF),
        pltpu.VMEM((192, L), F32),
        pltpu.VMEM((L, 192), BF),
        pltpu.VMEM((L, 192), F32),
        pltpu.VMEM((L, 192), F32),
        pltpu.VMEM((256, D), F32),
        pltpu.VMEM((256, D), F32),
        pltpu.VMEM((1024, 192), F32),
        pltpu.VMEM((96, D), F32),
        pltpu.VMEM((96, D), F32),
        pltpu.VMEM((96, 256), F32),
        pltpu.VMEM((3, 96, 256), F32),
        pltpu.VMEM((8, 8, D), F32),
        DMA((7,)),
        DMA((4,)),
        DMA((4,)),
        pltpu.VMEM((4, 256, D), BF),
        pltpu.VMEM((4, 256, D), BF),
        pltpu.VMEM((4, 256, D), BF),
        DMA((4, 4)),
        pltpu.VMEM((3, 4, 2, 96, 256), BF),
        pltpu.VMEM((4, 128, 384), BF),
        pltpu.VMEM((8, 4, 128, 384), BF),
        pltpu.VMEM((1024, 1024), BF),
        pltpu.VMEM((8, D), F32),
        pltpu.VMEM((4, 8, D), F32),
        pltpu.VMEM((8, D), F32),
        DMA((3,)),
        DMA((3,)),
        DMA((4,)),
        DMA((4,)),
        DMA((16,)),
        DMA((16,)),
        DMA((7,)),
        DMA((7,)),
        DMA((2,)),
    ]
    for i, (nq, w) in enumerate(SHAPES):
        scratch += [
            pltpu.VMEM((nq, 4, 96, w), BF),
            pltpu.VMEM((nq, 2, 48, w), BF),
            pltpu.VMEM((nq, 2, 48, w), BF),
            pltpu.VMEM((nq, 48, w), BF),
            pltpu.VMEM((nq, 48, w), BF),
            DMA((2, 7)),
            DMA,
        ]
        if i == 3:
            scratch += [pltpu.VMEM((nq, 4, 96, w), BF)]
        else:
            scratch += [pltpu.VMEM((4, 96, w), BF), pltpu.VMEM((4, 96, w), BF), DMA((4, 4))]
    return pl.pallas_call(
        back_kernel,
        out_shape=(
            shape((256, D), F32),
            shape((1024, 192), F32),
            shape((96, D), F32),
            shape((96, D), F32),
            shape((96, 256), F32),
            shape((3, 96, 256), F32),
            shape((8, 8, D), F32),
        ),
        in_specs=[ANY] * 16 + [VM, pl.BlockSpec(memory_space=pltpu.SMEM)],
        out_specs=(ANY,) * 7,
        scratch_shapes=scratch,
        compiler_params=params(1),
        name="back",
    )(*args)


def tail_kernel(sp, din, tok, up, down, wout, qkv, *outs):
    o_time, o_din, o_tok, o_up, o_down, o_out, o_qkv = outs[:7]
    i = pl.program_id(0)
    row = (200 * i + lax.broadcasted_iota(jnp.int32, (200, D), 0)).astype(F32)
    total = jnp.zeros((200, D), F32)
    for d in range(8):
        total = total + jnp.where(row == sp[d, 7:8, :], sp[d, 6:7, :], 0.0)
    o_time[...] = total

    @pl.when(i == 0)
    def _():
        sums = sp[0]
        for d in range(1, 8):
            sums = sums + sp[d]
        for n, ref in enumerate(outs[7:]):
            ref[...] = sums[n : n + 1, :].reshape(D)
        o_din[...] = din[...]
        o_tok[...] = tok[...].T
        o_up[...] = up[...]
        o_down[...] = down[...]
        o_out[...] = wout[...].T[0:192, :]
        o_qkv[...] = qkv[:, :, 0:192]


def tail(*args):
    whole = lambda a: pl.BlockSpec(a.shape, lambda i: (0,) * len(a.shape))
    outs = (
        shape((256, D), F32),
        shape((192, 1024), F32),
        shape((96, D), F32),
        shape((96, D), F32),
        shape((192, 96), F32),
        shape((3, 96, 192), F32),
    ) + (shape((D,), F32),) * 6
    return pl.pallas_call(
        tail_kernel,
        grid=(5,),
        out_shape=(shape((1000, D), F32),) + outs,
        in_specs=[whole(a) for a in args],
        out_specs=(pl.BlockSpec((200, D), lambda i: (i, 0)),) + tuple(whole(a) for a in outs),
        compiler_params=pltpu.CompilerParams(vmem_limit_bytes=63 << 20, dimension_semantics=("arbitrary",)),
        name="tail",
    )(*args)


class Native:
    def __init__(self, ndp, nmp):
        self.ndp, self.nmp = ndp, nmp

    def gather_all(self, emb, trow, ids, w2, wo):
        over_mp = lambda a: lax.all_gather(a, "mp", axis=0, tiled=False)
        return (
            over_mp(emb),
            over_mp(trow),
            lax.all_gather(ids, "dp", axis=0, tiled=False),
            over_mp(w2),
            over_mp(wo),
        )

    def exchange(self, x, cid, name):
        return lax.all_to_all(x, "mp", split_axis=0, concat_axis=0, tiled=True)

    def reduce_all(self, gn, dw, dwo, dqkv):
        sum_mp = lambda a: lax.psum_scatter(a.astype(F32), "mp", scatter_dimension=0, tiled=True)
        sum_dp = lambda a: lax.psum_scatter(a, "dp", scatter_dimension=0, tiled=True)
        flat = lambda a: a.reshape(D, a.shape[-1])
        return (
            sum_mp(gn).reshape(gn.shape[1:]),
            sum_dp(flat(sum_mp(dw[0]))),
            sum_dp(flat(sum_mp(dw[1]))),
            sum_dp(flat(sum_mp(dwo[..., : D // self.nmp]))),
            sum_dp(flat(dqkv[..., : 3 * D // self.nmp].astype(F32))),
        )

    def final_exchange(self, tp, vec):
        x = lax.all_to_all(tp, "mp", split_axis=0, concat_axis=0, tiled=True)
        return (
            lax.all_gather(x, "dp", axis=0, tiled=False),
            lax.all_gather(lax.psum(vec, "mp"), "dp", axis=0, tiled=False),
        )


def layer_norm(stream, gain, shift):
    average = jnp.mean(stream, axis=-1, keepdims=True)
    centered = stream - average
    variance = jnp.mean(centered * centered, axis=-1, keepdims=True)
    return centered * lax.rsqrt(variance + 1e-05) * gain + shift


def allowed_pairs(seg_query, segments, first_row):
    key_pos = jnp.arange(L)
    query_pos = first_row + jnp.arange(QBLK)
    same_text = seg_query[:, None] == segments[None, :]
    self_or_text = (seg_query[:, None] != 0) | (query_pos[:, None] == key_pos[None, :])
    return same_text & self_or_text


def attend_forward(queries, key_rows, value_rows, segments):
    outputs = []
    log_parts = []
    for block_index in range(L // QBLK):
        first_row = block_index * QBLK
        query_block = queries[first_row : first_row + QBLK]
        allowed = allowed_pairs(segments[first_row : first_row + QBLK], segments, first_row)
        scores = jnp.einsum("qhd,khd->hqk", query_block, key_rows, preferred_element_type=F32) * 0.125
        masked = jnp.where(allowed[None], scores, -1e30)
        highest = jnp.max(masked, axis=-1, keepdims=True)
        exponents = jnp.exp(masked - highest)
        totals = jnp.sum(exponents, axis=-1, keepdims=True)
        weights = (exponents / totals).astype(BF)
        outputs.append(jnp.einsum("hqk,khd->qhd", weights, value_rows, preferred_element_type=F32).astype(BF))
        log_parts.append((highest + jnp.log(totals))[..., 0])
    return (jnp.concatenate(outputs, axis=0), jnp.concatenate(log_parts, axis=1))


def attend_backward(queries, key_rows, value_rows, segments, log_sums, grad_heads):
    grad_keys = jnp.zeros(key_rows.shape, F32)
    grad_values = jnp.zeros(value_rows.shape, F32)
    grad_queries = []
    for block_index in range(L // QBLK):
        first_row = block_index * QBLK
        query_block = queries[first_row : first_row + QBLK]
        grad_block = grad_heads[first_row : first_row + QBLK]
        allowed = allowed_pairs(segments[first_row : first_row + QBLK], segments, first_row)
        scores = jnp.einsum("qhd,khd->hqk", query_block, key_rows, preferred_element_type=F32) * 0.125
        masked = jnp.where(allowed[None], scores, -1e30)
        probs = jnp.exp(masked - log_sums[:, first_row : first_row + QBLK, None])
        rounded = probs.astype(BF)
        grad_probs = jnp.einsum("qhd,khd->hqk", grad_block, value_rows, preferred_element_type=F32)
        inner = jnp.sum(probs * grad_probs, axis=-1, keepdims=True)
        grad_scores = (probs * (grad_probs - inner)).astype(BF)
        grad_queries.append(
            jnp.einsum("hqk,khd->qhd", grad_scores, key_rows, preferred_element_type=F32) * 0.125
        )
        grad_keys = (
            grad_keys
            + jnp.einsum("hqk,qhd->khd", grad_scores, query_block, preferred_element_type=F32) * 0.125
        )
        grad_values = grad_values + jnp.einsum("hqk,qhd->khd", rounded, grad_block, preferred_element_type=F32)
    return (
        jnp.concatenate(grad_queries, axis=0).astype(BF),
        grad_keys.astype(BF),
        grad_values.astype(BF),
    )


def on_device_native(
    comm,
    token_ids,
    segment_ids,
    timesteps,
    token_table,
    time_table,
    ln1_gain,
    ln1_bias,
    w_qkv,
    w_out,
    attn_bias,
    ln2_gain,
    ln2_bias,
    w_up,
    w_down,
    mlp_bias,
    cotangent,
):
    group = lax.axis_size("mp")
    ndp = lax.axis_size("dp")
    member = lax.axis_index("mp")
    own_rows = L // group
    width = token_table.shape[1]
    heads_local = width // HD

    emb = fold(token_table[token_ids])
    time_row = lax.dynamic_slice_in_dim(time_table, timesteps[0], 1, 0)
    trow = jnp.broadcast_to(jnp.pad(time_row, ((0, 0), (0, 256 - width))), (16, 256))
    ids = token_ids.reshape(8, 128)
    w2 = jnp.stack((w_up, w_down))
    wo = w_out.reshape(width, 6, 128).transpose(1, 0, 2).reshape(6 * width, 128)
    E, TR, IDS, W2, WO = comm.gather_all(emb, trow, ids, w2, wo)

    time_full = TR[:, 0, :width].reshape(1, D).astype(F32)
    tokens = unfold(E).transpose(1, 0, 2).reshape(L, D)
    stream_all = tokens.astype(F32) + time_full
    stream_in = lax.dynamic_slice_in_dim(stream_all, member * own_rows, own_rows, 0)
    normed_one = layer_norm(stream_all, ln1_gain, ln1_bias).astype(BF)
    wq = w_qkv.transpose(1, 2, 0).reshape(3 * width, D)
    packed = contract_cols(normed_one, wq).astype(BF).reshape(L, 3, heads_local, HD)
    queries, key_rows, value_rows = packed[:, 0], packed[:, 1], packed[:, 2]
    attended, log_sums = attend_forward(queries, key_rows, value_rows, segment_ids)
    sent = fold(attended.reshape(group, own_rows, width))
    got = comm.exchange(sent, 1, "to_rows")

    att_own = unfold(got).transpose(1, 0, 2).reshape(own_rows, D)
    w_out_full = WO.reshape(group, 6, width, 128).transpose(0, 2, 1, 3).reshape(D, D)
    stream_mid = stream_in + dot(att_own, w_out_full) + attn_bias
    normed_two = layer_norm(stream_mid, ln2_gain, ln2_bias).astype(BF)
    own_segments = lax.dynamic_slice_in_dim(segment_ids, member * own_rows, own_rows, 0)
    grad_out = cotangent.astype(F32) * (own_segments != 0).astype(F32)[:, None]
    grad_mlp = grad_out.astype(BF)
    out = stream_mid + mlp_bias
    grad_norm_two = jnp.zeros((own_rows, D), F32)
    grads_up, grads_down = [], []
    for q in range(group):
        pre = dot(normed_two, W2[q, 0])
        act, back = jax.vjp(lambda v: jax.nn.gelu(v, approximate=True), pre)
        act = act.astype(BF)
        out = out + dot(act, W2[q, 1])
        grad_pre = back(contract_cols(grad_mlp, W2[q, 1]))[0].astype(BF)
        grad_norm_two = grad_norm_two + contract_cols(grad_pre, W2[q, 0])
        grads_up.append(contract_rows(normed_two, grad_pre).astype(BF))
        grads_down.append(contract_rows(grad_mlp, act).astype(BF))
    dw = jnp.stack((jnp.stack(grads_up), jnp.stack(grads_down)))
    norm_back_two = jax.vjp(layer_norm, stream_mid, ln2_gain, ln2_bias)[1]
    grad_mid_norm, grad_ln2_gain, grad_ln2_bias = norm_back_two(grad_norm_two)
    grad_mid = grad_out + grad_mid_norm
    grad_attn = grad_mid.astype(BF)
    dwo = contract_rows(grad_attn, att_own).astype(BF).reshape(D, group, width).transpose(1, 0, 2)
    dwo = jnp.pad(dwo, ((0, 0), (0, 0), (0, 256 - width)))
    grad_attended = contract_cols(grad_attn, w_out_full).astype(BF)
    sent = fold(grad_attended.reshape(own_rows, group, width).transpose(1, 0, 2))
    got = comm.exchange(sent, 2, "to_heads")

    grad_heads = unfold(got).reshape(L, heads_local, HD)
    grad_q, grad_k, grad_v = attend_backward(
        queries, key_rows, value_rows, segment_ids, log_sums, grad_heads
    )
    grad_packed = jnp.stack((grad_q, grad_k, grad_v), axis=1).reshape(L, 3 * width)
    dqkv = jnp.pad(contract_rows(normed_one, grad_packed).astype(BF), ((0, 0), (0, 640 - 3 * width)))
    gn = dot(grad_packed, wq).astype(BF).reshape(group, own_rows, D)

    pieces = lambda a: a.reshape(a.shape[:-2] + (ndp // 2, 2, D // ndp, a.shape[-1]))
    grad_norm_one, g_up, g_down, g_out, g_qkv = comm.reduce_all(
        gn, pieces(dw), pieces(dwo), pieces(dqkv)[None]
    )
    norm_back_one = jax.vjp(layer_norm, stream_in, ln1_gain, ln1_bias)[1]
    grad_in_norm, grad_ln1_gain, grad_ln1_bias = norm_back_one(grad_norm_one)
    input_grad = grad_mid + grad_in_norm
    tp = fold(input_grad.astype(BF).reshape(own_rows, group, width).transpose(1, 0, 2))
    step_row = jnp.where(member == 0, timesteps[0], 0).astype(F32)
    vec = jnp.stack(
        (
            grad_ln1_gain,
            grad_ln1_bias,
            jnp.sum(grad_mid, axis=0),
            grad_ln2_gain,
            grad_ln2_bias,
            jnp.sum(grad_out, axis=0),
            jnp.sum(input_grad, axis=0),
            jnp.broadcast_to(step_row, (D,)),
        )
    )
    X, SP = comm.final_exchange(tp, vec)
    rows_table = token_table.shape[0] // ndp
    columns = unfold(X).reshape(ndp * L, width)
    first = lax.axis_index("dp") * rows_table
    hot = (first + jnp.arange(rows_table))[:, None] == IDS.reshape(1, ndp * L)
    grad_token_table = dot(hot.astype(BF), columns)
    steps = SP[:, 7, 0].astype(jnp.int32)
    grad_time_table = jnp.zeros(time_table.shape[:1] + (D,), F32)
    at_row = jnp.arange(time_table.shape[0])[:, None]
    if ndp <= 8:
        for i in range(ndp):
            grad_time_table = grad_time_table + jnp.where(at_row == steps[i], SP[i, 6][None], 0.0)
    else:
        grad_time_table = grad_time_table.at[steps].add(SP[:, 6])
    sums = jnp.sum(SP[:, :6], axis=0)
    return (
        out.astype(BF),
        input_grad,
        grad_token_table,
        grad_time_table,
        sums[0],
        sums[1],
        g_qkv[:, : 3 * width].reshape(-1, 3, width),
        g_out[:, :width].T,
        sums[2],
        sums[3],
        sums[4],
        g_up,
        g_down.T,
        sums[5],
    )


def on_device_tuned(
    token_ids, segment_ids, timesteps, token_table, time_table, ln1_gain, ln1_bias, w_qkv, w_out, attn_bias,
    ln2_gain, ln2_bias, w_up, w_down, mlp_bias, cotangent,
):
    width = 192
    ids8 = token_ids.reshape(8, 128)
    wq = w_qkv.transpose(1, 2, 0).reshape(3 * width, D)
    qm, k, v, kt, normed_one, stream_in, lse, segr, segc, grad_mid, grad_attended, vec, out, IDS, dw, dwo = front(
        token_ids, segment_ids, timesteps, ids8, token_table.T, time_table.T, ln1_gain, ln1_bias, wq, w_up, w_down, w_out,
        cotangent, attn_bias, ln2_gain, ln2_bias, mlp_bias,
    )
    input_grad, grad_token_table, g_up, g_down, g_out, g_qkv, SP = back(
        grad_attended, qm, k, v, kt, lse, normed_one, wq, stream_in, grad_mid, segc, segr, vec, IDS, dw, dwo, ln1_gain,
        timesteps,
    )
    o_time, o_in, o_tok, o_up, o_down, o_out, o_qkv, *sums = tail(
        SP, input_grad, grad_token_table, g_up, g_down, g_out, g_qkv
    )
    return (
        out, o_in, o_tok.T, o_time, sums[0], sums[1], o_qkv.transpose(1, 0, 2), o_out, sums[2], sums[3], sums[4],
        o_up, o_down.T, sums[5],
    )


def solution(mesh):
    placed = (
        P("dp"),
        P("dp"),
        P("dp"),
        P(None, "mp"),
        P(None, "mp"),
        P(),
        P(),
        P(None, None, "mp"),
        P("mp", None),
        P(),
        P(),
        P(),
        P(None, "mp"),
        P("mp", None),
        P(),
        P(("dp", "mp"), None),
    )
    ndp, nmp = mesh.shape["dp"], mesh.shape["mp"]
    return jax.shard_map(
        on_device_tuned if (ndp, nmp) == (8, 4) else functools.partial(on_device_native, Native(ndp, nmp)),
        mesh=mesh,
        in_specs=placed,
        out_specs=(
            P(("dp", "mp"), None),
            P(("dp", "mp"), None),
            P("dp", "mp"),
            P(),
            P(),
            P(),
            P("dp", None, "mp"),
            P("mp", "dp"),
            P(),
            P(),
            P(),
            P("dp", "mp"),
            P("mp", "dp"),
            P(),
        ),
        check_vma=False,
    )
```

```python
import functools

import jax
import jax.numpy as jnp
from jax import lax
from jax.experimental import pallas as pl
from jax.experimental.pallas import tpu as pltpu
from jax.sharding import PartitionSpec as P

D = 768
HD = 64
L = 1024
QBLK = 512
BF = jnp.bfloat16
F32 = jnp.float32
MESH = pl.DeviceIdType.MESH
ANY = pl.BlockSpec(memory_space=pl.ANY)
VM = pl.BlockSpec(memory_space=pltpu.VMEM)
DMA = pltpu.SemaphoreType.DMA
EPS = 1e-05


def shape(dims, dtype):
    return jax.ShapeDtypeStruct(dims, dtype)


def dot(a, b):
    return jnp.dot(a, b, preferred_element_type=F32)


def contract_rows(left, right):
    return lax.dot_general(left, right, (((0,), (0,)), ((), ())), preferred_element_type=F32)


def contract_cols(left, right):
    return lax.dot_general(left, right, (((1,), (1,)), ((), ())), preferred_element_type=F32)


class Place:
    def __init__(self):
        self.p = p = lax.axis_index("dp")
        self.j = lax.axis_index("mp")
        core, x, y = p % 2, (p // 2) % 2, p // 4
        self.core, self.m = core, p // 2
        self.px = p + 2 - 4 * x
        self.py = p + 4 - 8 * y
        self.pd = self.px + 4 - 8 * y
        self.pc = p + 1 - 2 * core
        self.mx = self.px // 2
        self.my = self.py // 2
        self.md = self.pd // 2

    def z(self, hop):
        return (self.p, (self.j + hop) % 4)

    def at(self, dp):
        return (dp, self.j)


def meet(devices):
    barrier = pltpu.get_barrier_semaphore()
    for device in devices:
        pl.semaphore_signal(barrier, inc=1, device_id=device, device_id_type=MESH)
    pl.semaphore_wait(barrier, len(devices))


def push(src, dst, send, recv, device):
    return pltpu.make_async_remote_copy(
        src_ref=src, dst_ref=dst, send_sem=send, recv_sem=recv, device_id=device, device_id_type=MESH
    )


def params(cid):
    return pltpu.CompilerParams(collective_id=cid, has_side_effects=True, vmem_limit_bytes=60 << 20)


def head_mask(width, h):
    lane = lax.broadcasted_iota(jnp.int32, (1, width), 1)
    return ((lane >= HD * h) & (lane < HD * h + HD)).astype(F32)


def fold(rows):
    half = rows.shape[-2] // 2
    return jnp.concatenate((rows[..., :half, :], rows[..., half:, :]), axis=-1)


def unfold(packed):
    width = packed.shape[-1] // 2
    return jnp.concatenate((packed[..., :width], packed[..., width:]), axis=-2)


CH = 32


def line_of(ref):
    return ref[...].reshape(1, ref.shape[0])


def across(row):
    return jnp.broadcast_to(row, (128, row.shape[1])).T


def allowed(segc, sq, b, c):
    key = CH * c + lax.broadcasted_iota(jnp.int32, (CH, 256), 0)
    query = 256 * b + lax.broadcasted_iota(jnp.int32, (CH, 256), 1)
    return ((segc[CH * c : CH * c + CH, :] == sq) & (sq != 0.0)) | (key == query)


def lanes(b):
    return pl.ds(pl.multiple_of(256 * b, 256), 256)


def groups(x):
    return x.reshape(CH // 8, 8, 256)


def write_segments(seg, segr, segc):
    row = line_of(seg).astype(F32)
    segr[...] = row
    for i in range(8):
        segc[128 * i : 128 * i + 128, :] = across(row[:, 128 * i : 128 * i + 128])[:, 0:1]


class Weights:
    def __init__(self, me, W2, WO, zs, zr, ps, pr):
        self.me, self.W2, self.WO = me, W2, WO
        self.zs, self.zr, self.ps, self.pr = zs, zr, ps, pr

    def zpart(self, a, q, piece):
        if a < 2:
            return self.W2.at[q, a, pl.ds(96 * piece, 96), :]
        return self.WO.at[pl.ds(192 * q + 48 * (piece // 2), 48), pl.ds(384 * (piece % 2), 384)]

    def part(self, a, q, piece, half=None):
        if a < 2:
            lo, n = (0, 96) if half is None else (48 * half, 48)
            return self.W2.at[q, a, pl.ds(96 * piece + lo, n), :]
        lo, n = (0, 48) if half is None else ((0, 32), (32, 16))[half]
        return self.WO.at[pl.ds(192 * q + 48 * (piece // 2) + lo, n), pl.ds(384 * (piece % 2), 384)]

    def quarter(self, d, k):
        j = self.me.j
        return (j - k + 4) % 4 if d == 0 else (j + k) % 4

    def sends(self, d, k):
        j = self.me.j
        return (j < 3) & (j >= k) if d == 0 else (j > 0) & (j + k <= 3)

    def gets(self, d, k):
        j = self.me.j
        return j >= k + 1 if d == 0 else j + k + 1 <= 3

    def zcopy(self, d, k, a):
        p, q = self.me.p, self.quarter(d, k)
        part = self.zpart(a, q, p)
        return push(part, part, self.zs.at[d, k, a], self.zr.at[d, k, a], self.me.z(1 if d == 0 else 3))

    def zgot(self, d, k, a):
        dst = self.zpart(a, self.quarter(d, k + 1), self.me.p)
        return push(dst, dst, self.zs.at[d, k, a], self.zr.at[d, k, a], self.me.z(1))

    def zstart(self, k, arrays):
        for d in (0, 1):

            @pl.when(self.sends(d, k))
            def _():
                for a in arrays:
                    self.zcopy(d, k, a).start()

    def spread(self, k, a):
        self.zwait(k, (a,))
        self.pstart(k, 0, (a,))

    def turn(self, k, a):
        self.pwait(k, 0, (0, 1), (a,))
        self.pstart(k, 1, (a,))

    def last(self, k, a):
        self.pwait(k, 1, (0, 1), (a,))
        self.pstart(k, 2, (a,))

    def zown(self, k):
        for d in (0, 1):
            last = self.me.j == (k if d == 0 else 3 - k)

            @pl.when(self.sends(d, 0) & last)
            def _():
                self.zcopy(d, 0, 1).start()

    def zwait(self, k, arrays):
        for d in (0, 1):

            @pl.when(self.gets(d, k))
            def _():
                for a in arrays:
                    self.zgot(d, k, a).wait_recv()

    def routes(self, d, k, a, stage):
        me, q = self.me, self.quarter(d, k + 1)
        if stage == 0:
            return [(self.part(a, q, me.p), me.px), (self.part(a, q, me.p), me.py), (self.part(a, q, me.p), me.pc)]
        if stage == 1:
            return [
                (self.part(a, q, me.py, 0), me.px),
                (self.part(a, q, me.px, 1), me.py),
                (self.part(a, q, me.px), me.pc),
                (self.part(a, q, me.py), me.pc),
            ]
        return [(self.part(a, q, me.pd), me.pc)]

    def arrivals(self, d, k, a, stage):
        me, q = self.me, self.quarter(d, k + 1)
        c = me.pc - me.p
        if stage == 0:
            return [self.part(a, q, me.px), self.part(a, q, me.py), self.part(a, q, me.pc)]
        if stage == 1:
            return [
                self.part(a, q, me.pd, 0),
                self.part(a, q, me.pd, 1),
                self.part(a, q, me.px + c),
                self.part(a, q, me.py + c),
            ]
        return [self.part(a, q, me.pd + c)]

    def pstart(self, k, stage, arrays):
        for d in (0, 1):

            @pl.when(self.gets(d, k))
            def _():
                for a in arrays:
                    for i, (ref, dp) in enumerate(self.routes(d, k, a, stage)):
                        s = 3 * stage + i if stage < 2 else 7
                        push(ref, ref, self.ps.at[d, k, a, s], self.pr.at[d, k, a, s], self.me.at(dp)).start()

    def pwait(self, k, stage, which, arrays, send=False):
        for d in (0, 1):

            @pl.when(self.gets(d, k))
            def _():
                for a in arrays:
                    self.one(d, k, stage, which, a, send)

    def one(self, d, k, stage, which, a, send=False):
        if send:
            refs = [r for r, _ in self.routes(d, k, a, stage)]
        else:
            refs = self.arrivals(d, k, a, stage)
        for i in which:
            s = 3 * stage + i if stage < 2 else 7
            c = push(refs[i], refs[i], self.ps.at[d, k, a, s], self.pr.at[d, k, a, s], self.me.at(self.me.pc))
            c.wait_send() if send else c.wait_recv()

    def rest(self, step):
        for d, k, devices in NEEDS[step]:
            here = self.me.j == devices[0]
            for other in devices[1:]:
                here = here | (self.me.j == other)

            @pl.when(here)
            def _():
                for a in (0, 1):
                    self.one(d, k, 0, (2,), a)
                    self.one(d, k, 1, (2, 3), a)
                    self.one(d, k, 2, (0,), a)

    def out_rest(self):
        for k in range(3):
            self.pwait(k, 0, (2,), (2,))
            self.pwait(k, 1, (2, 3), (2,))
            self.pwait(k, 2, (0,), (2,))

    def finish(self):
        for k in range(3):
            self.pwait(k, 0, (0, 1, 2), (0, 1, 2), send=True)
            self.pwait(k, 1, (0, 1, 2, 3), (0, 1, 2), send=True)
            self.pwait(k, 2, (0,), (0, 1, 2), send=True)
            for d in (0, 1):

                @pl.when(self.sends(d, k))
                def _():
                    for a in (0, 1, 2):
                        self.zcopy(d, k, a).wait_send()


NEEDS = {
    1: ((0, 0, (1, 2, 3)), (1, 0, (0,))),
    2: ((1, 1, (0,)), (1, 0, (1, 2)), (0, 1, (3,))),
    3: ((1, 2, (0,)), (1, 1, (1,)), (0, 1, (2,)), (0, 2, (3,))),
}
ORDER = ((0, 1, 2, 3), (1, 0, 2, 3), (2, 1, 3, 0), (3, 2, 1, 0))


def quarter_at(j, i):
    total = 0
    for n in range(4):
        for m in range(4):
            total = total + ORDER[n][m] * ((j == n) & (i == m)).astype(jnp.int32)
    return total


def front_kernel(
    ids, seg, step, ids8, tabt, h_timet, g1, b1, h_wq, w_up, w_down, w_out, h_cot, pa, pg, pb2, pm,
    h_qm, h_k, h_v, h_kt, h_n1, h_x, h_lse, h_segr, h_segc, h_gmid, h_gatt, h_vec, h_out, IDS, dw_o, dwo_o,
    qm_o, k_o, v_o, kt_o, n1_o, x_o, lse_o, segr, segc, gmid_o, gatt_o, vec_o, out_o, wq, cot, timet,
    W2, WO, tab, hot, eb, E, tb, TR, vt, s, pb, ot, sendb, attg,
    att, hat, n2, n2t, gmt, gm, acc, gn2, stage, rc, accb, wst, wrc, wacc,
    es, er, ts, tr, is_, ir, zs, zr, ps, pr, as_, ar, ls, cs, cr, ws, wr, hs, os,
):
    me = Place()
    p, j = me.p, me.j
    fetch = pltpu.make_async_copy(tabt, tab, ls.at[0])
    fetch_time = pltpu.make_async_copy(h_timet, timet, ls.at[1])
    later = [pltpu.make_async_copy(h_wq, wq, ls.at[6]), pltpu.make_async_copy(h_cot, cot, ls.at[7])]
    fetch_time.start()
    fetch.start()
    pairs = (
        (qm_o, h_qm), (k_o, h_k), (v_o, h_v), (kt_o, h_kt), (n1_o, h_n1), (x_o, h_x), (lse_o, h_lse), (segr, h_segr),
        (segc, h_segc), (gmid_o, h_gmid), (gatt_o, h_gatt), (vec_o, h_vec), (out_o, h_out),
    )
    homes = [pltpu.make_async_copy(src, dst, os.at[i]) for i, (src, dst) in enumerate(pairs)]
    load = [
        pltpu.make_async_copy(w_up, W2.at[j, 0], ls.at[3]),
        pltpu.make_async_copy(w_down, W2.at[j, 1], ls.at[4]),
        pltpu.make_async_copy(w_out, WO.at[pl.ds(192 * j, 192), :], ls.at[5]),
    ]
    for c in load:
        c.start()
    for c in later:
        c.start()
    write_segments(seg, segr, segc)
    homes[7].start()
    homes[8].start()
    fetch_time.wait()
    lane = lax.broadcasted_iota(jnp.int32, (192, 1000), 1)
    column = jnp.sum(jnp.where(lane == step[0], timet[...].astype(F32), 0.0), axis=1, keepdims=True)
    tb[:, 0:192] = jnp.broadcast_to(column, (192, 128)).T[0:16, :].astype(BF)
    meet([me.z(1), me.z(2), me.z(3)] + [me.at((p + k) % 8) for k in range(1, 8)])
    w = Weights(me, W2, WO, zs, zr, ps, pr)

    def ecopy(d, k, c):
        q = w.quarter(d, k)
        dev = me.z(1 if d == 0 else 3)
        return push(eb.at[c] if k == 0 else E.at[q, c], E.at[q, c], es.at[d, k, c], er.at[d, k, c], dev)

    def estart(k, c):
        for d in (0, 1):

            @pl.when(w.sends(d, k))
            def _():
                ecopy(d, k, c).start()

    def ewait(k, c):
        for d in (0, 1):

            @pl.when(w.gets(d, k))
            def _():
                dst = E.at[w.quarter(d, k + 1), c]
                push(dst, dst, es.at[d, k, c], er.at[d, k, c], me.z(1)).wait_recv()

    here = [pltpu.make_async_copy(ids8, IDS.at[p], ls.at[2])]
    small = [push(tb, TR.at[j], ts.at[k - 1], tr.at[k - 1], me.z(k)) for k in (1, 2, 3)]
    small_ids = [push(ids8, IDS.at[p], is_.at[k - 1], ir.at[k - 1], me.at((p + k) % 8)) for k in range(1, 8)]
    ids_row = line_of(ids).astype(F32)

    def embed(c):
        token = across(ids_row[:, 256 * c : 256 * c + 256])
        s[0:256, 0:192] = jnp.zeros((256, 192), F32)

        @pl.loop(0, 4)
        def _(v):
            base = (2048 * v).astype(F32)
            for i in range(16):
                word = lax.broadcasted_iota(jnp.int32, (256, 128), 1).astype(F32) + (base + 128.0 * i)
                hot[:, 128 * i : 128 * i + 128] = (token == word).astype(F32).astype(BF)
            s[0:256, 0:192] += contract_cols(hot[...], tab[:, pl.ds(pl.multiple_of(2048 * v, 2048), 2048)])

        eb[c] = fold(s[0:256, 0:192].astype(BF))
        estart(0, c)

    fetch.wait()
    for c in load:
        c.wait()
    w.zstart(0, (2, 0))
    embed(0)
    for c in small + here + small_ids:
        c.start()
    embed(1)
    w.spread(0, 2)
    w.zstart(1, (2,))
    embed(2)
    ewait(0, 0)
    estart(1, 0)
    w.spread(0, 0)
    embed(3)
    w.zown(0)
    ewait(0, 1)
    estart(1, 1)
    w.spread(1, 2)
    w.zstart(2, (2,))
    ewait(0, 2)
    estart(1, 2)
    ewait(1, 0)
    estart(2, 0)
    ewait(0, 3)
    estart(1, 3)
    w.zown(1)
    ewait(1, 1)
    estart(2, 1)
    w.spread(2, 2)
    ewait(1, 2)
    estart(2, 2)
    for c in small:
        c.wait()
    E[j] = eb[...]
    TR[j] = tb[...]
    for c in later:
        c.wait()
    time_row = jnp.concatenate([TR[q].astype(F32)[0:1, 0:192] for q in range(4)], axis=1)
    gain, shift = line_of(g1), line_of(b1)

    def norm_qkv(r):
        rows = slice(256 * r, 256 * r + 256)
        x = jnp.concatenate([unfold(E[q, r]) for q in range(4)], axis=1)
        x = x.astype(F32) + time_row
        centered = x - jnp.mean(x, axis=1, keepdims=True)
        variance = jnp.mean(centered * centered, axis=1, keepdims=True)
        normed = (centered * lax.rsqrt(variance + EPS) * gain + shift).astype(BF)
        n1_o[rows, :] = normed

        @pl.when(j == r)
        def _():
            x_o[...] = x

        q = contract_cols(normed, wq[0:192, :]).astype(BF).astype(F32) * 0.125
        for i in range(3):
            qm_o[i, rows, :] = (q * head_mask(192, i)).astype(BF)
        k_o[rows, :] = contract_cols(normed, wq[192:384, :]).astype(BF)
        v_o[rows, :] = contract_cols(normed, wq[384:576, :]).astype(BF)
        kt_o[:, rows] = contract_cols(wq[192:384, :], normed).astype(BF)
        vt[:, rows] = contract_cols(wq[384:576, :], normed).astype(BF)

    ewait(1, 3)
    estart(2, 3)
    w.zown(2)
    w.zstart(1, (0,))
    ewait(2, 0)
    norm_qkv(0)
    for k in range(3):
        w.turn(k, 2)
    w.turn(0, 0)
    ewait(2, 1)
    norm_qkv(1)
    for k in range(3):
        w.last(k, 2)
    w.last(0, 0)
    ewait(2, 2)
    norm_qkv(2)
    ewait(2, 3)
    norm_qkv(3)
    for c in homes[:6]:
        c.start()
    w.spread(0, 1)
    w.zstart(1, (1,))

    def att_copy(b):
        return push(sendb.at[b], attg.at[j], as_.at[b], ar.at[j], (p, b))

    def step0():
        w.spread(1, 0)
        w.zstart(2, (0,))

    def step1():
        w.turn(0, 1)

    def step2():
        w.spread(1, 1)
        w.zstart(2, (1,))

    def step3():
        w.turn(1, 0)
        w.last(0, 1)

    def step4():
        w.spread(2, 0)

    def step5():
        w.turn(1, 1)
        w.last(1, 0)

    steps = {1: step0, 3: step1, 4: step2, 6: step3, 9: step5, 11: step4}

    def slot(i, n):
        for k, step in {k: v for k, v in steps.items() if k % 3 == n}.items():
            pl.when(i == k // 3)(step)

    @pl.loop(0, 4)
    def _(i):
        b = (j + 1 + i) % 4
        sq = segr[0:1, lanes(b)]
        s[...] = contract_cols(k_o[...], qm_o[:, lanes(b), :].reshape(768, 192))
        slot(i, 0)
        top = [jnp.full((8, 256), -jnp.inf, F32)] * 3
        for c in range(L // CH):
            rows = slice(CH * c, CH * c + CH)
            ok = allowed(segc, sq, b, c)
            for h in range(3):
                part = slice(256 * h, 256 * h + 256)
                x = jnp.where(ok, s[rows, part], -1e30)
                s[rows, part] = x
                top[h] = jnp.maximum(top[h], jnp.max(groups(x), axis=0))
        top = [jnp.max(m, axis=0, keepdims=True) for m in top]
        slot(i, 1)
        total = [jnp.zeros((8, 256), F32)] * 3
        for c in range(L // CH):
            rows = slice(CH * c, CH * c + CH)
            for h in range(3):
                part = slice(256 * h, 256 * h + 256)
                e = jnp.exp(s[rows, part] - top[h])
                pb[rows, part] = e.astype(BF)
                total[h] = total[h] + jnp.sum(groups(e), axis=0)
        summed = dot(vt[...], pb[...])
        for h in range(3):
            t = jnp.sum(total[h], axis=0, keepdims=True)
            lse_o[3 * b + h] = top[h] + jnp.log(t)
            part = slice(64 * h, 64 * h + 64)
            ot[part, :] = summed[part, 256 * h : 256 * h + 256] * (1.0 / t)
        sendb[b] = fold(ot[...].T.astype(BF))

        @pl.when(b != j)
        def _():
            att_copy(b).start()

        slot(i, 2)

    homes[6].start()
    attg[j] = sendb[j]
    valid = across((segr[:, lanes(j)] != 0.0).astype(F32))[:, 0:1]
    gmid_o[...] = cot[...].astype(F32) * valid
    gm[...] = gmid_o[...].astype(BF)
    gmt[...] = gmid_o[...].T.astype(BF)
    gn2[...] = jnp.zeros_like(gn2)
    vec_o[...] = jnp.zeros_like(vec_o)
    vec_o[5:6, :] = rows_sum(gmid_o[...])
    w.out_rest()
    for q in range(4):

        @pl.when(j != q)
        def _():
            push(attg.at[q], attg.at[q], as_.at[q], ar.at[q], me.z(1)).wait_recv()

    w.last(1, 1)
    att[...] = jnp.concatenate([unfold(attg[q]) for q in range(4)], axis=1)
    mid = x_o[...] + dot(att[...], WO[...]) + line_of(pa)
    h0, scale = norm_stats(mid)
    hat[...] = h0
    normed = h0 * line_of(pg) + line_of(pb2)
    n2[...] = normed.astype(BF)
    n2t[...] = normed.T.astype(BF)
    acc[...] = mid + line_of(pm)

    def to_sibling(i):
        return push(stage.at[i % 2, :, :, 1 - me.core], rc.at[i], cs.at[i], cr.at[i], me.at(me.pc))

    def save(i):
        return pltpu.make_async_copy(accb.at[i % 2], dw_o.at[:, quarter_at(j, i)], hs.at[i % 2])

    def chip(i):
        to_sibling(i).wait_recv()
        for u in range(2):
            for m in range(4):
                accb[i % 2, u, m] = stage[i % 2, u, m, me.core] + rc[i, u, m]
        save(i).start()

    def pump1():
        w.rest(1)
        w.turn(2, 0)
        w.spread(2, 1)

    def pump2():
        w.rest(2)
        w.last(2, 0)

    def pump3():
        w.last(2, 1)
        w.rest(3)

    @pl.loop(0, 4)
    def _(i):
        q = quarter_at(j, i)
        pl.when(i == 1)(pump1)
        pl.when(i == 2)(pump2)
        pl.when(i == 3)(pump3)
        pre = dot(n2[...], W2[q, 0])
        c = 0.7978845608028654
        t = jnp.tanh(c * (pre + 0.044715 * pre * pre * pre))
        act = (0.5 * pre * (1.0 + t)).astype(BF)
        slope = 0.5 * (1.0 + t) + 0.5 * pre * (1.0 - t * t) * (c * (1.0 + 3 * 0.044715 * pre * pre))
        acc[...] += dot(act, W2[q, 1])
        grad_pre = (contract_cols(gm[...], W2[q, 1]) * slope).astype(BF)
        gn2[...] += contract_cols(grad_pre, W2[q, 0])
        pl.when(i == 2)(functools.partial(w.turn, 2, 1))

        @pl.when(i >= 2)
        def _():
            to_sibling(i - 2).wait_send()
            save(i - 2).wait()

        for u, full in ((0, dot(n2t[...], grad_pre)), (1, dot(gmt[...], act))):
            for n in range(8):
                stage[i % 2, u, n // 2, n % 2] = full[96 * n : 96 * n + 96, :].astype(BF)
        to_sibling(i).start()

        @pl.when(i >= 1)
        def _():
            chip(i - 1)

    grad = gmid_o[...]
    gn, h0 = gn2[...], hat[...]
    vec_o[3:4, :] = rows_sum(gn * h0)
    vec_o[4:5, :] = rows_sum(gn)
    gmid = grad + norm_back(gn, line_of(pg), h0, scale)
    gmid_o[...] = gmid
    vec_o[2:3, :] = rows_sum(gmid)
    gatt_o[...] = contract_cols(gmid.astype(BF), WO[...]).astype(BF)
    for c in homes[9:12]:
        c.start()
    out_o[...] = acc[...].astype(BF)
    homes[12].start()
    full = dot(gmid.T.astype(BF), att[...]).astype(BF)
    for n in range(8):
        wst[0, n // 2, n % 2] = full[96 * n : 96 * n + 96, :]
    wo_copy = push(wst.at[:, :, 1 - me.core], wrc, ws, wr, me.at(me.pc))
    wo_copy.start()
    save(2).wait()
    chip(3)
    wo_copy.wait_recv()
    for m in range(4):
        wacc[0, m] = wst[0, m, me.core] + wrc[0, m]
    wsave = pltpu.make_async_copy(wacc, dwo_o, hs.at[0])
    to_sibling(2).wait_send()
    to_sibling(3).wait_send()
    wo_copy.wait_send()
    wsave.start()
    for b in range(4):

        @pl.when(j != b)
        def _():
            att_copy(b).wait_send()

    for k in range(3):
        for d in (0, 1):

            @pl.when(w.sends(d, k))
            def _():
                for c in range(4):
                    ecopy(d, k, c).wait_send()

    w.finish()
    for c in small_ids + here:
        c.wait()
    save(3).wait()
    wsave.wait()
    for c in homes:
        c.wait()


FRONT_KEPT = (
    ((3, L, 192), BF),
    ((L, 192), BF),
    ((L, 192), BF),
    ((192, L), BF),
    ((L, D), BF),
    ((256, D), F32),
    ((12, 1, 256), F32),
    ((1, L), F32),
    ((L, 1), F32),
    ((256, D), F32),
    ((256, D), BF),
    ((8, D), F32),
    ((256, D), BF),
)


def front(*args):
    return pl.pallas_call(
        front_kernel,
        out_shape=tuple(shape(*a) for a in FRONT_KEPT)
        + (
            shape((8, 8, 128), jnp.int32),
            shape((2, 4, 4, 96, D), BF),
            shape((1, 4, 96, D), BF),
        ),
        in_specs=[VM] * 2 + [pl.BlockSpec(memory_space=pltpu.SMEM)] + [ANY] * 3 + [VM] * 2 + [ANY] * 5 + [VM] * 4,
        out_specs=(ANY,) * 16,
        scratch_shapes=[pltpu.VMEM(*a) for a in FRONT_KEPT]
        + [
            pltpu.VMEM((576, D), BF),
            pltpu.VMEM((256, D), BF),
            pltpu.VMEM((192, 1000), BF),
            pltpu.VMEM((4, 2, D, D), BF),
            pltpu.VMEM((D, D), BF),
            pltpu.VMEM((192, 8192), BF),
            pltpu.VMEM((256, 2048), BF),
            pltpu.VMEM((4, 128, 384), BF),
            pltpu.VMEM((4, 4, 128, 384), BF),
            pltpu.VMEM((16, 256), BF),
            pltpu.VMEM((4, 16, 256), BF),
            pltpu.VMEM((192, L), BF),
            pltpu.VMEM((L, 768), F32),
            pltpu.VMEM((L, 768), BF),
            pltpu.VMEM((192, 256), F32),
            pltpu.VMEM((4, 128, 384), BF),
            pltpu.VMEM((4, 128, 384), BF),
            pltpu.VMEM((256, D), BF),
            pltpu.VMEM((256, D), F32),
            pltpu.VMEM((256, D), BF),
            pltpu.VMEM((D, 256), BF),
            pltpu.VMEM((D, 256), BF),
            pltpu.VMEM((256, D), BF),
            pltpu.VMEM((256, D), F32),
            pltpu.VMEM((256, D), F32),
            pltpu.VMEM((2, 2, 4, 2, 96, D), BF),
            pltpu.VMEM((4, 2, 4, 96, D), BF),
            pltpu.VMEM((2, 2, 4, 96, D), BF),
            pltpu.VMEM((1, 4, 2, 96, D), BF),
            pltpu.VMEM((1, 4, 96, D), BF),
            pltpu.VMEM((1, 4, 96, D), BF),
            DMA((2, 3, 4)),
            DMA((2, 3, 4)),
            DMA((3,)),
            DMA((3,)),
            DMA((7,)),
            DMA((7,)),
            DMA((2, 3, 3)),
            DMA((2, 3, 3)),
            DMA((2, 3, 3, 8)),
            DMA((2, 3, 3, 8)),
            DMA((4,)),
            DMA((4,)),
            DMA((8,)),
            DMA((4,)),
            DMA((4,)),
            DMA,
            DMA,
            DMA((2,)),
            DMA((13,)),
        ],
        compiler_params=params(0),
        name="front",
    )(*args)

def norm_stats(x):
    centered = x - jnp.mean(x, axis=1, keepdims=True)
    scale = lax.rsqrt(jnp.mean(centered * centered, axis=1, keepdims=True) + EPS)
    return centered * scale, scale


def norm_back(grad, gain, hat, scale):
    t = grad * gain
    return scale * (t - jnp.mean(t, axis=1, keepdims=True) - hat * jnp.mean(t * hat, axis=1, keepdims=True))


def rows_sum(x):
    return jnp.sum(x, axis=0, keepdims=True)


class Line:
    def __init__(self, me, acc, up, down, sems):
        self.me, self.acc, self.up, self.down = me, acc, up, down
        self.us, self.ur, self.ds, self.dr = (sems.at[i] for i in range(4))

    def send(self, q, d):
        if d == 0:
            return push(self.acc(q), self.up.at[q], self.us.at[q], self.ur.at[q], self.me.z(1))
        return push(self.acc(q), self.down.at[q], self.ds.at[q], self.dr.at[q], self.me.z(3))

    def end(self, q, d):
        @pl.when(self.me.j == (0 if d == 0 else 3))
        def _():
            self.send(q, d).start()

    def inner(self, steps):
        for q, d, j in steps:

            @pl.when(self.me.j == j)
            def _():
                c = self.send(q, d)
                c.wait_recv()
                ref = self.acc(q)
                ref[...] = ref[...] + (self.up if d == 0 else self.down)[q]
                c.start()

    def finish(self, out):
        j = self.me.j
        for q in range(4):

            @pl.when(j == q)
            def _():
                total = self.acc(q)[...].astype(F32)
                if q > 0:
                    self.send(q, 0).wait_recv()
                    total = total + self.up[q].astype(F32)
                if q < 3:
                    self.send(q, 1).wait_recv()
                    total = total + self.down[q].astype(F32)
                out[...] = total

    def close(self):
        j = self.me.j
        for q in range(4):

            @pl.when(j < q)
            def _():
                self.send(q, 0).wait_send()

            @pl.when(j > q)
            def _():
                self.send(q, 1).wait_send()


class Halved:
    def __init__(self, me, acc, up, down, sems, parts):
        self.parts = parts
        self.lines = [
            Line(me, lambda q, r=r: acc(q).at[r], up.at[:, r], down.at[:, r], sems.at[i]) for i, r in enumerate(parts)
        ]

    def end(self, q, d):
        for line in self.lines:
            line.end(q, d)

    def first(self):
        for q, d in ((3, 0), (0, 1), (2, 0), (1, 1), (1, 0), (2, 1)):
            self.end(q, d)

    def inner(self, steps):
        for line in self.lines:
            line.inner(steps)

    def finish(self, out):
        for line, r in zip(self.lines, self.parts):
            line.finish(out.at[r])

    def close(self):
        for line in self.lines:
            line.close()


NEAR = ((3, 0, 1), (0, 1, 2))
FAR = ((3, 0, 2), (0, 1, 1), (2, 0, 1), (1, 1, 2))


class Unit:
    def __init__(self, me, src, acc, rc, rx, ry, rx2, ry2, sems, lsem):
        self.me, self.src, self.acc = me, src, acc
        self.rc, self.rx, self.ry, self.rx2, self.ry2 = rc, rx, ry, rx2, ry2
        self.s, self.r, self.lsem = sems.at[0], sems.at[1], lsem
        self.nq = acc.shape[0]

    def copies(self, stage):
        me, acc, s, r = self.me, self.acc, self.s, self.r
        lo, hi = pl.ds(0, 48), pl.ds(48, 48)
        if stage == 0:
            return [push(self.src.at[:, :, 1 - me.core], self.rc, s.at[0], r.at[0], me.at(me.pc))]
        if stage == 1:
            return [
                push(acc.at[:, me.md, lo], self.rx.at[:, 1], s.at[1], r.at[1], me.at(me.px)),
                push(acc.at[:, me.md, hi], self.ry.at[:, 1], s.at[2], r.at[2], me.at(me.py)),
                push(acc.at[:, me.mx, lo], self.rx.at[:, 0], s.at[3], r.at[3], me.at(me.px)),
                push(acc.at[:, me.my, hi], self.ry.at[:, 0], s.at[4], r.at[4], me.at(me.py)),
            ]
        return [
            push(acc.at[:, me.my, lo], self.ry2, s.at[5], r.at[5], me.at(me.py)),
            push(acc.at[:, me.mx, hi], self.rx2, s.at[6], r.at[6], me.at(me.px)),
        ]

    def load(self):
        src = self.src if self.rc is None else self.src.at[:, :, self.me.core]
        return pltpu.make_async_copy(src, self.acc, self.lsem)

    def begin(self):
        self.load().start()
        if self.rc is not None:
            self.copies(0)[0].start()

    def chip(self):
        self.load().wait()
        if self.rc is None:
            return
        self.copies(0)[0].wait_recv()

        @pl.loop(0, self.nq)
        def _(q):
            for m in range(4):
                self.acc[q, m] = self.acc[q, m] + self.rc[q, m]

    def cross(self):
        for c in self.copies(1):
            c.start()

    def turn(self):
        me = self.me
        first = self.copies(1)
        for c in first[:2]:
            c.wait()
        second = self.copies(2)

        @pl.loop(0, self.nq)
        def _(q):
            self.acc[q, me.my, 0:48] = self.acc[q, me.my, 0:48] + self.rx[q, 1]
            self.acc[q, me.mx, 48:96] = self.acc[q, me.mx, 48:96] + self.ry[q, 1]

        for c in second:
            c.start()
        for c in first[2:]:
            c.wait()

        @pl.loop(0, self.nq)
        def _(q):
            self.acc[q, me.m, 0:48] = self.acc[q, me.m, 0:48] + self.rx[q, 0]
            self.acc[q, me.m, 48:96] = self.acc[q, me.m, 48:96] + self.ry[q, 0]

    def settle(self):
        me = self.me
        for c in self.copies(2):
            c.wait()

        @pl.loop(0, self.nq)
        def _(q):
            self.acc[q, me.m, 0:48] = self.acc[q, me.m, 0:48] + self.ry2[q]
            self.acc[q, me.m, 48:96] = self.acc[q, me.m, 48:96] + self.rx2[q]

        if self.rc is not None:
            self.copies(0)[0].wait_send()

    def own(self, q):
        return self.acc.at[q, self.me.m]


SHAPES = ((4, 768), (4, 768), (1, 768), (1, 640))


def back_kernel(
    h_gatt, h_qm, h_k, h_v, h_kt, h_lse, h_n1, h_wq, h_x, h_gmid, h_segc, h_segr, h_vec, h_ids, dw, dwo, g1, step,
    h_in, h_tok, h_up, h_down, h_out, h_qkv, h_sp,
    gatt, qm, k, v, kt, lse, n1, wq, x, gmid, segc, segr, vec, IDS, gs, *scratch,
):
    me = Place()
    p, j = me.p, me.j
    pairs = (
        (h_gatt, gatt), (h_k, k), (h_qm, qm), (h_v, v), (h_segc, segc), (h_segr, segr), (h_lse, lse), (h_kt, kt),
        (h_n1, n1), (h_wq, wq), (h_x, x), (h_gmid, gmid), (h_vec, vec), (h_ids, IDS),
    )
    loads = [pltpu.make_async_copy(src, dst, gs.at[i]) for i, (src, dst) in enumerate(pairs)]
    for c in loads[:8]:
        c.start()
    meet([me.z(1), me.z(2), me.z(3)] + [me.at((p + i) % 8) for i in range(1, 8)])
    it = iter(scratch)
    take = lambda n: [next(it) for _ in range(n)]
    sendb, gbuf, dom, s, dp, pb, dsb, dqt, dqn, dk, dv, gn = take(12)
    o_in, o_tok, o_up, o_down, o_out, o_qkv, o_sp, hs = take(8)
    as_, ar = take(2)
    gacc, gup, gdown, gsem = take(4)
    qk, tb, X, hot, vbuf, SZ, vs, wz = take(8)
    vzs, vzr, ts, tr, ps, pr, vps, vpr, ls = take(9)
    sources = (dw.at[1], dw.at[0], dwo, qk)
    units, lines = [], []
    for i, src in enumerate(sources):
        acc, rx, ry, rx2, ry2, sems, lsem = take(7)
        rc = take(1)[0] if i == 3 else None
        unit = Unit(me, src, acc, rc, rx, ry, rx2, ry2, sems, lsem)
        units.append(unit)
        if i < 3:
            up, down, sem = take(3)
            block = unit.own if i < 2 else lambda q: wz.at[q]
            lines.append(Halved(me, block, up, down, sem, [pl.ds(0, 48), pl.ds(48, 48)]))
    own = Halved(me, lambda q: gacc.at[q], gup, gdown, gsem, [pl.ds(0, 128), pl.ds(128, 128)])
    homes = [
        pltpu.make_async_copy(src, dst, hs.at[i])
        for i, (src, dst) in enumerate(
            ((o_in, h_in), (o_tok, h_tok), (o_up, h_up), (o_down, h_down), (o_out, h_out), (o_qkv, h_qkv), (o_sp, h_sp))
        )
    ]

    def to_heads(d):
        return push(sendb.at[d], gbuf.at[j], as_.at[d], ar.at[j], (p, d))

    loads[0].wait()
    for d in range(4):
        sendb[d] = fold(gatt[:, 192 * d : 192 * d + 192])

    for i in (3, 2, 1):
        to_heads((j + i) % 4).start()
    gbuf[j] = sendb[j]
    for i in (0, 2, 1):
        units[i].begin()
    for c in loads[8:]:
        c.start()
    dk[...] = jnp.zeros_like(dk)
    dv[...] = jnp.zeros_like(dv)

    units[0].chip()
    units[0].cross()
    units[2].chip()
    units[2].cross()
    units[1].chip()
    def step3():
        units[0].turn()

    steps = {11: step3}

    def slot(i, n):
        for c, fn in {c: fn for c, fn in steps.items() if c % 3 == n}.items():
            pl.when(i == c // 3)(fn)

    for c in loads[1:8]:
        c.wait()

    @pl.loop(0, 4)
    def _(i):
        b = (j + i) % 4
        sq = segr[0:1, lanes(b)]

        @pl.when(i > 0)
        def _():
            push(gbuf.at[b], gbuf.at[b], as_.at[b], ar.at[b], me.z(1)).wait_recv()

        do = unfold(gbuf[b]).astype(F32)
        for h in range(3):
            dom[h] = (do * head_mask(192, h)).astype(BF)
        s[...] = contract_cols(k[...], qm[:, lanes(b), :].reshape(768, 192))
        dp[...] = contract_cols(v[...], dom[...].reshape(768, 192))
        slot(i, 0)
        ls_ = [lse[3 * b + h] for h in range(3)]
        inner = [jnp.zeros((8, 256), F32)] * 3
        for c in range(L // CH):
            rows = slice(CH * c, CH * c + CH)
            ok = allowed(segc, sq, b, c)
            for h in range(3):
                part = slice(256 * h, 256 * h + 256)
                e = jnp.exp(jnp.where(ok, s[rows, part], -1e30) - ls_[h])
                s[rows, part] = e
                pb[rows, part] = e.astype(BF)
                inner[h] = inner[h] + jnp.sum(groups(e * dp[rows, part]), axis=0)
        inner = [jnp.sum(a, axis=0, keepdims=True) for a in inner]
        slot(i, 1)
        for c in range(L // CH):
            rows = slice(CH * c, CH * c + CH)
            for h in range(3):
                part = slice(256 * h, 256 * h + 256)
                dsb[rows, part] = (s[rows, part] * (dp[rows, part] - inner[h])).astype(BF)
        dv[...] += dot(pb[...], dom[...].reshape(768, 192))
        dk[...] += dot(dsb[...], qm[:, lanes(b), :].reshape(768, 192))
        summed = dot(kt[...], dsb[...])
        for h in range(3):
            part = slice(64 * h, 64 * h + 64)
            dqt[part, lanes(b)] = summed[part, 256 * h : 256 * h + 256] * 0.125
        slot(i, 2)

    for c in loads[8:]:
        c.wait()
    for q, starts in ((3, ((3, 0),)), (0, ((0, 1),)), (2, ((2, 0),)), (1, ((1, 1), (1, 0), (2, 1)))):
        rows = slice(256 * q, 256 * q + 256)
        dq = dqt[:, rows].T.astype(BF)
        dqn[rows, :] = dq
        total = dot(dq, wq[0:192, :]) + dot(dk[rows, :].astype(BF), wq[192:384, :])
        gacc[q] = (total + dot(dv[rows, :].astype(BF), wq[384:576, :])).astype(BF)
        for block, d in starts:
            own.end(block, d)
    units[2].turn()
    units[1].cross()
    for i, grad in enumerate((dqn[...], dk[...].astype(BF), dv[...].astype(BF))):
        full = contract_rows(n1[...], grad).astype(BF)
        for piece in range(8):
            qk[0, piece // 2, piece % 2, :, 192 * i : 192 * i + 192] = full[96 * piece : 96 * piece + 96, :]
    for piece in range(8):
        qk[0, piece // 2, piece % 2, :, 576:640] = jnp.zeros((96, 64), BF)
    units[3].begin()
    own.inner(NEAR)
    units[3].chip()
    units[3].cross()
    units[0].settle()
    lines[0].first()
    own.inner(FAR)
    units[2].settle()
    for q in range(4):
        wz[q, :, 0:192] = units[2].acc[0, me.m, :, 192 * q : 192 * q + 192]
        wz[q, :, 192:256] = jnp.zeros((96, 64), BF)
    units[1].turn()
    units[3].turn()
    def to_columns(d, half):
        return push(tb.at[d, half], X.at[p, j, half], ts.at[d, half], tr.at[j, half], (p, d))

    sums = [jnp.zeros((1, D), F32)] * 3

    def norm_half(half):
        rows = slice(128 * half, 128 * half + 128)
        own.lines[half].finish(gn.at[own.parts[half]])
        hat, scale = norm_stats(x[rows, :])
        grad = gn[rows, :]
        dx = gmid[rows, :] + norm_back(grad, line_of(g1), hat, scale)
        o_in[rows, :] = dx
        dxb = dx.astype(BF)
        for d in range(4):
            tb[d, half] = fold(dxb[:, 192 * d : 192 * d + 192])
        for i in (2, 1, 3):
            to_columns((j + i) % 4, half).start()
        X[p, j, half] = tb[j, half]
        for n, v in enumerate((grad * hat, grad, dx)):
            sums[n] = sums[n] + rows_sum(v)

    def hop(ref, i, dev):
        return push(ref, ref, ps.at[i], pr.at[i], me.at(dev))

    def table(d, start=False):
        vocab = 1024 * p + lax.broadcasted_iota(jnp.int32, (1024, 128), 0)
        for g in range(8):
            hot[:, 128 * g : 128 * g + 128] = (vocab == IDS[d, g : g + 1, :]).astype(F32).astype(BF)
        rows = jnp.concatenate([unfold(X[d, q, i]) for q in range(4) for i in range(2)], axis=0)
        part = dot(hot[...], rows)
        if start:
            o_tok[...] = part
        else:
            o_tok[...] += part

    sent = []
    here = me.pc - p

    def spread(i, half):
        q = quarter_at(j, i)
        ref = X.at[p, q, half]
        if i > 0:
            push(ref, ref, ts.at[q, half], tr.at[q, half], me.z(1)).wait_recv()
        for c in (hop(ref, 4 * q + 2 * half, me.px), hop(ref, 4 * q + 2 * half + 1, me.py)):
            c.start()
            sent.append(c)

    def on_x(q, half):
        return hop(X.at[me.py, q, half], 16 + 2 * q + half, me.px)

    def on_y(q, half):
        return hop(X.at[me.px, q, half], 16 + 2 * q + half, me.py)

    def corner(i, half):
        q = quarter_at(j, i)
        hop(X.at[me.px, q, half], 4 * q + 2 * half, me.px).wait_recv()
        hop(X.at[me.py, q, half], 4 * q + 2 * half + 1, me.py).wait_recv()

        @pl.when(q < 2)
        def _():
            on_x(q, half).start()

        @pl.when(q >= 2)
        def _():
            on_y(q, half).start()

    def to_core(d, i):
        c = hop(X.at[d], i, me.pc)
        c.start()
        sent.append(c)

    norm_half(0)
    spread(0, 0)
    norm_half(1)
    homes[0].start()
    vbuf[...] = vec[...]
    vbuf[0:1, :] = sums[0]
    vbuf[1:2, :] = sums[1]
    vbuf[6:7, :] = sums[2]
    first = jnp.where(j == 0, step[0], 0).astype(F32)
    vbuf[7:8, :] = jnp.full((1, D), 1.0, F32) * first
    small = [push(vbuf, SZ.at[j], vzs.at[i - 1], vzr.at[i - 1], me.z(i)) for i in (1, 2, 3)]
    for c in small:
        c.start()
    SZ[j] = vbuf[...]
    spread(0, 1)
    lines[0].inner(NEAR)
    units[1].settle()
    lines[1].first()
    spread(1, 0)
    spread(2, 0)
    spread(1, 1)
    spread(2, 1)
    lines[2].first()
    corner(0, 0)
    corner(0, 1)
    for c in small:
        c.wait()
    vs[...] = SZ[0] + SZ[1] + SZ[2] + SZ[3]
    out_v = [push(vs, o_sp.at[p], vps.at[i - 1], vpr.at[i - 1], me.at((p + i) % 8)) for i in range(1, 8)]
    for c in out_v:
        c.start()
    o_sp[p] = vs[...]
    lines[0].inner(FAR)
    spread(3, 0)
    spread(3, 1)
    to_core(p, 24)
    corner(1, 0)
    corner(2, 0)
    corner(1, 1)
    corner(2, 1)
    table(p, start=True)
    lines[1].inner(NEAR)
    corner(3, 0)
    corner(3, 1)
    to_core(me.px, 25)
    to_core(me.py, 26)
    units[3].settle()
    lines[2].inner(NEAR)
    hop(X.at[me.pc], 24, me.pc).wait_recv()
    table(me.pc)
    lines[1].inner(FAR)
    table(me.px)
    for q in range(4):
        for half in range(2):
            hop(X.at[me.pd, q, half], 16 + 2 * q + half, me.px).wait_recv()
    to_core(me.pd, 27)
    lines[2].inner(FAR)
    table(me.py)
    table(me.pd)
    hop(X.at[me.px + here], 25, me.pc).wait_recv()
    table(me.px + here)
    hop(X.at[me.py + here], 26, me.pc).wait_recv()
    table(me.py + here)
    hop(X.at[me.pd + here], 27, me.pc).wait_recv()
    table(me.pd + here)
    homes[1].start()
    lines[0].finish(o_down)
    homes[3].start()
    lines[2].finish(o_out)
    homes[4].start()
    lines[1].finish(o_up)
    homes[2].start()
    o_qkv[...] = units[3].acc[0, me.m].astype(F32)
    homes[5].start()
    for c in out_v:
        c.wait()
    homes[6].start()
    for c in homes:
        c.wait()
    for c in sent:
        c.wait_send()
    for q in range(4):
        for half in range(2):
            on_x(q, half).wait_send() if q < 2 else on_y(q, half).wait_send()
    for d in range(4):

        @pl.when(j != d)
        def _():
            to_heads(d).wait_send()
            to_columns(d, 0).wait_send()
            to_columns(d, 1).wait_send()

    for line in lines + [own]:
        line.close()


BACK_KEPT = (
    ((256, D), BF),
    ((3, L, 192), BF),
    ((L, 192), BF),
    ((L, 192), BF),
    ((192, L), BF),
    ((12, 1, 256), F32),
    ((L, D), BF),
    ((576, D), BF),
    ((256, D), F32),
    ((256, D), F32),
    ((L, 1), F32),
    ((1, L), F32),
    ((8, D), F32),
    ((8, 8, 128), jnp.int32),
)


def back(*args):
    scratch = [pltpu.VMEM(*a) for a in BACK_KEPT] + [
        DMA((14,)),
        pltpu.VMEM((4, 128, 384), BF),
        pltpu.VMEM((4, 128, 384), BF),
        pltpu.VMEM((3, 256, 192), BF),
        pltpu.VMEM((L, 768), F32),
        pltpu.VMEM((L, 768), F32),
        pltpu.VMEM((L, 768), BF),
        pltpu.VMEM((L, 768), BF),
        pltpu.VMEM((192, L), F32),
        pltpu.VMEM((L, 192), BF),
        pltpu.VMEM((L, 192), F32),
        pltpu.VMEM((L, 192), F32),
        pltpu.VMEM((256, D), F32),
        pltpu.VMEM((256, D), F32),
        pltpu.VMEM((1024, 192), F32),
        pltpu.VMEM((96, D), F32),
        pltpu.VMEM((96, D), F32),
        pltpu.VMEM((96, 256), F32),
        pltpu.VMEM((96, 640), F32),
        pltpu.VMEM((8, 8, D), F32),
        DMA((7,)),
        DMA((4,)),
        DMA((4,)),
        pltpu.VMEM((4, 256, D), BF),
        pltpu.VMEM((4, 256, D), BF),
        pltpu.VMEM((4, 256, D), BF),
        DMA((2, 4, 4)),
        pltpu.VMEM((1, 4, 2, 96, 640), BF),
        pltpu.VMEM((4, 2, 64, 384), BF),
        pltpu.VMEM((8, 4, 2, 64, 384), BF),
        pltpu.VMEM((1024, 1024), BF),
        pltpu.VMEM((8, D), F32),
        pltpu.VMEM((4, 8, D), F32),
        pltpu.VMEM((8, D), F32),
        pltpu.VMEM((4, 96, 256), BF),
        DMA((3,)),
        DMA((3,)),
        DMA((4, 2)),
        DMA((4, 2)),
        DMA((28,)),
        DMA((28,)),
        DMA((7,)),
        DMA((7,)),
        DMA((2,)),
    ]
    for i, (nq, w) in enumerate(SHAPES):
        scratch += [
            pltpu.VMEM((nq, 4, 96, w), BF),
            pltpu.VMEM((nq, 2, 48, w), BF),
            pltpu.VMEM((nq, 2, 48, w), BF),
            pltpu.VMEM((nq, 48, w), BF),
            pltpu.VMEM((nq, 48, w), BF),
            DMA((2, 7)),
            DMA,
        ]
        if i == 3:
            scratch += [pltpu.VMEM((nq, 4, 96, w), BF)]
        else:
            wide = w if i < 2 else 256
            scratch += [pltpu.VMEM((4, 96, wide), BF), pltpu.VMEM((4, 96, wide), BF), DMA((2, 4, 4))]
    return pl.pallas_call(
        back_kernel,
        out_shape=(
            shape((256, D), F32),
            shape((1024, 192), F32),
            shape((96, D), F32),
            shape((96, D), F32),
            shape((96, 256), F32),
            shape((96, 640), F32),
            shape((8, 8, D), F32),
        ),
        in_specs=[ANY] * 16 + [VM, pl.BlockSpec(memory_space=pltpu.SMEM)],
        out_specs=(ANY,) * 7,
        scratch_shapes=scratch,
        compiler_params=params(1),
        name="back",
    )(*args)


def tail_kernel(sp, din, tok, up, down, wout, qkv, *outs):
    o_time, o_din, o_tok, o_up, o_down, o_out, o_qkv = outs[:7]
    i = pl.program_id(0)
    row = (200 * i + lax.broadcasted_iota(jnp.int32, (200, D), 0)).astype(F32)
    total = jnp.zeros((200, D), F32)
    for d in range(8):
        total = total + jnp.where(row == sp[d, 7:8, :], sp[d, 6:7, :], 0.0)
    o_time[...] = total

    @pl.when(i == 0)
    def _():
        sums = sp[0]
        for d in range(1, 8):
            sums = sums + sp[d]
        for n, ref in enumerate(outs[7:]):
            ref[...] = sums[n : n + 1, :].reshape(D)
        o_din[...] = din[...]
        o_tok[...] = tok[...].T
        o_up[...] = up[...]
        o_down[...] = down[...]
        o_out[...] = wout[...].T[0:192, :]
        for n in range(3):
            o_qkv[n] = qkv[:, 192 * n : 192 * n + 192]


def tail(*args):
    whole = lambda a: pl.BlockSpec(a.shape, lambda i: (0,) * len(a.shape))
    outs = (
        shape((256, D), F32),
        shape((192, 1024), F32),
        shape((96, D), F32),
        shape((96, D), F32),
        shape((192, 96), F32),
        shape((3, 96, 192), F32),
    ) + (shape((D,), F32),) * 6
    return pl.pallas_call(
        tail_kernel,
        grid=(5,),
        out_shape=(shape((1000, D), F32),) + outs,
        in_specs=[whole(a) for a in args],
        out_specs=(pl.BlockSpec((200, D), lambda i: (i, 0)),) + tuple(whole(a) for a in outs),
        compiler_params=pltpu.CompilerParams(vmem_limit_bytes=63 << 20, dimension_semantics=("arbitrary",)),
        name="tail",
    )(*args)


class Native:
    def __init__(self, ndp, nmp):
        self.ndp, self.nmp = ndp, nmp

    def gather_all(self, emb, trow, ids, w2, wo):
        over_mp = lambda a: lax.all_gather(a, "mp", axis=0, tiled=False)
        return (
            over_mp(emb),
            over_mp(trow),
            lax.all_gather(ids, "dp", axis=0, tiled=False),
            over_mp(w2),
            over_mp(wo),
        )

    def exchange(self, x, cid, name):
        return lax.all_to_all(x, "mp", split_axis=0, concat_axis=0, tiled=True)

    def reduce_all(self, gn, dw, dwo, dqkv):
        sum_mp = lambda a: lax.psum_scatter(a.astype(F32), "mp", scatter_dimension=0, tiled=True)
        sum_dp = lambda a: lax.psum_scatter(a, "dp", scatter_dimension=0, tiled=True)
        flat = lambda a: a.reshape(D, a.shape[-1])
        return (
            sum_mp(gn).reshape(gn.shape[1:]),
            sum_dp(flat(sum_mp(dw[0]))),
            sum_dp(flat(sum_mp(dw[1]))),
            sum_dp(flat(sum_mp(dwo[..., : D // self.nmp]))),
            sum_dp(flat(dqkv[..., : 3 * D // self.nmp].astype(F32))),
        )

    def final_exchange(self, tp, vec):
        x = lax.all_to_all(tp, "mp", split_axis=0, concat_axis=0, tiled=True)
        return (
            lax.all_gather(x, "dp", axis=0, tiled=False),
            lax.all_gather(lax.psum(vec, "mp"), "dp", axis=0, tiled=False),
        )


def layer_norm(stream, gain, shift):
    average = jnp.mean(stream, axis=-1, keepdims=True)
    centered = stream - average
    variance = jnp.mean(centered * centered, axis=-1, keepdims=True)
    return centered * lax.rsqrt(variance + 1e-05) * gain + shift


def allowed_pairs(seg_query, segments, first_row):
    key_pos = jnp.arange(L)
    query_pos = first_row + jnp.arange(QBLK)
    same_text = seg_query[:, None] == segments[None, :]
    self_or_text = (seg_query[:, None] != 0) | (query_pos[:, None] == key_pos[None, :])
    return same_text & self_or_text


def attend_forward(queries, key_rows, value_rows, segments):
    outputs = []
    log_parts = []
    for block_index in range(L // QBLK):
        first_row = block_index * QBLK
        query_block = queries[first_row : first_row + QBLK]
        allowed = allowed_pairs(segments[first_row : first_row + QBLK], segments, first_row)
        scores = jnp.einsum("qhd,khd->hqk", query_block, key_rows, preferred_element_type=F32) * 0.125
        masked = jnp.where(allowed[None], scores, -1e30)
        highest = jnp.max(masked, axis=-1, keepdims=True)
        exponents = jnp.exp(masked - highest)
        totals = jnp.sum(exponents, axis=-1, keepdims=True)
        weights = (exponents / totals).astype(BF)
        outputs.append(jnp.einsum("hqk,khd->qhd", weights, value_rows, preferred_element_type=F32).astype(BF))
        log_parts.append((highest + jnp.log(totals))[..., 0])
    return (jnp.concatenate(outputs, axis=0), jnp.concatenate(log_parts, axis=1))


def attend_backward(queries, key_rows, value_rows, segments, log_sums, grad_heads):
    grad_keys = jnp.zeros(key_rows.shape, F32)
    grad_values = jnp.zeros(value_rows.shape, F32)
    grad_queries = []
    for block_index in range(L // QBLK):
        first_row = block_index * QBLK
        query_block = queries[first_row : first_row + QBLK]
        grad_block = grad_heads[first_row : first_row + QBLK]
        allowed = allowed_pairs(segments[first_row : first_row + QBLK], segments, first_row)
        scores = jnp.einsum("qhd,khd->hqk", query_block, key_rows, preferred_element_type=F32) * 0.125
        masked = jnp.where(allowed[None], scores, -1e30)
        probs = jnp.exp(masked - log_sums[:, first_row : first_row + QBLK, None])
        rounded = probs.astype(BF)
        grad_probs = jnp.einsum("qhd,khd->hqk", grad_block, value_rows, preferred_element_type=F32)
        inner = jnp.sum(probs * grad_probs, axis=-1, keepdims=True)
        grad_scores = (probs * (grad_probs - inner)).astype(BF)
        grad_queries.append(
            jnp.einsum("hqk,khd->qhd", grad_scores, key_rows, preferred_element_type=F32) * 0.125
        )
        grad_keys = (
            grad_keys
            + jnp.einsum("hqk,qhd->khd", grad_scores, query_block, preferred_element_type=F32) * 0.125
        )
        grad_values = grad_values + jnp.einsum("hqk,qhd->khd", rounded, grad_block, preferred_element_type=F32)
    return (
        jnp.concatenate(grad_queries, axis=0).astype(BF),
        grad_keys.astype(BF),
        grad_values.astype(BF),
    )


def on_device_native(
    comm,
    token_ids,
    segment_ids,
    timesteps,
    token_table,
    time_table,
    ln1_gain,
    ln1_bias,
    w_qkv,
    w_out,
    attn_bias,
    ln2_gain,
    ln2_bias,
    w_up,
    w_down,
    mlp_bias,
    cotangent,
):
    group = lax.axis_size("mp")
    ndp = lax.axis_size("dp")
    member = lax.axis_index("mp")
    own_rows = L // group
    width = token_table.shape[1]
    heads_local = width // HD

    emb = fold(token_table[token_ids])
    time_row = lax.dynamic_slice_in_dim(time_table, timesteps[0], 1, 0)
    trow = jnp.broadcast_to(jnp.pad(time_row, ((0, 0), (0, 256 - width))), (16, 256))
    ids = token_ids.reshape(8, 128)
    w2 = jnp.stack((w_up, w_down))
    wo = w_out.reshape(width, 6, 128).transpose(1, 0, 2).reshape(6 * width, 128)
    E, TR, IDS, W2, WO = comm.gather_all(emb, trow, ids, w2, wo)

    time_full = TR[:, 0, :width].reshape(1, D).astype(F32)
    tokens = unfold(E).transpose(1, 0, 2).reshape(L, D)
    stream_all = tokens.astype(F32) + time_full
    stream_in = lax.dynamic_slice_in_dim(stream_all, member * own_rows, own_rows, 0)
    normed_one = layer_norm(stream_all, ln1_gain, ln1_bias).astype(BF)
    wq = w_qkv.transpose(1, 2, 0).reshape(3 * width, D)
    packed = contract_cols(normed_one, wq).astype(BF).reshape(L, 3, heads_local, HD)
    queries, key_rows, value_rows = packed[:, 0], packed[:, 1], packed[:, 2]
    attended, log_sums = attend_forward(queries, key_rows, value_rows, segment_ids)
    sent = fold(attended.reshape(group, own_rows, width))
    got = comm.exchange(sent, 1, "to_rows")

    att_own = unfold(got).transpose(1, 0, 2).reshape(own_rows, D)
    w_out_full = WO.reshape(group, 6, width, 128).transpose(0, 2, 1, 3).reshape(D, D)
    stream_mid = stream_in + dot(att_own, w_out_full) + attn_bias
    normed_two = layer_norm(stream_mid, ln2_gain, ln2_bias).astype(BF)
    own_segments = lax.dynamic_slice_in_dim(segment_ids, member * own_rows, own_rows, 0)
    grad_out = cotangent.astype(F32) * (own_segments != 0).astype(F32)[:, None]
    grad_mlp = grad_out.astype(BF)
    out = stream_mid + mlp_bias
    grad_norm_two = jnp.zeros((own_rows, D), F32)
    grads_up, grads_down = [], []
    for q in range(group):
        pre = dot(normed_two, W2[q, 0])
        act, back = jax.vjp(lambda v: jax.nn.gelu(v, approximate=True), pre)
        act = act.astype(BF)
        out = out + dot(act, W2[q, 1])
        grad_pre = back(contract_cols(grad_mlp, W2[q, 1]))[0].astype(BF)
        grad_norm_two = grad_norm_two + contract_cols(grad_pre, W2[q, 0])
        grads_up.append(contract_rows(normed_two, grad_pre).astype(BF))
        grads_down.append(contract_rows(grad_mlp, act).astype(BF))
    dw = jnp.stack((jnp.stack(grads_up), jnp.stack(grads_down)))
    norm_back_two = jax.vjp(layer_norm, stream_mid, ln2_gain, ln2_bias)[1]
    grad_mid_norm, grad_ln2_gain, grad_ln2_bias = norm_back_two(grad_norm_two)
    grad_mid = grad_out + grad_mid_norm
    grad_attn = grad_mid.astype(BF)
    dwo = contract_rows(grad_attn, att_own).astype(BF).reshape(D, group, width).transpose(1, 0, 2)
    dwo = jnp.pad(dwo, ((0, 0), (0, 0), (0, 256 - width)))
    grad_attended = contract_cols(grad_attn, w_out_full).astype(BF)
    sent = fold(grad_attended.reshape(own_rows, group, width).transpose(1, 0, 2))
    got = comm.exchange(sent, 2, "to_heads")

    grad_heads = unfold(got).reshape(L, heads_local, HD)
    grad_q, grad_k, grad_v = attend_backward(
        queries, key_rows, value_rows, segment_ids, log_sums, grad_heads
    )
    grad_packed = jnp.stack((grad_q, grad_k, grad_v), axis=1).reshape(L, 3 * width)
    dqkv = jnp.pad(contract_rows(normed_one, grad_packed).astype(BF), ((0, 0), (0, 640 - 3 * width)))
    gn = dot(grad_packed, wq).astype(BF).reshape(group, own_rows, D)

    pieces = lambda a: a.reshape(a.shape[:-2] + (ndp // 2, 2, D // ndp, a.shape[-1]))
    grad_norm_one, g_up, g_down, g_out, g_qkv = comm.reduce_all(
        gn, pieces(dw), pieces(dwo), pieces(dqkv)[None]
    )
    norm_back_one = jax.vjp(layer_norm, stream_in, ln1_gain, ln1_bias)[1]
    grad_in_norm, grad_ln1_gain, grad_ln1_bias = norm_back_one(grad_norm_one)
    input_grad = grad_mid + grad_in_norm
    tp = fold(input_grad.astype(BF).reshape(own_rows, group, width).transpose(1, 0, 2))
    step_row = jnp.where(member == 0, timesteps[0], 0).astype(F32)
    vec = jnp.stack(
        (
            grad_ln1_gain,
            grad_ln1_bias,
            jnp.sum(grad_mid, axis=0),
            grad_ln2_gain,
            grad_ln2_bias,
            jnp.sum(grad_out, axis=0),
            jnp.sum(input_grad, axis=0),
            jnp.broadcast_to(step_row, (D,)),
        )
    )
    X, SP = comm.final_exchange(tp, vec)
    rows_table = token_table.shape[0] // ndp
    columns = unfold(X).reshape(ndp * L, width)
    first = lax.axis_index("dp") * rows_table
    hot = (first + jnp.arange(rows_table))[:, None] == IDS.reshape(1, ndp * L)
    grad_token_table = dot(hot.astype(BF), columns)
    steps = SP[:, 7, 0].astype(jnp.int32)
    grad_time_table = jnp.zeros(time_table.shape[:1] + (D,), F32)
    at_row = jnp.arange(time_table.shape[0])[:, None]
    if ndp <= 8:
        for i in range(ndp):
            grad_time_table = grad_time_table + jnp.where(at_row == steps[i], SP[i, 6][None], 0.0)
    else:
        grad_time_table = grad_time_table.at[steps].add(SP[:, 6])
    sums = jnp.sum(SP[:, :6], axis=0)
    return (
        out.astype(BF),
        input_grad,
        grad_token_table,
        grad_time_table,
        sums[0],
        sums[1],
        g_qkv[:, : 3 * width].reshape(-1, 3, width),
        g_out[:, :width].T,
        sums[2],
        sums[3],
        sums[4],
        g_up,
        g_down.T,
        sums[5],
    )


def on_device_tuned(
    token_ids, segment_ids, timesteps, token_table, time_table, ln1_gain, ln1_bias, w_qkv, w_out, attn_bias,
    ln2_gain, ln2_bias, w_up, w_down, mlp_bias, cotangent,
):
    width = 192
    ids8 = token_ids.reshape(8, 128)
    wq = w_qkv.transpose(1, 2, 0).reshape(3 * width, D)
    qm, k, v, kt, normed_one, stream_in, lse, segr, segc, grad_mid, grad_attended, vec, out, IDS, dw, dwo = front(
        token_ids, segment_ids, timesteps, ids8, token_table.T, time_table.T, ln1_gain, ln1_bias, wq, w_up, w_down, w_out,
        cotangent, attn_bias, ln2_gain, ln2_bias, mlp_bias,
    )
    input_grad, grad_token_table, g_up, g_down, g_out, g_qkv, SP = back(
        grad_attended, qm, k, v, kt, lse, normed_one, wq, stream_in, grad_mid, segc, segr, vec, IDS, dw, dwo, ln1_gain,
        timesteps,
    )
    o_time, o_in, o_tok, o_up, o_down, o_out, o_qkv, *sums = tail(
        SP, input_grad, grad_token_table, g_up, g_down, g_out, g_qkv
    )
    return (
        out, o_in, o_tok.T, o_time, sums[0], sums[1], o_qkv.transpose(1, 0, 2), o_out, sums[2], sums[3], sums[4],
        o_up, o_down.T, sums[5],
    )


def solution(mesh):
    placed = (
        P("dp"),
        P("dp"),
        P("dp"),
        P(None, "mp"),
        P(None, "mp"),
        P(),
        P(),
        P(None, None, "mp"),
        P("mp", None),
        P(),
        P(),
        P(),
        P(None, "mp"),
        P("mp", None),
        P(),
        P(("dp", "mp"), None),
    )
    ndp, nmp = mesh.shape["dp"], mesh.shape["mp"]
    return jax.shard_map(
        on_device_tuned if (ndp, nmp) == (8, 4) else functools.partial(on_device_native, Native(ndp, nmp)),
        mesh=mesh,
        in_specs=placed,
        out_specs=(
            P(("dp", "mp"), None),
            P(("dp", "mp"), None),
            P("dp", "mp"),
            P(),
            P(),
            P(),
            P("dp", None, "mp"),
            P("mp", "dp"),
            P(),
            P(),
            P(),
            P("dp", "mp"),
            P("mp", "dp"),
            P(),
        ),
        check_vma=False,
    )
```

```python
import functools

import jax
import jax.numpy as jnp
from jax import lax
from jax.experimental import pallas as pl
from jax.experimental.pallas import tpu as pltpu
from jax.sharding import PartitionSpec as P

D = 768
HD = 64
L = 1024
QBLK = 512
BF = jnp.bfloat16
F32 = jnp.float32
MESH = pl.DeviceIdType.MESH
ANY = pl.BlockSpec(memory_space=pl.ANY)
VM = pl.BlockSpec(memory_space=pltpu.VMEM)
DMA = pltpu.SemaphoreType.DMA
EPS = 1e-05


def shape(dims, dtype):
    return jax.ShapeDtypeStruct(dims, dtype)


def dot(a, b):
    return jnp.dot(a, b, preferred_element_type=F32)


def contract_rows(left, right):
    return lax.dot_general(left, right, (((0,), (0,)), ((), ())), preferred_element_type=F32)


def contract_cols(left, right):
    return lax.dot_general(left, right, (((1,), (1,)), ((), ())), preferred_element_type=F32)


class Place:
    def __init__(self):
        self.p = p = lax.axis_index("dp")
        self.j = lax.axis_index("mp")
        core, x, y = p % 2, (p // 2) % 2, p // 4
        self.core, self.m = core, p // 2
        self.px = p + 2 - 4 * x
        self.py = p + 4 - 8 * y
        self.pd = self.px + 4 - 8 * y
        self.pc = p + 1 - 2 * core
        self.mx = self.px // 2
        self.my = self.py // 2
        self.md = self.pd // 2

    def z(self, hop):
        return (self.p, (self.j + hop) % 4)

    def at(self, dp):
        return (dp, self.j)


def meet(devices):
    barrier = pltpu.get_barrier_semaphore()
    for device in devices:
        pl.semaphore_signal(barrier, inc=1, device_id=device, device_id_type=MESH)
    pl.semaphore_wait(barrier, len(devices))


def push(src, dst, send, recv, device):
    return pltpu.make_async_remote_copy(
        src_ref=src, dst_ref=dst, send_sem=send, recv_sem=recv, device_id=device, device_id_type=MESH
    )


def params(cid):
    return pltpu.CompilerParams(collective_id=cid, has_side_effects=True, vmem_limit_bytes=60 << 20)


def head_mask(width, h):
    lane = lax.broadcasted_iota(jnp.int32, (1, width), 1)
    return ((lane >= HD * h) & (lane < HD * h + HD)).astype(F32)


def fold(rows):
    half = rows.shape[-2] // 2
    return jnp.concatenate((rows[..., :half, :], rows[..., half:, :]), axis=-1)


def unfold(packed):
    width = packed.shape[-1] // 2
    return jnp.concatenate((packed[..., :width], packed[..., width:]), axis=-2)


CH = 32


def line_of(ref):
    return ref[...].reshape(1, ref.shape[0])


def across(row):
    return jnp.broadcast_to(row, (128, row.shape[1])).T


def allowed(segc, sq, b, c):
    key = CH * c + lax.broadcasted_iota(jnp.int32, (CH, 256), 0)
    query = 256 * b + lax.broadcasted_iota(jnp.int32, (CH, 256), 1)
    return ((segc[CH * c : CH * c + CH, :] == sq) & (sq != 0.0)) | (key == query)


def lanes(b):
    return pl.ds(pl.multiple_of(256 * b, 256), 256)


def groups(x):
    return x.reshape(CH // 8, 8, 256)


def write_segments(seg, segr, segc):
    row = line_of(seg).astype(F32)
    segr[...] = row
    for i in range(8):
        segc[128 * i : 128 * i + 128, :] = across(row[:, 128 * i : 128 * i + 128])[:, 0:1]


class Weights:
    def __init__(self, me, W2, WO, zs, zr, ps, pr):
        self.me, self.W2, self.WO = me, W2, WO
        self.zs, self.zr, self.ps, self.pr = zs, zr, ps, pr

    def zpart(self, a, q, piece):
        if a < 2:
            return self.W2.at[q, a, pl.ds(96 * piece, 96), :]
        return self.WO.at[pl.ds(192 * q + 48 * (piece // 2), 48), pl.ds(384 * (piece % 2), 384)]

    def part(self, a, q, piece, half=None):
        if a < 2:
            lo, n = (0, 96) if half is None else (48 * half, 48)
            return self.W2.at[q, a, pl.ds(96 * piece + lo, n), :]
        lo, n = (0, 48) if half is None else ((0, 32), (32, 16))[half]
        return self.WO.at[pl.ds(192 * q + 48 * (piece // 2) + lo, n), pl.ds(384 * (piece % 2), 384)]

    def quarter(self, d, k):
        j = self.me.j
        return (j - k + 4) % 4 if d == 0 else (j + k) % 4

    def sends(self, d, k):
        j = self.me.j
        return (j < 3) & (j >= k) if d == 0 else (j > 0) & (j + k <= 3)

    def gets(self, d, k):
        j = self.me.j
        return j >= k + 1 if d == 0 else j + k + 1 <= 3

    def zcopy(self, d, k, a):
        p, q = self.me.p, self.quarter(d, k)
        part = self.zpart(a, q, p)
        return push(part, part, self.zs.at[d, k, a], self.zr.at[d, k, a], self.me.z(1 if d == 0 else 3))

    def zgot(self, d, k, a):
        dst = self.zpart(a, self.quarter(d, k + 1), self.me.p)
        return push(dst, dst, self.zs.at[d, k, a], self.zr.at[d, k, a], self.me.z(1))

    def zstart(self, k, arrays):
        for d in (0, 1):

            @pl.when(self.sends(d, k))
            def _():
                for a in arrays:
                    self.zcopy(d, k, a).start()

    def spread(self, k, a):
        self.zwait(k, (a,))
        self.pstart(k, 0, (a,))

    def turn(self, k, a):
        self.pwait(k, 0, (0, 1), (a,))
        self.pstart(k, 1, (a,))

    def last(self, k, a):
        self.pwait(k, 1, (0, 1), (a,))
        self.pstart(k, 2, (a,))

    def zown(self, k):
        for d in (0, 1):
            last = self.me.j == (k if d == 0 else 3 - k)

            @pl.when(self.sends(d, 0) & last)
            def _():
                self.zcopy(d, 0, 1).start()

    def zwait(self, k, arrays):
        for d in (0, 1):

            @pl.when(self.gets(d, k))
            def _():
                for a in arrays:
                    self.zgot(d, k, a).wait_recv()

    def routes(self, d, k, a, stage):
        me, q = self.me, self.quarter(d, k + 1)
        if stage == 0:
            return [(self.part(a, q, me.p), me.px), (self.part(a, q, me.p), me.py), (self.part(a, q, me.p), me.pc)]
        if stage == 1:
            return [
                (self.part(a, q, me.py, 0), me.px),
                (self.part(a, q, me.px, 1), me.py),
                (self.part(a, q, me.px), me.pc),
                (self.part(a, q, me.py), me.pc),
            ]
        return [(self.part(a, q, me.pd), me.pc)]

    def arrivals(self, d, k, a, stage):
        me, q = self.me, self.quarter(d, k + 1)
        c = me.pc - me.p
        if stage == 0:
            return [self.part(a, q, me.px), self.part(a, q, me.py), self.part(a, q, me.pc)]
        if stage == 1:
            return [
                self.part(a, q, me.pd, 0),
                self.part(a, q, me.pd, 1),
                self.part(a, q, me.px + c),
                self.part(a, q, me.py + c),
            ]
        return [self.part(a, q, me.pd + c)]

    def pstart(self, k, stage, arrays):
        for d in (0, 1):

            @pl.when(self.gets(d, k))
            def _():
                for a in arrays:
                    for i, (ref, dp) in enumerate(self.routes(d, k, a, stage)):
                        s = 3 * stage + i if stage < 2 else 7
                        push(ref, ref, self.ps.at[d, k, a, s], self.pr.at[d, k, a, s], self.me.at(dp)).start()

    def pwait(self, k, stage, which, arrays, send=False):
        for d in (0, 1):

            @pl.when(self.gets(d, k))
            def _():
                for a in arrays:
                    self.one(d, k, stage, which, a, send)

    def one(self, d, k, stage, which, a, send=False):
        if send:
            refs = [r for r, _ in self.routes(d, k, a, stage)]
        else:
            refs = self.arrivals(d, k, a, stage)
        for i in which:
            s = 3 * stage + i if stage < 2 else 7
            c = push(refs[i], refs[i], self.ps.at[d, k, a, s], self.pr.at[d, k, a, s], self.me.at(self.me.pc))
            c.wait_send() if send else c.wait_recv()

    def rest(self, step):
        for d, k, devices in NEEDS[step]:
            here = self.me.j == devices[0]
            for other in devices[1:]:
                here = here | (self.me.j == other)

            @pl.when(here)
            def _():
                for a in (0, 1):
                    self.one(d, k, 0, (2,), a)
                    self.one(d, k, 1, (2, 3), a)
                    self.one(d, k, 2, (0,), a)

    def out_rest(self):
        for k in range(3):
            self.pwait(k, 0, (2,), (2,))
            self.pwait(k, 1, (2, 3), (2,))
            self.pwait(k, 2, (0,), (2,))

    def finish(self):
        for k in range(3):
            self.pwait(k, 0, (0, 1, 2), (0, 1, 2), send=True)
            self.pwait(k, 1, (0, 1, 2, 3), (0, 1, 2), send=True)
            self.pwait(k, 2, (0,), (0, 1, 2), send=True)
            for d in (0, 1):

                @pl.when(self.sends(d, k))
                def _():
                    for a in (0, 1, 2):
                        self.zcopy(d, k, a).wait_send()


NEEDS = {
    1: ((0, 0, (1, 2, 3)), (1, 0, (0,))),
    2: ((1, 1, (0,)), (1, 0, (1, 2)), (0, 1, (3,))),
    3: ((1, 2, (0,)), (1, 1, (1,)), (0, 1, (2,)), (0, 2, (3,))),
}
ORDER = ((0, 1, 2, 3), (1, 0, 2, 3), (2, 1, 3, 0), (3, 2, 1, 0))


def quarter_at(j, i):
    total = 0
    for n in range(4):
        for m in range(4):
            total = total + ORDER[n][m] * ((j == n) & (i == m)).astype(jnp.int32)
    return total


def front_kernel(
    ids, seg, step, ids8, tabt, h_timet, g1, b1, h_wq, w_up, w_down, w_out, h_cot, pa, pg, pb2, pm,
    h_qm, h_k, h_v, h_kt, h_n1, h_x, h_lse, h_segr, h_segc, h_gmid, h_gatt, h_vec, h_out, IDS, dw_o, dwo_o,
    qm_o, k_o, v_o, kt_o, n1_o, x_o, lse_o, segr, segc, gmid_o, gatt_o, vec_o, out_o, wq, cot, timet,
    W2, WO, tab, hot, eb, E, tb, TR, vt, s, pb, ot, sendb, attg,
    att, hat, n2, n2t, gmt, gm, acc, gn2, stage, rc, accb, wst, wrc, wacc,
    es, er, ts, tr, is_, ir, zs, zr, ps, pr, as_, ar, ls, cs, cr, ws, wr, hs, os,
):
    me = Place()
    p, j = me.p, me.j
    fetch = pltpu.make_async_copy(tabt, tab, ls.at[0])
    fetch_time = pltpu.make_async_copy(h_timet, timet, ls.at[1])
    later = [pltpu.make_async_copy(h_wq, wq, ls.at[6]), pltpu.make_async_copy(h_cot, cot, ls.at[7])]
    fetch_time.start()
    fetch.start()
    pairs = (
        (qm_o, h_qm), (k_o, h_k), (v_o, h_v), (kt_o, h_kt), (n1_o, h_n1), (x_o, h_x), (lse_o, h_lse), (segr, h_segr),
        (segc, h_segc), (gmid_o, h_gmid), (gatt_o, h_gatt), (vec_o, h_vec), (out_o, h_out),
    )
    homes = [pltpu.make_async_copy(src, dst, os.at[i]) for i, (src, dst) in enumerate(pairs)]
    load = [
        pltpu.make_async_copy(w_up, W2.at[j, 0], ls.at[3]),
        pltpu.make_async_copy(w_down, W2.at[j, 1], ls.at[4]),
        pltpu.make_async_copy(w_out, WO.at[pl.ds(192 * j, 192), :], ls.at[5]),
    ]
    for c in load:
        c.start()
    for c in later:
        c.start()
    write_segments(seg, segr, segc)
    homes[7].start()
    homes[8].start()
    fetch_time.wait()
    lane = lax.broadcasted_iota(jnp.int32, (192, 1000), 1)
    column = jnp.sum(jnp.where(lane == step[0], timet[...].astype(F32), 0.0), axis=1, keepdims=True)
    tb[:, 0:192] = jnp.broadcast_to(column, (192, 128)).T[0:16, :].astype(BF)
    meet([me.z(1), me.z(2), me.z(3)] + [me.at((p + k) % 8) for k in range(1, 8)])
    w = Weights(me, W2, WO, zs, zr, ps, pr)

    def ecopy(d, k, c):
        q = w.quarter(d, k)
        dev = me.z(1 if d == 0 else 3)
        return push(eb.at[c] if k == 0 else E.at[q, c], E.at[q, c], es.at[d, k, c], er.at[d, k, c], dev)

    def estart(k, c):
        for d in (0, 1):

            @pl.when(w.sends(d, k))
            def _():
                ecopy(d, k, c).start()

    def ewait(k, c):
        for d in (0, 1):

            @pl.when(w.gets(d, k))
            def _():
                dst = E.at[w.quarter(d, k + 1), c]
                push(dst, dst, es.at[d, k, c], er.at[d, k, c], me.z(1)).wait_recv()

    here = [pltpu.make_async_copy(ids8, IDS.at[p], ls.at[2])]
    small = [push(tb, TR.at[j], ts.at[k - 1], tr.at[k - 1], me.z(k)) for k in (1, 2, 3)]
    small_ids = [push(ids8, IDS.at[p], is_.at[k - 1], ir.at[k - 1], me.at((p + k) % 8)) for k in range(1, 8)]
    ids_row = line_of(ids).astype(F32)

    def embed(c):
        token = across(ids_row[:, 256 * c : 256 * c + 256])
        s[0:256, 0:192] = jnp.zeros((256, 192), F32)

        @pl.loop(0, 4)
        def _(v):
            base = (2048 * v).astype(F32)
            for i in range(16):
                word = lax.broadcasted_iota(jnp.int32, (256, 128), 1).astype(F32) + (base + 128.0 * i)
                hot[:, 128 * i : 128 * i + 128] = (token == word).astype(F32).astype(BF)
            s[0:256, 0:192] += contract_cols(hot[...], tab[:, pl.ds(pl.multiple_of(2048 * v, 2048), 2048)])

        eb[c] = fold(s[0:256, 0:192].astype(BF))
        estart(0, c)

    fetch.wait()
    for c in load:
        c.wait()
    w.zstart(0, (2, 0))
    embed(0)
    for c in small + here + small_ids:
        c.start()
    embed(1)
    w.spread(0, 2)
    w.zstart(1, (2,))
    embed(2)
    ewait(0, 0)
    estart(1, 0)
    w.spread(0, 0)
    embed(3)
    w.zown(0)
    ewait(0, 1)
    estart(1, 1)
    w.spread(1, 2)
    w.zstart(2, (2,))
    ewait(0, 2)
    estart(1, 2)
    ewait(1, 0)
    estart(2, 0)
    ewait(0, 3)
    estart(1, 3)
    w.zown(1)
    ewait(1, 1)
    estart(2, 1)
    w.spread(2, 2)
    ewait(1, 2)
    estart(2, 2)
    for c in small:
        c.wait()
    E[j] = eb[...]
    TR[j] = tb[...]
    for c in later:
        c.wait()
    time_row = jnp.concatenate([TR[q].astype(F32)[0:1, 0:192] for q in range(4)], axis=1)
    gain, shift = line_of(g1), line_of(b1)

    def norm_qkv(r):
        rows = slice(256 * r, 256 * r + 256)
        x = jnp.concatenate([unfold(E[q, r]) for q in range(4)], axis=1)
        x = x.astype(F32) + time_row
        centered = x - jnp.mean(x, axis=1, keepdims=True)
        variance = jnp.mean(centered * centered, axis=1, keepdims=True)
        normed = (centered * lax.rsqrt(variance + EPS) * gain + shift).astype(BF)
        n1_o[rows, :] = normed

        @pl.when(j == r)
        def _():
            x_o[...] = x

        q = contract_cols(normed, wq[0:192, :]).astype(BF).astype(F32) * 0.125
        for i in range(3):
            qm_o[i, rows, :] = (q * head_mask(192, i)).astype(BF)
        k_o[rows, :] = contract_cols(normed, wq[192:384, :]).astype(BF)
        v_o[rows, :] = contract_cols(normed, wq[384:576, :]).astype(BF)
        kt_o[:, rows] = contract_cols(wq[192:384, :], normed).astype(BF)
        vt[:, rows] = contract_cols(wq[384:576, :], normed).astype(BF)

    ewait(1, 3)
    estart(2, 3)
    w.zown(2)
    w.zstart(1, (0,))
    ewait(2, 0)
    norm_qkv(0)
    for k in range(3):
        w.turn(k, 2)
    w.turn(0, 0)
    ewait(2, 1)
    norm_qkv(1)
    for k in range(3):
        w.last(k, 2)
    w.last(0, 0)
    ewait(2, 2)
    norm_qkv(2)
    ewait(2, 3)
    norm_qkv(3)
    for c in homes[:6]:
        c.start()
    w.spread(0, 1)
    w.zstart(1, (1,))

    def att_copy(b):
        return push(sendb.at[b], attg.at[j], as_.at[b], ar.at[j], (p, b))

    def step0():
        w.spread(1, 0)
        w.zstart(2, (0,))

    def step1():
        w.turn(0, 1)

    def step2():
        w.spread(1, 1)
        w.zstart(2, (1,))

    def step3():
        w.turn(1, 0)
        w.last(0, 1)

    def step4():
        w.spread(2, 0)

    def step5():
        w.turn(1, 1)
        w.last(1, 0)

    steps = {1: step0, 3: step1, 4: step2, 6: step3, 9: step5, 11: step4}

    def slot(i, n):
        for k, step in {k: v for k, v in steps.items() if k % 3 == n}.items():
            pl.when(i == k // 3)(step)

    @pl.loop(0, 4)
    def _(i):
        b = (j + 1 + i) % 4
        sq = segr[0:1, lanes(b)]
        s[...] = contract_cols(k_o[...], qm_o[:, lanes(b), :].reshape(768, 192))
        slot(i, 0)
        top = [jnp.full((8, 256), -jnp.inf, F32)] * 3
        for c in range(L // CH):
            rows = slice(CH * c, CH * c + CH)
            ok = allowed(segc, sq, b, c)
            for h in range(3):
                part = slice(256 * h, 256 * h + 256)
                x = jnp.where(ok, s[rows, part], -1e30)
                s[rows, part] = x
                top[h] = jnp.maximum(top[h], jnp.max(groups(x), axis=0))
        top = [jnp.max(m, axis=0, keepdims=True) for m in top]
        slot(i, 1)
        total = [jnp.zeros((8, 256), F32)] * 3
        for c in range(L // CH):
            rows = slice(CH * c, CH * c + CH)
            for h in range(3):
                part = slice(256 * h, 256 * h + 256)
                e = jnp.exp(s[rows, part] - top[h])
                pb[rows, part] = e.astype(BF)
                total[h] = total[h] + jnp.sum(groups(e), axis=0)
        summed = dot(vt[...], pb[...])
        for h in range(3):
            t = jnp.sum(total[h], axis=0, keepdims=True)
            lse_o[3 * b + h] = top[h] + jnp.log(t)
            part = slice(64 * h, 64 * h + 64)
            ot[part, :] = summed[part, 256 * h : 256 * h + 256] * (1.0 / t)
        sendb[b] = fold(ot[...].T.astype(BF))

        @pl.when(b != j)
        def _():
            att_copy(b).start()

        slot(i, 2)

    homes[6].start()
    attg[j] = sendb[j]
    valid = across((segr[:, lanes(j)] != 0.0).astype(F32))[:, 0:1]
    gmid_o[...] = cot[...].astype(F32) * valid
    gm[...] = gmid_o[...].astype(BF)
    gmt[...] = gmid_o[...].T.astype(BF)
    gn2[...] = jnp.zeros_like(gn2)
    vec_o[...] = jnp.zeros_like(vec_o)
    vec_o[5:6, :] = rows_sum(gmid_o[...])
    w.out_rest()
    for q in range(4):

        @pl.when(j != q)
        def _():
            push(attg.at[q], attg.at[q], as_.at[q], ar.at[q], me.z(1)).wait_recv()

    w.last(1, 1)
    att[...] = jnp.concatenate([unfold(attg[q]) for q in range(4)], axis=1)
    mid = x_o[...] + dot(att[...], WO[...]) + line_of(pa)
    h0, scale = norm_stats(mid)
    hat[...] = h0
    normed = h0 * line_of(pg) + line_of(pb2)
    n2[...] = normed.astype(BF)
    n2t[...] = normed.T.astype(BF)
    acc[...] = mid + line_of(pm)

    def to_sibling(i):
        return push(stage.at[i % 2, :, :, 1 - me.core], rc.at[i], cs.at[i], cr.at[i], me.at(me.pc))

    def save(i):
        return pltpu.make_async_copy(accb.at[i % 2], dw_o.at[:, quarter_at(j, i)], hs.at[i % 2])

    def chip(i):
        to_sibling(i).wait_recv()
        for u in range(2):
            for m in range(4):
                accb[i % 2, u, m] = stage[i % 2, u, m, me.core] + rc[i, u, m]
        save(i).start()

    def pump1():
        w.rest(1)
        w.turn(2, 0)
        w.spread(2, 1)

    def pump2():
        w.rest(2)
        w.last(2, 0)

    def pump3():
        w.last(2, 1)
        w.rest(3)

    @pl.loop(0, 4)
    def _(i):
        q = quarter_at(j, i)
        pl.when(i == 1)(pump1)
        pl.when(i == 2)(pump2)
        pl.when(i == 3)(pump3)
        pre = dot(n2[...], W2[q, 0])
        c = 0.7978845608028654
        t = jnp.tanh(c * (pre + 0.044715 * pre * pre * pre))
        act = (0.5 * pre * (1.0 + t)).astype(BF)
        slope = 0.5 * (1.0 + t) + 0.5 * pre * (1.0 - t * t) * (c * (1.0 + 3 * 0.044715 * pre * pre))
        acc[...] += dot(act, W2[q, 1])
        grad_pre = (contract_cols(gm[...], W2[q, 1]) * slope).astype(BF)
        gn2[...] += contract_cols(grad_pre, W2[q, 0])
        pl.when(i == 2)(functools.partial(w.turn, 2, 1))

        @pl.when(i >= 2)
        def _():
            to_sibling(i - 2).wait_send()
            save(i - 2).wait()

        for u, full in ((0, dot(n2t[...], grad_pre)), (1, dot(gmt[...], act))):
            for n in range(8):
                stage[i % 2, u, n // 2, n % 2] = full[96 * n : 96 * n + 96, :].astype(BF)
        to_sibling(i).start()

        @pl.when(i >= 1)
        def _():
            chip(i - 1)

    grad = gmid_o[...]
    gn, h0 = gn2[...], hat[...]
    vec_o[3:4, :] = rows_sum(gn * h0)
    vec_o[4:5, :] = rows_sum(gn)
    gmid = grad + norm_back(gn, line_of(pg), h0, scale)
    gmid_o[...] = gmid
    vec_o[2:3, :] = rows_sum(gmid)
    gatt_o[...] = contract_cols(gmid.astype(BF), WO[...]).astype(BF)
    for c in homes[9:12]:
        c.start()
    out_o[...] = acc[...].astype(BF)
    homes[12].start()
    full = dot(gmid.T.astype(BF), att[...]).astype(BF)
    for n in range(8):
        wst[0, n // 2, n % 2] = full[96 * n : 96 * n + 96, :]
    wo_copy = push(wst.at[:, :, 1 - me.core], wrc, ws, wr, me.at(me.pc))
    wo_copy.start()
    save(2).wait()
    chip(3)
    wo_copy.wait_recv()
    for m in range(4):
        wacc[0, m] = wst[0, m, me.core] + wrc[0, m]
    wsave = pltpu.make_async_copy(wacc, dwo_o, hs.at[0])
    to_sibling(2).wait_send()
    to_sibling(3).wait_send()
    wo_copy.wait_send()
    wsave.start()
    for b in range(4):

        @pl.when(j != b)
        def _():
            att_copy(b).wait_send()

    for k in range(3):
        for d in (0, 1):

            @pl.when(w.sends(d, k))
            def _():
                for c in range(4):
                    ecopy(d, k, c).wait_send()

    w.finish()
    for c in small_ids + here:
        c.wait()
    save(3).wait()
    wsave.wait()
    for c in homes:
        c.wait()


FRONT_KEPT = (
    ((3, L, 192), BF),
    ((L, 192), BF),
    ((L, 192), BF),
    ((192, L), BF),
    ((L, D), BF),
    ((256, D), F32),
    ((12, 1, 256), F32),
    ((1, L), F32),
    ((L, 1), F32),
    ((256, D), F32),
    ((256, D), BF),
    ((8, D), F32),
    ((256, D), BF),
)


def front(*args):
    return pl.pallas_call(
        front_kernel,
        out_shape=tuple(shape(*a) for a in FRONT_KEPT)
        + (
            shape((8, 8, 128), jnp.int32),
            shape((2, 4, 4, 96, D), BF),
            shape((1, 4, 96, D), BF),
        ),
        in_specs=[VM] * 2 + [pl.BlockSpec(memory_space=pltpu.SMEM)] + [ANY] * 3 + [VM] * 2 + [ANY] * 5 + [VM] * 4,
        out_specs=(ANY,) * 16,
        scratch_shapes=[pltpu.VMEM(*a) for a in FRONT_KEPT]
        + [
            pltpu.VMEM((576, D), BF),
            pltpu.VMEM((256, D), BF),
            pltpu.VMEM((192, 1000), BF),
            pltpu.VMEM((4, 2, D, D), BF),
            pltpu.VMEM((D, D), BF),
            pltpu.VMEM((192, 8192), BF),
            pltpu.VMEM((256, 2048), BF),
            pltpu.VMEM((4, 128, 384), BF),
            pltpu.VMEM((4, 4, 128, 384), BF),
            pltpu.VMEM((16, 256), BF),
            pltpu.VMEM((4, 16, 256), BF),
            pltpu.VMEM((192, L), BF),
            pltpu.VMEM((L, 768), F32),
            pltpu.VMEM((L, 768), BF),
            pltpu.VMEM((192, 256), F32),
            pltpu.VMEM((4, 128, 384), BF),
            pltpu.VMEM((4, 128, 384), BF),
            pltpu.VMEM((256, D), BF),
            pltpu.VMEM((256, D), F32),
            pltpu.VMEM((256, D), BF),
            pltpu.VMEM((D, 256), BF),
            pltpu.VMEM((D, 256), BF),
            pltpu.VMEM((256, D), BF),
            pltpu.VMEM((256, D), F32),
            pltpu.VMEM((256, D), F32),
            pltpu.VMEM((2, 2, 4, 2, 96, D), BF),
            pltpu.VMEM((4, 2, 4, 96, D), BF),
            pltpu.VMEM((2, 2, 4, 96, D), BF),
            pltpu.VMEM((1, 4, 2, 96, D), BF),
            pltpu.VMEM((1, 4, 96, D), BF),
            pltpu.VMEM((1, 4, 96, D), BF),
            DMA((2, 3, 4)),
            DMA((2, 3, 4)),
            DMA((3,)),
            DMA((3,)),
            DMA((7,)),
            DMA((7,)),
            DMA((2, 3, 3)),
            DMA((2, 3, 3)),
            DMA((2, 3, 3, 8)),
            DMA((2, 3, 3, 8)),
            DMA((4,)),
            DMA((4,)),
            DMA((8,)),
            DMA((4,)),
            DMA((4,)),
            DMA,
            DMA,
            DMA((2,)),
            DMA((13,)),
        ],
        compiler_params=params(0),
        name="front",
    )(*args)

def norm_stats(x):
    centered = x - jnp.mean(x, axis=1, keepdims=True)
    scale = lax.rsqrt(jnp.mean(centered * centered, axis=1, keepdims=True) + EPS)
    return centered * scale, scale


def norm_back(grad, gain, hat, scale):
    t = grad * gain
    return scale * (t - jnp.mean(t, axis=1, keepdims=True) - hat * jnp.mean(t * hat, axis=1, keepdims=True))


def rows_sum(x):
    return jnp.sum(x, axis=0, keepdims=True)


class Line:
    def __init__(self, me, acc, up, down, sems):
        self.me, self.acc, self.up, self.down = me, acc, up, down
        self.us, self.ur, self.ds, self.dr = (sems.at[i] for i in range(4))

    def send(self, q, d):
        if d == 0:
            return push(self.acc(q), self.up.at[q], self.us.at[q], self.ur.at[q], self.me.z(1))
        return push(self.acc(q), self.down.at[q], self.ds.at[q], self.dr.at[q], self.me.z(3))

    def end(self, q, d):
        @pl.when(self.me.j == (0 if d == 0 else 3))
        def _():
            self.send(q, d).start()

    def inner(self, steps):
        for q, d, j in steps:

            @pl.when(self.me.j == j)
            def _():
                c = self.send(q, d)
                c.wait_recv()
                ref = self.acc(q)
                ref[...] = ref[...] + (self.up if d == 0 else self.down)[q]
                c.start()

    def finish(self, out):
        j = self.me.j
        for q in range(4):

            @pl.when(j == q)
            def _():
                total = self.acc(q)[...].astype(F32)
                if q > 0:
                    self.send(q, 0).wait_recv()
                    total = total + self.up[q].astype(F32)
                if q < 3:
                    self.send(q, 1).wait_recv()
                    total = total + self.down[q].astype(F32)
                out[...] = total

    def close(self):
        j = self.me.j
        for q in range(4):

            @pl.when(j < q)
            def _():
                self.send(q, 0).wait_send()

            @pl.when(j > q)
            def _():
                self.send(q, 1).wait_send()


class Halved:
    def __init__(self, me, acc, up, down, sems, parts):
        self.parts = parts
        self.lines = [
            Line(me, lambda q, r=r: acc(q).at[r], up.at[:, r], down.at[:, r], sems.at[i]) for i, r in enumerate(parts)
        ]

    def end(self, q, d):
        for line in self.lines:
            line.end(q, d)

    def first(self):
        for q, d in ((3, 0), (0, 1), (2, 0), (1, 1), (1, 0), (2, 1)):
            self.end(q, d)

    def inner(self, steps):
        for line in self.lines:
            line.inner(steps)

    def finish(self, out):
        for line, r in zip(self.lines, self.parts):
            line.finish(out.at[r])

    def close(self):
        for line in self.lines:
            line.close()


NEAR = ((3, 0, 1), (0, 1, 2))
FAR = ((3, 0, 2), (0, 1, 1), (2, 0, 1), (1, 1, 2))


class Unit:
    def __init__(self, me, src, acc, rc, rx, ry, rx2, ry2, sems, lsem):
        self.me, self.src, self.acc = me, src, acc
        self.rc, self.rx, self.ry, self.rx2, self.ry2 = rc, rx, ry, rx2, ry2
        self.s, self.r, self.lsem = sems.at[0], sems.at[1], lsem
        self.nq = acc.shape[0]

    def copies(self, stage):
        me, acc, s, r = self.me, self.acc, self.s, self.r
        lo, hi = pl.ds(0, 48), pl.ds(48, 48)
        if stage == 0:
            return [push(self.src.at[:, :, 1 - me.core], self.rc, s.at[0], r.at[0], me.at(me.pc))]
        if stage == 1:
            return [
                push(acc.at[:, me.md, lo], self.rx.at[:, 1], s.at[1], r.at[1], me.at(me.px)),
                push(acc.at[:, me.md, hi], self.ry.at[:, 1], s.at[2], r.at[2], me.at(me.py)),
                push(acc.at[:, me.mx, lo], self.rx.at[:, 0], s.at[3], r.at[3], me.at(me.px)),
                push(acc.at[:, me.my, hi], self.ry.at[:, 0], s.at[4], r.at[4], me.at(me.py)),
            ]
        return [
            push(acc.at[:, me.my, lo], self.ry2, s.at[5], r.at[5], me.at(me.py)),
            push(acc.at[:, me.mx, hi], self.rx2, s.at[6], r.at[6], me.at(me.px)),
        ]

    def load(self):
        src = self.src if self.rc is None else self.src.at[:, :, self.me.core]
        return pltpu.make_async_copy(src, self.acc, self.lsem)

    def begin(self):
        self.load().start()
        if self.rc is not None:
            self.copies(0)[0].start()

    def chip(self):
        self.load().wait()
        if self.rc is None:
            return
        self.copies(0)[0].wait_recv()

        @pl.loop(0, self.nq)
        def _(q):
            for m in range(4):
                self.acc[q, m] = self.acc[q, m] + self.rc[q, m]

    def cross(self):
        for c in self.copies(1):
            c.start()

    def turn(self):
        me = self.me
        first = self.copies(1)
        for c in first[:2]:
            c.wait()
        second = self.copies(2)

        @pl.loop(0, self.nq)
        def _(q):
            self.acc[q, me.my, 0:48] = self.acc[q, me.my, 0:48] + self.rx[q, 1]
            self.acc[q, me.mx, 48:96] = self.acc[q, me.mx, 48:96] + self.ry[q, 1]

        for c in second:
            c.start()
        for c in first[2:]:
            c.wait()

        @pl.loop(0, self.nq)
        def _(q):
            self.acc[q, me.m, 0:48] = self.acc[q, me.m, 0:48] + self.rx[q, 0]
            self.acc[q, me.m, 48:96] = self.acc[q, me.m, 48:96] + self.ry[q, 0]

    def settle(self):
        me = self.me
        for c in self.copies(2):
            c.wait()

        @pl.loop(0, self.nq)
        def _(q):
            self.acc[q, me.m, 0:48] = self.acc[q, me.m, 0:48] + self.ry2[q]
            self.acc[q, me.m, 48:96] = self.acc[q, me.m, 48:96] + self.rx2[q]

        if self.rc is not None:
            self.copies(0)[0].wait_send()

    def own(self, q):
        return self.acc.at[q, self.me.m]


SHAPES = ((4, 768), (4, 768), (1, 768), (1, 640))


def back_kernel(
    h_gatt, h_qm, h_k, h_v, h_kt, h_lse, h_n1, h_wq, h_x, h_gmid, h_segc, h_segr, h_vec, h_ids, dw, dwo, g1, step,
    h_in, h_tok, h_up, h_down, h_out, h_qkv, h_sp,
    gatt, qm, k, v, kt, lse, n1, wq, x, gmid, segc, segr, vec, IDS, gs, *scratch,
):
    me = Place()
    p, j = me.p, me.j
    pairs = (
        (h_gatt, gatt), (h_k, k), (h_qm, qm), (h_v, v), (h_segc, segc), (h_segr, segr), (h_lse, lse), (h_kt, kt),
        (h_n1, n1), (h_wq, wq), (h_x, x), (h_gmid, gmid), (h_vec, vec), (h_ids, IDS),
    )
    loads = [pltpu.make_async_copy(src, dst, gs.at[i]) for i, (src, dst) in enumerate(pairs)]
    for c in loads[:8]:
        c.start()
    meet([me.z(1), me.z(2), me.z(3)] + [me.at((p + i) % 8) for i in range(1, 8)])
    it = iter(scratch)
    take = lambda n: [next(it) for _ in range(n)]
    sendb, gbuf, dom, s, dp, pb, dsb, dqt, dqn, dk, dv, gn = take(12)
    o_in, o_tok, o_up, o_down, o_out, o_qkv, o_sp, hs = take(8)
    as_, ar = take(2)
    gacc, gup, gdown, gsem = take(4)
    qk, tb, X, hot, vbuf, SZ, vs, wz = take(8)
    vzs, vzr, ts, tr, ps, pr, vps, vpr, ls = take(9)
    sources = (dw.at[1], dw.at[0], dwo, qk)
    units, lines = [], []
    for i, src in enumerate(sources):
        acc, rx, ry, rx2, ry2, sems, lsem = take(7)
        rc = take(1)[0] if i == 3 else None
        unit = Unit(me, src, acc, rc, rx, ry, rx2, ry2, sems, lsem)
        units.append(unit)
        if i < 3:
            up, down, sem = take(3)
            block = unit.own if i < 2 else lambda q: wz.at[q]
            lines.append(Halved(me, block, up, down, sem, [pl.ds(0, 48), pl.ds(48, 48)]))
    own = Halved(me, lambda q: gacc.at[q], gup, gdown, gsem, [pl.ds(0, 128), pl.ds(128, 128)])
    homes = [
        pltpu.make_async_copy(src, dst, hs.at[i])
        for i, (src, dst) in enumerate(
            ((o_in, h_in), (o_tok, h_tok), (o_up, h_up), (o_down, h_down), (o_out, h_out), (o_qkv, h_qkv), (o_sp, h_sp))
        )
    ]

    def to_heads(d):
        return push(sendb.at[d], gbuf.at[j], as_.at[d], ar.at[j], (p, d))

    loads[0].wait()
    for d in range(4):
        sendb[d] = fold(gatt[:, 192 * d : 192 * d + 192])

    for i in (3, 2, 1):
        to_heads((j + i) % 4).start()
    gbuf[j] = sendb[j]
    for i in (0, 2, 1):
        units[i].begin()
    for c in loads[8:]:
        c.start()
    dk[...] = jnp.zeros_like(dk)
    dv[...] = jnp.zeros_like(dv)

    units[0].chip()
    units[0].cross()
    units[2].chip()
    units[2].cross()
    units[1].chip()
    def step3():
        units[0].turn()

    steps = {11: step3}

    def slot(i, n):
        for c, fn in {c: fn for c, fn in steps.items() if c % 3 == n}.items():
            pl.when(i == c // 3)(fn)

    for c in loads[1:8]:
        c.wait()

    @pl.loop(0, 4)
    def _(i):
        b = (j + i) % 4
        sq = segr[0:1, lanes(b)]

        @pl.when(i > 0)
        def _():
            push(gbuf.at[b], gbuf.at[b], as_.at[b], ar.at[b], me.z(1)).wait_recv()

        do = unfold(gbuf[b]).astype(F32)
        for h in range(3):
            dom[h] = (do * head_mask(192, h)).astype(BF)
        s[...] = contract_cols(k[...], qm[:, lanes(b), :].reshape(768, 192))
        dp[...] = contract_cols(v[...], dom[...].reshape(768, 192))
        slot(i, 0)
        ls_ = [lse[3 * b + h] for h in range(3)]
        inner = [jnp.zeros((8, 256), F32)] * 3
        for c in range(L // CH):
            rows = slice(CH * c, CH * c + CH)
            ok = allowed(segc, sq, b, c)
            for h in range(3):
                part = slice(256 * h, 256 * h + 256)
                e = jnp.exp(jnp.where(ok, s[rows, part], -1e30) - ls_[h])
                s[rows, part] = e
                pb[rows, part] = e.astype(BF)
                inner[h] = inner[h] + jnp.sum(groups(e * dp[rows, part]), axis=0)
        inner = [jnp.sum(a, axis=0, keepdims=True) for a in inner]
        slot(i, 1)
        for c in range(L // CH):
            rows = slice(CH * c, CH * c + CH)
            for h in range(3):
                part = slice(256 * h, 256 * h + 256)
                dsb[rows, part] = (s[rows, part] * (dp[rows, part] - inner[h])).astype(BF)
        dv[...] += dot(pb[...], dom[...].reshape(768, 192))
        dk[...] += dot(dsb[...], qm[:, lanes(b), :].reshape(768, 192))
        summed = dot(kt[...], dsb[...])
        for h in range(3):
            part = slice(64 * h, 64 * h + 64)
            dqt[part, lanes(b)] = summed[part, 256 * h : 256 * h + 256] * 0.125
        slot(i, 2)

    for c in loads[8:]:
        c.wait()
    for q, starts in ((3, ((3, 0),)), (0, ((0, 1),)), (2, ((2, 0),)), (1, ((1, 1), (1, 0), (2, 1)))):
        rows = slice(256 * q, 256 * q + 256)
        dq = dqt[:, rows].T.astype(BF)
        dqn[rows, :] = dq
        total = dot(dq, wq[0:192, :]) + dot(dk[rows, :].astype(BF), wq[192:384, :])
        gacc[q] = (total + dot(dv[rows, :].astype(BF), wq[384:576, :])).astype(BF)
        for block, d in starts:
            own.end(block, d)
    units[2].turn()
    units[1].cross()
    for i, grad in enumerate((dqn[...], dk[...].astype(BF), dv[...].astype(BF))):
        full = contract_rows(n1[...], grad).astype(BF)
        for piece in range(8):
            qk[0, piece // 2, piece % 2, :, 192 * i : 192 * i + 192] = full[96 * piece : 96 * piece + 96, :]
    for piece in range(8):
        qk[0, piece // 2, piece % 2, :, 576:640] = jnp.zeros((96, 64), BF)
    units[3].begin()
    own.inner(NEAR)
    units[3].chip()
    units[3].cross()
    units[0].settle()
    lines[0].first()
    own.inner(FAR)
    units[2].settle()
    for q in range(4):
        wz[q, :, 0:192] = units[2].acc[0, me.m, :, 192 * q : 192 * q + 192]
        wz[q, :, 192:256] = jnp.zeros((96, 64), BF)
    units[1].turn()
    units[3].turn()
    def to_columns(d, half):
        return push(tb.at[d, half], X.at[p, j, half], ts.at[d, half], tr.at[j, half], (p, d))

    sums = [jnp.zeros((1, D), F32)] * 3

    def norm_half(half):
        rows = slice(128 * half, 128 * half + 128)
        own.lines[half].finish(gn.at[own.parts[half]])
        hat, scale = norm_stats(x[rows, :])
        grad = gn[rows, :]
        dx = gmid[rows, :] + norm_back(grad, line_of(g1), hat, scale)
        o_in[rows, :] = dx
        dxb = dx.astype(BF)
        for d in range(4):
            tb[d, half] = fold(dxb[:, 192 * d : 192 * d + 192])
        for i in (2, 1, 3):
            to_columns((j + i) % 4, half).start()
        X[p, j, half] = tb[j, half]
        for n, v in enumerate((grad * hat, grad, dx)):
            sums[n] = sums[n] + rows_sum(v)

    def hop(ref, i, dev):
        return push(ref, ref, ps.at[i], pr.at[i], me.at(dev))

    def table(d, start=False):
        vocab = 1024 * p + lax.broadcasted_iota(jnp.int32, (1024, 128), 0)
        for g in range(8):
            hot[:, 128 * g : 128 * g + 128] = (vocab == IDS[d, g : g + 1, :]).astype(F32).astype(BF)
        rows = jnp.concatenate([unfold(X[d, q, i]) for q in range(4) for i in range(2)], axis=0)
        part = dot(hot[...], rows)
        if start:
            o_tok[...] = part
        else:
            o_tok[...] += part

    sent = []
    here = me.pc - p

    def spread(i, half):
        q = quarter_at(j, i)
        ref = X.at[p, q, half]
        if i > 0:
            push(ref, ref, ts.at[q, half], tr.at[q, half], me.z(1)).wait_recv()
        for c in (hop(ref, 4 * q + 2 * half, me.px), hop(ref, 4 * q + 2 * half + 1, me.py)):
            c.start()
            sent.append(c)

    def on_x(q, half):
        return hop(X.at[me.py, q, half], 16 + 2 * q + half, me.px)

    def on_y(q, half):
        return hop(X.at[me.px, q, half], 16 + 2 * q + half, me.py)

    def corner(i, half):
        q = quarter_at(j, i)
        hop(X.at[me.px, q, half], 4 * q + 2 * half, me.px).wait_recv()
        hop(X.at[me.py, q, half], 4 * q + 2 * half + 1, me.py).wait_recv()

        @pl.when(q < 2)
        def _():
            on_x(q, half).start()

        @pl.when(q >= 2)
        def _():
            on_y(q, half).start()

    def to_core(d, i):
        c = hop(X.at[d], i, me.pc)
        c.start()
        sent.append(c)

    norm_half(0)
    spread(0, 0)
    norm_half(1)
    homes[0].start()
    vbuf[...] = vec[...]
    vbuf[0:1, :] = sums[0]
    vbuf[1:2, :] = sums[1]
    vbuf[6:7, :] = sums[2]
    first = jnp.where(j == 0, step[0], 0).astype(F32)
    vbuf[7:8, :] = jnp.full((1, D), 1.0, F32) * first
    small = [push(vbuf, SZ.at[j], vzs.at[i - 1], vzr.at[i - 1], me.z(i)) for i in (1, 2, 3)]
    for c in small:
        c.start()
    SZ[j] = vbuf[...]
    spread(0, 1)
    lines[0].inner(NEAR)
    units[1].settle()
    lines[1].first()
    spread(1, 0)
    spread(2, 0)
    spread(1, 1)
    spread(2, 1)
    lines[2].first()
    corner(0, 0)
    corner(0, 1)
    for c in small:
        c.wait()
    vs[...] = SZ[0] + SZ[1] + SZ[2] + SZ[3]
    out_v = [push(vs, o_sp.at[p], vps.at[i - 1], vpr.at[i - 1], me.at((p + i) % 8)) for i in range(1, 8)]
    for c in out_v:
        c.start()
    o_sp[p] = vs[...]
    lines[0].inner(FAR)
    spread(3, 0)
    spread(3, 1)
    to_core(p, 24)
    corner(1, 0)
    corner(2, 0)
    corner(1, 1)
    corner(2, 1)
    table(p, start=True)
    lines[1].inner(NEAR)
    corner(3, 0)
    corner(3, 1)
    to_core(me.px, 25)
    to_core(me.py, 26)
    units[3].settle()
    lines[2].inner(NEAR)
    hop(X.at[me.pc], 24, me.pc).wait_recv()
    table(me.pc)
    lines[1].inner(FAR)
    table(me.px)
    for q in range(4):
        for half in range(2):
            hop(X.at[me.pd, q, half], 16 + 2 * q + half, me.px).wait_recv()
    to_core(me.pd, 27)
    lines[2].inner(FAR)
    table(me.py)
    table(me.pd)
    hop(X.at[me.px + here], 25, me.pc).wait_recv()
    table(me.px + here)
    hop(X.at[me.py + here], 26, me.pc).wait_recv()
    table(me.py + here)
    hop(X.at[me.pd + here], 27, me.pc).wait_recv()
    table(me.pd + here)
    homes[1].start()
    lines[0].finish(o_down)
    homes[3].start()
    lines[2].finish(o_out)
    homes[4].start()
    lines[1].finish(o_up)
    homes[2].start()
    o_qkv[...] = units[3].acc[0, me.m].astype(F32)
    homes[5].start()
    for c in out_v:
        c.wait()
    homes[6].start()
    for c in homes:
        c.wait()
    for c in sent:
        c.wait_send()
    for q in range(4):
        for half in range(2):
            on_x(q, half).wait_send() if q < 2 else on_y(q, half).wait_send()
    for d in range(4):

        @pl.when(j != d)
        def _():
            to_heads(d).wait_send()
            to_columns(d, 0).wait_send()
            to_columns(d, 1).wait_send()

    for line in lines + [own]:
        line.close()


BACK_KEPT = (
    ((256, D), BF),
    ((3, L, 192), BF),
    ((L, 192), BF),
    ((L, 192), BF),
    ((192, L), BF),
    ((12, 1, 256), F32),
    ((L, D), BF),
    ((576, D), BF),
    ((256, D), F32),
    ((256, D), F32),
    ((L, 1), F32),
    ((1, L), F32),
    ((8, D), F32),
    ((8, 8, 128), jnp.int32),
)


def back(*args):
    scratch = [pltpu.VMEM(*a) for a in BACK_KEPT] + [
        DMA((14,)),
        pltpu.VMEM((4, 128, 384), BF),
        pltpu.VMEM((4, 128, 384), BF),
        pltpu.VMEM((3, 256, 192), BF),
        pltpu.VMEM((L, 768), F32),
        pltpu.VMEM((L, 768), F32),
        pltpu.VMEM((L, 768), BF),
        pltpu.VMEM((L, 768), BF),
        pltpu.VMEM((192, L), F32),
        pltpu.VMEM((L, 192), BF),
        pltpu.VMEM((L, 192), F32),
        pltpu.VMEM((L, 192), F32),
        pltpu.VMEM((256, D), F32),
        pltpu.VMEM((256, D), F32),
        pltpu.VMEM((1024, 192), F32),
        pltpu.VMEM((96, D), F32),
        pltpu.VMEM((96, D), F32),
        pltpu.VMEM((96, 256), F32),
        pltpu.VMEM((96, 640), F32),
        pltpu.VMEM((8, 8, D), F32),
        DMA((7,)),
        DMA((4,)),
        DMA((4,)),
        pltpu.VMEM((4, 256, D), BF),
        pltpu.VMEM((4, 256, D), BF),
        pltpu.VMEM((4, 256, D), BF),
        DMA((2, 4, 4)),
        pltpu.VMEM((1, 4, 2, 96, 640), BF),
        pltpu.VMEM((4, 2, 64, 384), BF),
        pltpu.VMEM((8, 4, 2, 64, 384), BF),
        pltpu.VMEM((1024, 1024), BF),
        pltpu.VMEM((8, D), F32),
        pltpu.VMEM((4, 8, D), F32),
        pltpu.VMEM((8, D), F32),
        pltpu.VMEM((4, 96, 256), BF),
        DMA((3,)),
        DMA((3,)),
        DMA((4, 2)),
        DMA((4, 2)),
        DMA((28,)),
        DMA((28,)),
        DMA((7,)),
        DMA((7,)),
        DMA((2,)),
    ]
    for i, (nq, w) in enumerate(SHAPES):
        scratch += [
            pltpu.VMEM((nq, 4, 96, w), BF),
            pltpu.VMEM((nq, 2, 48, w), BF),
            pltpu.VMEM((nq, 2, 48, w), BF),
            pltpu.VMEM((nq, 48, w), BF),
            pltpu.VMEM((nq, 48, w), BF),
            DMA((2, 7)),
            DMA,
        ]
        if i == 3:
            scratch += [pltpu.VMEM((nq, 4, 96, w), BF)]
        else:
            wide = w if i < 2 else 256
            scratch += [pltpu.VMEM((4, 96, wide), BF), pltpu.VMEM((4, 96, wide), BF), DMA((2, 4, 4))]
    return pl.pallas_call(
        back_kernel,
        out_shape=(
            shape((256, D), F32),
            shape((1024, 192), F32),
            shape((96, D), F32),
            shape((96, D), F32),
            shape((96, 256), F32),
            shape((96, 640), F32),
            shape((8, 8, D), F32),
        ),
        in_specs=[ANY] * 16 + [VM, pl.BlockSpec(memory_space=pltpu.SMEM)],
        out_specs=(ANY,) * 7,
        scratch_shapes=scratch,
        compiler_params=params(1),
        name="back",
    )(*args)


def tail_kernel(sp, din, tok, up, down, wout, qkv, res, *outs):
    o_time, o_din, o_tok, o_up, o_down, o_out, o_qkv = outs[:7]
    i = pl.program_id(0)
    row = (200 * i + lax.broadcasted_iota(jnp.int32, (200, D), 0)).astype(F32)
    total = jnp.zeros((200, D), F32)
    for d in range(8):
        total = total + jnp.where(row == sp[d, 7:8, :], sp[d, 6:7, :], 0.0)
    o_time[...] = total

    @pl.when(i == 0)
    def _():
        sums = sp[0]
        for d in range(1, 8):
            sums = sums + sp[d]
        for n, ref in enumerate(outs[7:13]):
            ref[...] = sums[n : n + 1, :].reshape(D)
        outs[13][...] = res[...]
        o_din[...] = din[...]
        o_tok[...] = tok[...].T
        o_up[...] = up[...]
        o_down[...] = down[...]
        o_out[...] = wout[...].T[0:192, :]
        for n in range(3):
            o_qkv[n] = qkv[:, 192 * n : 192 * n + 192]


def tail(*args):
    whole = lambda a: pl.BlockSpec(a.shape, lambda i: (0,) * len(a.shape))
    outs = (
        shape((256, D), F32),
        shape((192, 1024), F32),
        shape((96, D), F32),
        shape((96, D), F32),
        shape((192, 96), F32),
        shape((3, 96, 192), F32),
    ) + (shape((D,), F32),) * 6 + (shape((256, D), BF),)
    return pl.pallas_call(
        tail_kernel,
        grid=(5,),
        out_shape=(shape((1000, D), F32),) + outs,
        in_specs=[whole(a) for a in args],
        out_specs=(pl.BlockSpec((200, D), lambda i: (i, 0)),) + tuple(whole(a) for a in outs),
        compiler_params=pltpu.CompilerParams(vmem_limit_bytes=63 << 20, dimension_semantics=("arbitrary",)),
        name="tail",
    )(*args)


class Native:
    def __init__(self, ndp, nmp):
        self.ndp, self.nmp = ndp, nmp

    def gather_all(self, emb, trow, ids, w2, wo):
        over_mp = lambda a: lax.all_gather(a, "mp", axis=0, tiled=False)
        return (
            over_mp(emb),
            over_mp(trow),
            lax.all_gather(ids, "dp", axis=0, tiled=False),
            over_mp(w2),
            over_mp(wo),
        )

    def exchange(self, x, cid, name):
        return lax.all_to_all(x, "mp", split_axis=0, concat_axis=0, tiled=True)

    def reduce_all(self, gn, dw, dwo, dqkv):
        sum_mp = lambda a: lax.psum_scatter(a.astype(F32), "mp", scatter_dimension=0, tiled=True)
        sum_dp = lambda a: lax.psum_scatter(a, "dp", scatter_dimension=0, tiled=True)
        flat = lambda a: a.reshape(D, a.shape[-1])
        return (
            sum_mp(gn).reshape(gn.shape[1:]),
            sum_dp(flat(sum_mp(dw[0]))),
            sum_dp(flat(sum_mp(dw[1]))),
            sum_dp(flat(sum_mp(dwo[..., : D // self.nmp]))),
            sum_dp(flat(dqkv[..., : 3 * D // self.nmp].astype(F32))),
        )

    def final_exchange(self, tp, vec):
        x = lax.all_to_all(tp, "mp", split_axis=0, concat_axis=0, tiled=True)
        return (
            lax.all_gather(x, "dp", axis=0, tiled=False),
            lax.all_gather(lax.psum(vec, "mp"), "dp", axis=0, tiled=False),
        )


def layer_norm(stream, gain, shift):
    average = jnp.mean(stream, axis=-1, keepdims=True)
    centered = stream - average
    variance = jnp.mean(centered * centered, axis=-1, keepdims=True)
    return centered * lax.rsqrt(variance + 1e-05) * gain + shift


def allowed_pairs(seg_query, segments, first_row):
    key_pos = jnp.arange(L)
    query_pos = first_row + jnp.arange(QBLK)
    same_text = seg_query[:, None] == segments[None, :]
    self_or_text = (seg_query[:, None] != 0) | (query_pos[:, None] == key_pos[None, :])
    return same_text & self_or_text


def attend_forward(queries, key_rows, value_rows, segments):
    outputs = []
    log_parts = []
    for block_index in range(L // QBLK):
        first_row = block_index * QBLK
        query_block = queries[first_row : first_row + QBLK]
        allowed = allowed_pairs(segments[first_row : first_row + QBLK], segments, first_row)
        scores = jnp.einsum("qhd,khd->hqk", query_block, key_rows, preferred_element_type=F32) * 0.125
        masked = jnp.where(allowed[None], scores, -1e30)
        highest = jnp.max(masked, axis=-1, keepdims=True)
        exponents = jnp.exp(masked - highest)
        totals = jnp.sum(exponents, axis=-1, keepdims=True)
        weights = (exponents / totals).astype(BF)
        outputs.append(jnp.einsum("hqk,khd->qhd", weights, value_rows, preferred_element_type=F32).astype(BF))
        log_parts.append((highest + jnp.log(totals))[..., 0])
    return (jnp.concatenate(outputs, axis=0), jnp.concatenate(log_parts, axis=1))


def attend_backward(queries, key_rows, value_rows, segments, log_sums, grad_heads):
    grad_keys = jnp.zeros(key_rows.shape, F32)
    grad_values = jnp.zeros(value_rows.shape, F32)
    grad_queries = []
    for block_index in range(L // QBLK):
        first_row = block_index * QBLK
        query_block = queries[first_row : first_row + QBLK]
        grad_block = grad_heads[first_row : first_row + QBLK]
        allowed = allowed_pairs(segments[first_row : first_row + QBLK], segments, first_row)
        scores = jnp.einsum("qhd,khd->hqk", query_block, key_rows, preferred_element_type=F32) * 0.125
        masked = jnp.where(allowed[None], scores, -1e30)
        probs = jnp.exp(masked - log_sums[:, first_row : first_row + QBLK, None])
        rounded = probs.astype(BF)
        grad_probs = jnp.einsum("qhd,khd->hqk", grad_block, value_rows, preferred_element_type=F32)
        inner = jnp.sum(probs * grad_probs, axis=-1, keepdims=True)
        grad_scores = (probs * (grad_probs - inner)).astype(BF)
        grad_queries.append(
            jnp.einsum("hqk,khd->qhd", grad_scores, key_rows, preferred_element_type=F32) * 0.125
        )
        grad_keys = (
            grad_keys
            + jnp.einsum("hqk,qhd->khd", grad_scores, query_block, preferred_element_type=F32) * 0.125
        )
        grad_values = grad_values + jnp.einsum("hqk,qhd->khd", rounded, grad_block, preferred_element_type=F32)
    return (
        jnp.concatenate(grad_queries, axis=0).astype(BF),
        grad_keys.astype(BF),
        grad_values.astype(BF),
    )


def on_device_native(
    comm,
    token_ids,
    segment_ids,
    timesteps,
    token_table,
    time_table,
    ln1_gain,
    ln1_bias,
    w_qkv,
    w_out,
    attn_bias,
    ln2_gain,
    ln2_bias,
    w_up,
    w_down,
    mlp_bias,
    cotangent,
):
    group = lax.axis_size("mp")
    ndp = lax.axis_size("dp")
    member = lax.axis_index("mp")
    own_rows = L // group
    width = token_table.shape[1]
    heads_local = width // HD

    emb = fold(token_table[token_ids])
    time_row = lax.dynamic_slice_in_dim(time_table, timesteps[0], 1, 0)
    trow = jnp.broadcast_to(jnp.pad(time_row, ((0, 0), (0, 256 - width))), (16, 256))
    ids = token_ids.reshape(8, 128)
    w2 = jnp.stack((w_up, w_down))
    wo = w_out.reshape(width, 6, 128).transpose(1, 0, 2).reshape(6 * width, 128)
    E, TR, IDS, W2, WO = comm.gather_all(emb, trow, ids, w2, wo)

    time_full = TR[:, 0, :width].reshape(1, D).astype(F32)
    tokens = unfold(E).transpose(1, 0, 2).reshape(L, D)
    stream_all = tokens.astype(F32) + time_full
    stream_in = lax.dynamic_slice_in_dim(stream_all, member * own_rows, own_rows, 0)
    normed_one = layer_norm(stream_all, ln1_gain, ln1_bias).astype(BF)
    wq = w_qkv.transpose(1, 2, 0).reshape(3 * width, D)
    packed = contract_cols(normed_one, wq).astype(BF).reshape(L, 3, heads_local, HD)
    queries, key_rows, value_rows = packed[:, 0], packed[:, 1], packed[:, 2]
    attended, log_sums = attend_forward(queries, key_rows, value_rows, segment_ids)
    sent = fold(attended.reshape(group, own_rows, width))
    got = comm.exchange(sent, 1, "to_rows")

    att_own = unfold(got).transpose(1, 0, 2).reshape(own_rows, D)
    w_out_full = WO.reshape(group, 6, width, 128).transpose(0, 2, 1, 3).reshape(D, D)
    stream_mid = stream_in + dot(att_own, w_out_full) + attn_bias
    normed_two = layer_norm(stream_mid, ln2_gain, ln2_bias).astype(BF)
    own_segments = lax.dynamic_slice_in_dim(segment_ids, member * own_rows, own_rows, 0)
    grad_out = cotangent.astype(F32) * (own_segments != 0).astype(F32)[:, None]
    grad_mlp = grad_out.astype(BF)
    out = stream_mid + mlp_bias
    grad_norm_two = jnp.zeros((own_rows, D), F32)
    grads_up, grads_down = [], []
    for q in range(group):
        pre = dot(normed_two, W2[q, 0])
        act, back = jax.vjp(lambda v: jax.nn.gelu(v, approximate=True), pre)
        act = act.astype(BF)
        out = out + dot(act, W2[q, 1])
        grad_pre = back(contract_cols(grad_mlp, W2[q, 1]))[0].astype(BF)
        grad_norm_two = grad_norm_two + contract_cols(grad_pre, W2[q, 0])
        grads_up.append(contract_rows(normed_two, grad_pre).astype(BF))
        grads_down.append(contract_rows(grad_mlp, act).astype(BF))
    dw = jnp.stack((jnp.stack(grads_up), jnp.stack(grads_down)))
    norm_back_two = jax.vjp(layer_norm, stream_mid, ln2_gain, ln2_bias)[1]
    grad_mid_norm, grad_ln2_gain, grad_ln2_bias = norm_back_two(grad_norm_two)
    grad_mid = grad_out + grad_mid_norm
    grad_attn = grad_mid.astype(BF)
    dwo = contract_rows(grad_attn, att_own).astype(BF).reshape(D, group, width).transpose(1, 0, 2)
    dwo = jnp.pad(dwo, ((0, 0), (0, 0), (0, 256 - width)))
    grad_attended = contract_cols(grad_attn, w_out_full).astype(BF)
    sent = fold(grad_attended.reshape(own_rows, group, width).transpose(1, 0, 2))
    got = comm.exchange(sent, 2, "to_heads")

    grad_heads = unfold(got).reshape(L, heads_local, HD)
    grad_q, grad_k, grad_v = attend_backward(
        queries, key_rows, value_rows, segment_ids, log_sums, grad_heads
    )
    grad_packed = jnp.stack((grad_q, grad_k, grad_v), axis=1).reshape(L, 3 * width)
    dqkv = jnp.pad(contract_rows(normed_one, grad_packed).astype(BF), ((0, 0), (0, 640 - 3 * width)))
    gn = dot(grad_packed, wq).astype(BF).reshape(group, own_rows, D)

    pieces = lambda a: a.reshape(a.shape[:-2] + (ndp // 2, 2, D // ndp, a.shape[-1]))
    grad_norm_one, g_up, g_down, g_out, g_qkv = comm.reduce_all(
        gn, pieces(dw), pieces(dwo), pieces(dqkv)[None]
    )
    norm_back_one = jax.vjp(layer_norm, stream_in, ln1_gain, ln1_bias)[1]
    grad_in_norm, grad_ln1_gain, grad_ln1_bias = norm_back_one(grad_norm_one)
    input_grad = grad_mid + grad_in_norm
    tp = fold(input_grad.astype(BF).reshape(own_rows, group, width).transpose(1, 0, 2))
    step_row = jnp.where(member == 0, timesteps[0], 0).astype(F32)
    vec = jnp.stack(
        (
            grad_ln1_gain,
            grad_ln1_bias,
            jnp.sum(grad_mid, axis=0),
            grad_ln2_gain,
            grad_ln2_bias,
            jnp.sum(grad_out, axis=0),
            jnp.sum(input_grad, axis=0),
            jnp.broadcast_to(step_row, (D,)),
        )
    )
    X, SP = comm.final_exchange(tp, vec)
    rows_table = token_table.shape[0] // ndp
    columns = unfold(X).reshape(ndp * L, width)
    first = lax.axis_index("dp") * rows_table
    hot = (first + jnp.arange(rows_table))[:, None] == IDS.reshape(1, ndp * L)
    grad_token_table = dot(hot.astype(BF), columns)
    steps = SP[:, 7, 0].astype(jnp.int32)
    grad_time_table = jnp.zeros(time_table.shape[:1] + (D,), F32)
    at_row = jnp.arange(time_table.shape[0])[:, None]
    if ndp <= 8:
        for i in range(ndp):
            grad_time_table = grad_time_table + jnp.where(at_row == steps[i], SP[i, 6][None], 0.0)
    else:
        grad_time_table = grad_time_table.at[steps].add(SP[:, 6])
    sums = jnp.sum(SP[:, :6], axis=0)
    return (
        out.astype(BF),
        input_grad,
        grad_token_table,
        grad_time_table,
        sums[0],
        sums[1],
        g_qkv[:, : 3 * width].reshape(-1, 3, width),
        g_out[:, :width].T,
        sums[2],
        sums[3],
        sums[4],
        g_up,
        g_down.T,
        sums[5],
    )


def on_device_tuned(
    token_ids, segment_ids, timesteps, token_table, time_table, ln1_gain, ln1_bias, w_qkv, w_out, attn_bias,
    ln2_gain, ln2_bias, w_up, w_down, mlp_bias, cotangent,
):
    width = 192
    ids8 = token_ids.reshape(8, 128)
    wq = w_qkv.transpose(1, 2, 0).reshape(3 * width, D)
    qm, k, v, kt, normed_one, stream_in, lse, segr, segc, grad_mid, grad_attended, vec, out, IDS, dw, dwo = front(
        token_ids, segment_ids, timesteps, ids8, token_table.T, time_table.T, ln1_gain, ln1_bias, wq, w_up, w_down, w_out,
        cotangent, attn_bias, ln2_gain, ln2_bias, mlp_bias,
    )
    input_grad, grad_token_table, g_up, g_down, g_out, g_qkv, SP = back(
        grad_attended, qm, k, v, kt, lse, normed_one, wq, stream_in, grad_mid, segc, segr, vec, IDS, dw, dwo, ln1_gain,
        timesteps,
    )
    o_time, o_in, o_tok, o_up, o_down, o_out, o_qkv, *sums = tail(
        SP, input_grad, grad_token_table, g_up, g_down, g_out, g_qkv, out
    )
    return (
        sums[6], o_in, o_tok.T, o_time, sums[0], sums[1], o_qkv.transpose(1, 0, 2), o_out, sums[2], sums[3], sums[4],
        o_up, o_down.T, sums[5],
    )


def solution(mesh):
    placed = (
        P("dp"),
        P("dp"),
        P("dp"),
        P(None, "mp"),
        P(None, "mp"),
        P(),
        P(),
        P(None, None, "mp"),
        P("mp", None),
        P(),
        P(),
        P(),
        P(None, "mp"),
        P("mp", None),
        P(),
        P(("dp", "mp"), None),
    )
    ndp, nmp = mesh.shape["dp"], mesh.shape["mp"]
    return jax.shard_map(
        on_device_tuned if (ndp, nmp) == (8, 4) else functools.partial(on_device_native, Native(ndp, nmp)),
        mesh=mesh,
        in_specs=placed,
        out_specs=(
            P(("dp", "mp"), None),
            P(("dp", "mp"), None),
            P("dp", "mp"),
            P(),
            P(),
            P(),
            P("dp", None, "mp"),
            P("mp", "dp"),
            P(),
            P(),
            P(),
            P("dp", "mp"),
            P("mp", "dp"),
            P(),
        ),
        check_vma=False,
    )
```
